256 devices in a mesh: src: 8 (over z_hi, y), tile: 32 (over z_lo, x, core).
Axes of the slice: x: 4, y: 4, z: 8 (z_hi: 2, z_lo: 4; z = z_hi * 4 + z_lo), core: 2. Of those that a mesh axis runs over, the one named last changes fastest.
Arguments:
- near_field: float32 [2, 32, 36864], P(None, 'tile'), may hold values from -6 to 6
- source_shift: int32 [8, 2, 2], P('src'), may hold values from -38 to 38
- source_weight: float32 [8, 2], P('src'), may hold values from 0.25 to 1
- defocus: float32 [8], replicated, may hold values from -4 to 4
- dose: float32 [8], replicated, may hold values from 0.2 to 1
- quencher_load: float32 [8], replicated, may hold values from 0.2 to 0.6
Outputs:
- acid: float32 [8, 32, 36864], P(None, 'tile', 'src')
The draws below stay inside these ranges and needn't reach their ends.
All inputs are finite; a program needn't handle non-finite values.
Results may differ from the reference program's by a relative error of at most 0.0003.
Values sent between devices are 32-bit elements; how exact they have to be, the bound alone decides.
No kernel may reach another device: no remote copies, remote signals or barrier semaphores. Data moves between devices by JAX's collectives and lax.ppermute only.
A program may use at most 64 MiB of HBM per device.

```python
import math
import jax
import jax.numpy as jnp
from jax import lax

CORE = 192
MARGIN = 32
RADIUS = 48
SHIFT_MAX = 38
DEPTHS = 8
PTS = 2
BAKE_STEPS = 4
SECTORS = 8
TILES = 32


def touch_ends(result, key, low, top_value):
    spot = [jax.random.randint(jax.random.fold_in(key, axis), (), 0, length) for axis, length in enumerate(result.shape)]
    widest = result.shape.index(max(result.shape))
    neighbour = spot[:widest] + [(spot[widest] + 1) % result.shape[widest]] + spot[widest + 1:]
    return result.at[tuple(spot)].set(low).at[tuple(neighbour)].set(top_value)


def steps_of(key, extent, pieces, least, top_value):
    loudness, own = 1.0, jax.random.fold_in(key, 6)
    for dim, parts in pieces:
        heights = jnp.exp(jax.random.uniform(jax.random.fold_in(own, dim), (parts,), jnp.float32, least / len(pieces), top_value / len(pieces)))
        loudness = loudness * jnp.repeat(heights, extent[dim] // parts).reshape([-1 if axis == dim else 1 for axis in range(len(extent))])
    return loudness


def centred(rng, dims, scale, bound, pieces=(), held_as=jnp.bfloat16):
    entries = scale * jax.random.normal(rng, dims, jnp.float32)
    if pieces:
        entries = entries * steps_of(rng, dims, pieces, -0.22, 0.18)
    return jnp.clip(entries, -bound, bound).astype(held_as)


def setup_inputs(seed: int = 0) -> dict:
    key_of = jax.random.split(jax.random.key(seed), 7)
    near_field = centred(key_of[0], (2, TILES, CORE * CORE), 1.0, 6.0, ((1, 32),), jnp.float32)
    source_shift = touch_ends(jax.random.randint(key_of[1], (SECTORS, PTS, 2), 0 - SHIFT_MAX, SHIFT_MAX + 1), jax.random.fold_in(key_of[1], 1), 0 - SHIFT_MAX, SHIFT_MAX).astype(jnp.int32)
    source_weight = jnp.clip(jnp.exp(math.log(1.0) - 1.3862944 * jax.random.uniform(key_of[2], (SECTORS, PTS), jnp.float32) ** steps_of(key_of[2], (SECTORS, PTS), ((0, 8),), -0.2, 0.2)), 0.25, 1.0)
    defocus = jnp.clip(jax.random.uniform(key_of[3], (DEPTHS,), jnp.float32, -4.0, 4.0), -4.0, 4.0)
    dose = jnp.clip(jnp.exp(jax.random.uniform(key_of[4], (DEPTHS,), jnp.float32, math.log(0.2), math.log(1.0))), 0.2, 1.0)
    quencher_load = jnp.clip(jax.random.uniform(key_of[5], (DEPTHS,), jnp.float32, 0.2, 0.6), 0.2, 0.6)
    return dict(near_field=near_field, source_shift=source_shift, source_weight=source_weight, defocus=defocus, dose=dose, quencher_load=quencher_load)


acid_rate = 0.24
quench_rate = 0.12
depth_rate = 0.02
react_rate = 0.8


def frequencies(length):
    index = jnp.arange(length, dtype=jnp.int32)
    return (index + length // 2) % length - length // 2


def lateral(values):
    padded = jnp.pad(values, ((0, 0), (1, 1), (1, 1)))
    return padded[:, 2:, 1:-1] + padded[:, :-2, 1:-1] + padded[:, 1:-1, 2:] + padded[:, 1:-1, :-2] - 4.0 * values


def vertical(values):
    padded = jnp.concatenate([values[:1], values, values[-1:]], axis=0)
    return padded[2:] + padded[:-2] - 2.0 * values


def reference(near_field, source_shift, source_weight, defocus, dose, quencher_load):
    length = CORE + 2 * MARGIN
    tiles = near_field.shape[1]
    depths = defocus.shape[0]
    strip_field = near_field.reshape(2, tiles, CORE, CORE).transpose(0, 2, 1, 3).reshape(2, CORE, tiles * CORE)
    field = strip_field[0] + 1j * strip_field[1]
    padded = jnp.pad(field, ((MARGIN, MARGIN), (MARGIN, MARGIN)))
    freqs = frequencies(length)
    shifts = source_shift.reshape(-1, 2)
    weights = source_weight.reshape(-1)
    along_y = freqs[None, :, None] + shifts[:, 0, None, None]
    along_x = freqs[None, None, :] + shifts[:, 1, None, None]
    radius_sq = along_y * along_y + along_x * along_x
    inside = radius_sq <= RADIUS * RADIUS
    phase = defocus[None, :, None, None] * radius_sq[:, None].astype(defocus.dtype) / float(RADIUS * RADIUS)
    pupils = jnp.where(inside[:, None], jnp.cos(phase) + 1j * jnp.sin(phase), 0.0)

    def image_tile(index):
        window = lax.dynamic_slice(padded, (jnp.int32(0), (index * CORE).astype(jnp.int32)), (length, length))
        spectrum = jnp.fft.fft2(window)
        images = jnp.fft.ifft2(pupils * spectrum)[..., MARGIN:MARGIN + CORE, MARGIN:MARGIN + CORE]
        power = images.real * images.real + images.imag * images.imag
        return jnp.einsum("p,pdyx->dyx", weights, power)

    per_tile = lax.map(image_tile, jnp.arange(tiles, dtype=jnp.int32))
    intensity = per_tile.transpose(1, 2, 0, 3).reshape(depths, CORE, tiles * CORE)
    acid = 1.0 - jnp.exp(-dose[:, None, None] * intensity)
    quencher = jnp.broadcast_to(quencher_load[:, None, None], acid.shape)
    for counter in range(BAKE_STEPS):
        reaction = react_rate * acid * quencher
        new_acid = acid + acid_rate * lateral(acid) + depth_rate * vertical(acid) - reaction
        quencher = quencher + quench_rate * lateral(quencher) + depth_rate * vertical(quencher) - reaction
        acid = new_acid
    return acid.reshape(depths, CORE, tiles, CORE).transpose(0, 2, 1, 3).reshape(depths, tiles, CORE * CORE)
```

```python
import numpy as np

import jax
import jax.numpy as jnp
from jax import lax
from jax.experimental import pallas as pl
from jax.experimental.pallas import tpu as pltpu
from jax.sharding import PartitionSpec as P

CORE = 192
MARGIN = 32
LENGTH = CORE + 2 * MARGIN
RADIUS = 48
DEPTHS = 8
BAKE_STEPS = 4
SECTORS = 8
TILES = 32
POINTS = 2
ROWS = CORE // SECTORS
HALO_ROWS = ROWS + 2 * BAKE_STEPS
LOW = 88
SPEC_ROWS = 208
LANES = 128
UNROLL = 2

acid_rate = 0.24
quench_rate = 0.12
depth_rate = 0.02
react_rate = 0.8

bf16 = jnp.bfloat16
f32 = jnp.float32


def two_parts(table):
    table = table.astype(np.float32)
    high = table.astype(bf16)
    low = (table - high.astype(np.float32)).astype(bf16)
    return high, low


def waves(left, right):
    angle = 2.0 * np.pi / LENGTH * (np.outer(left, right) % LENGTH)
    return np.cos(angle), np.sin(angle)


def forward_rows():
    order = np.concatenate([np.arange(0, CORE, 2), np.arange(1, CORE, 2)])
    real, imag = waves(np.arange(SPEC_ROWS) - LOW, order + MARGIN)
    return two_parts(np.concatenate([real, -imag], 1))


def forward_columns():
    order = np.concatenate(
        [np.arange(CORE) + MARGIN, np.arange(MARGIN), np.arange(MARGIN) + MARGIN + CORE]
    )
    real, imag = waves(order, np.arange(256) - LOW)
    imag = -imag
    return two_parts(np.block([[real, imag], [-imag, real]]))


def inverse_columns():
    bins = np.arange(LANES) - RADIUS
    real, imag = waves(bins, np.arange(CORE) + MARGIN)
    keep = (np.abs(bins) <= RADIUS)[:, None] / LENGTH
    real, imag = real * keep, imag * keep
    top = np.concatenate([real[:, :128], imag[:, :128], real[:, 128:], imag[:, 128:]], 1)
    low = np.concatenate([-imag[:, :128], real[:, :128], -imag[:, 128:], real[:, 128:]], 1)
    return two_parts(np.concatenate([top, low], 0))


def inverse_rows():
    bins = np.arange(LANES) - RADIUS
    rows = np.arange(CORE + 2 * BAKE_STEPS) - BAKE_STEPS + MARGIN
    real, imag = waves(rows, bins)
    keep = (np.abs(bins) <= RADIUS)[None, :] / LENGTH
    return np.concatenate([real * keep, imag * keep], 1).astype(np.float32)


def split(values):
    high = values.astype(bf16)
    low = (values - high.astype(f32)).astype(bf16)
    return high, low


def product(left_high, left_low, right_high, right_low):
    def dot(a, b):
        return jnp.dot(a, b, preferred_element_type=f32)

    return dot(left_high, right_high) + (dot(left_low, right_high) + dot(left_high, right_low))


def lane_iota(shape):
    return lax.broadcasted_iota(jnp.int32, shape, len(shape) - 1)


def edges_kernel(near_ref, right_ref, left_ref):
    half = CORE // 4
    lane = lane_iota((half, LANES))
    odd = lane >= 64
    second = (lane % 64) >= 32
    for part in range(2):
        def rows(start, offset):
            return near_ref[part, pl.ds(3 * start + offset, half, stride=3), :]

        def right(start):
            return jnp.where(odd, rows(start, 2), rows(start, 1))

        def left(start):
            return jnp.where(odd, rows(start, 1), rows(start, 0))

        right_ref[part] = jnp.where(second, right(0), pltpu.roll(right(half), 96, 1))
        left_ref[part] = jnp.where(second, pltpu.roll(left(half), 32, 1), left(0))


def image_kernel(
    near_ref, from_left_ref, from_right_ref, q0_ref, q1_ref, q2_ref, q3_ref,
    defocus_ref, dose_ref, fyh_ref, fyl_ref, fxh_ref, fxl_ref, th_ref, tl_ref, rows_ref,
    acid_ref, left_ref, right_ref,
    wh_ref, wl_ref, spec_ref, lh_ref, ll_ref, zh_ref, zl_ref, acc_ref, start_sm, shift_sm, amp_sm,
):
    me = lax.axis_index("src")
    half = CORE // 4
    lane = lane_iota((half, LANES))
    low64 = lane < 64
    quarter = lane // 32

    for part in range(2):
        def put(row, col, high, low, negate):
            rows = pl.ds(row, half)
            cols = pl.ds(col, LANES)
            wh_ref[rows, cols] = -high if negate else high
            wl_ref[rows, cols] = -low if negate else low

        for piece in range(2):
            def rows(offset):
                return near_ref[part, pl.ds(3 * piece * half + offset, half, stride=3), :]

            a, b, c = rows(0), rows(1), rows(2)
            bt, ct = pltpu.roll(b, 64, 1), pltpu.roll(c, 64, 1)
            hl, hr = from_left_ref[part], from_right_ref[part]
            if piece == 0:
                even_tail = jnp.where(low64, b, jnp.where(quarter == 2, pltpu.roll(hl, 32, 1), pltpu.roll(hr, 96, 1)))
                odd_tail = jnp.where(low64, ct, jnp.where(quarter == 2, pltpu.roll(hl, 96, 1), pltpu.roll(hr, 32, 1)))
            else:
                even_tail = jnp.where(low64, b, jnp.where(quarter == 2, pltpu.roll(hl, 64, 1), pltpu.roll(hr, 64, 1)))
                odd_tail = jnp.where(low64, ct, jnp.where(quarter == 2, hl, hr))
            odd_head = jnp.where(low64, bt, ct)
            for base, head, tail in ((0, a, even_tail), (CORE // 2, odd_head, odd_tail)):
                row = base + piece * half
                for col, block in ((0, head), (LANES, tail)):
                    high, low = split(block)
                    if part == 0:
                        put(row, col, high, low, False)
                        put(CORE + row, 256 + col, high, low, False)
                    else:
                        put(row, 256 + col, high, low, False)
                        put(CORE + row, col, high, low, True)

    mixed = product(fyh_ref[...], fyl_ref[...], wh_ref[...], wl_ref[...])
    mixed_high, mixed_low = split(mixed)
    spec = product(mixed_high, mixed_low, fxh_ref[...], fxl_ref[...])
    for k in range(4):
        spec_ref[k] = spec[:, k * LANES:(k + 1) * LANES]

    depth = lax.broadcasted_iota(jnp.int32, (DEPTHS, LANES), 0)
    bins = lane_iota((DEPTHS, LANES)) - RADIUS

    def by_depth(ref):
        out = jnp.zeros((DEPTHS, LANES), f32)
        for d in range(DEPTHS):
            out = jnp.where(depth == d, ref[d], out)
        return out

    phase = by_depth(defocus_ref) * (bins * bins).astype(f32) / float(RADIUS * RADIUS)
    phase_real, phase_imag = jnp.cos(phase), jnp.sin(phase)
    table = rows_ref[pl.ds(pl.multiple_of(me * ROWS, 8), HALO_ROWS), :]
    table_real = table[:, None, :LANES]
    table_imag = table[:, None, LANES:]
    left_real = (table_real * phase_real - table_imag * phase_imag).reshape(HALO_ROWS * DEPTHS, LANES)
    left_imag = (table_real * phase_imag + table_imag * phase_real).reshape(HALO_ROWS * DEPTHS, LANES)
    for k, block in ((0, left_real), (1, left_imag)):
        high, low = split(block)
        lh_ref[:, k * LANES:(k + 1) * LANES] = high
        ll_ref[:, k * LANES:(k + 1) * LANES] = low

    for k, ref in enumerate((q0_ref, q1_ref, q2_ref, q3_ref)):
        for r in range(2):
            for j in range(POINTS):
                n = (k * 2 + r) * POINTS + j
                start_sm[n] = (LOW - RADIUS) - ref[r, 2 * j].astype(jnp.int32)
                shift_sm[n] = (LOW - RADIUS) - ref[r, 2 * j + 1].astype(jnp.int32)
                amp_sm[n] = ref[r, 4 + j]

    acc_ref[...] = jnp.zeros_like(acc_ref)
    rowbin = lax.broadcasted_iota(jnp.int32, (LANES, LANES), 0) - RADIUS
    colbin = lane_iota((LANES, LANES)) - RADIUS
    inside = rowbin * rowbin + colbin * colbin <= RADIUS * RADIUS
    lane_full = lane_iota((LANES, LANES))

    def point(n, carry):
        start, shift, amp = start_sm[n], shift_sm[n], amp_sm[n]

        def shifted(k):
            first = spec_ref[k, pl.ds(start, LANES), :]
            second = spec_ref[k + 1, pl.ds(start, LANES), :]
            turn = LANES - shift
            moved = jnp.where(lane_full < turn, pltpu.roll(first, turn, 1), pltpu.roll(second, turn, 1))
            return jnp.where(inside, moved * amp, 0.0)

        real, imag = shifted(0), shifted(2)
        real_high, real_low = split(real)
        imag_high, imag_low = split(imag)
        zh = jnp.concatenate([jnp.concatenate([real_high, imag_high], 1), jnp.concatenate([-imag_high, real_high], 1)], 0)
        zl = jnp.concatenate([jnp.concatenate([real_low, imag_low], 1), jnp.concatenate([-imag_low, real_low], 1)], 0)
        middle = product(lh_ref[...], ll_ref[...], zh, zl)
        shape = (HALO_ROWS, DEPTHS, LANES)
        mid_real = middle[:, :LANES].reshape(shape)
        mid_imag = middle[:, LANES:].reshape(shape)
        out_real = (mid_real * phase_real - mid_imag * phase_imag).reshape(-1, LANES)
        out_imag = (mid_real * phase_imag + mid_imag * phase_real).reshape(-1, LANES)
        rh, rl = split(out_real)
        ih, il = split(out_imag)
        image = product(jnp.concatenate([rh, ih], 1), jnp.concatenate([rl, il], 1), th_ref[...], tl_ref[...])
        acc_ref[...] += image * image
        return carry

    lax.fori_loop(0, SECTORS * POINTS, point, 0, unroll=UNROLL)

    dose = by_depth(dose_ref)
    shape = (HALO_ROWS, DEPTHS, LANES)
    acc = acc_ref[...]
    head = (acc[:, :128] + acc[:, 128:256]).reshape(shape)
    tail = acc[:, 256:]
    tail = (tail + pltpu.roll(tail, 64, 1)).reshape(shape)
    acid_head = 1.0 - jnp.exp(-dose * head)
    acid_tail = 1.0 - jnp.exp(-dose * tail)
    acid_ref[:, :, :LANES] = acid_head
    acid_ref[:, :, LANES:] = acid_tail
    lane1 = lane_iota((DEPTHS, LANES))
    left = jnp.zeros((DEPTHS, LANES), f32)
    right = jnp.zeros((DEPTHS, LANES), f32)
    for y in range(HALO_ROWS):
        here = (lane1 >= 4 * y) & (lane1 < 4 * y + 4)
        left = jnp.where(here, pltpu.roll(acid_head[y], 4 * y, 1) if y else acid_head[y], left)
        turn = (4 * y - 60) % LANES
        right = jnp.where(here, pltpu.roll(acid_tail[y], turn, 1) if turn else acid_tail[y], right)
    left_ref[...] = left
    right_ref[...] = right


def bake_kernel(acid_ref, from_left_ref, from_right_ref, load_ref, out_ref):
    me = lax.axis_index("src")
    tile = lax.axis_index("tile")
    lane1 = lane_iota((DEPTHS, LANES))
    depth = lax.broadcasted_iota(jnp.int32, (DEPTHS, LANES), 0)
    load = jnp.zeros((DEPTHS, LANES), f32)
    for d in range(DEPTHS):
        load = jnp.where(depth == d, load_ref[d], load)
    has_left = (tile > 0).astype(f32)
    has_right = (tile < TILES - 1).astype(f32)
    left_cells = lane1 >= 124
    right_cells = (lane1 >= 64) & (lane1 < 68)
    keep_tail = jnp.where(lane1 < 64, 1.0, jnp.where(left_cells, has_left, jnp.where(right_cells, has_right, 0.0)))

    def keep_row(y):
        row = me * ROWS - BAKE_STEPS + y
        return ((row >= 0) & (row < CORE)).astype(f32)

    from_left, from_right = from_left_ref[...], from_right_ref[...]
    acid, quencher = [], []
    for y in range(HALO_ROWS):
        tail = acid_ref[y, :, LANES:]
        turn_left, turn_right = (124 - 4 * y) % LANES, (64 - 4 * y) % LANES
        moved_left = pltpu.roll(from_left, turn_left, 1) if turn_left else from_left
        moved_right = pltpu.roll(from_right, turn_right, 1) if turn_right else from_right
        tail = jnp.where(lane1 < 64, tail, jnp.where(left_cells, moved_left, moved_right)) * keep_tail
        head = acid_ref[y, :, :LANES]
        pair = [head, tail]
        loads = [load, load * keep_tail]
        if y < BAKE_STEPS or y >= HALO_ROWS - BAKE_STEPS:
            keep = keep_row(y)
            pair = [v * keep for v in pair]
            loads = [v * keep for v in loads]
        acid.append(pair)
        quencher.append(loads)

    first_lane, last_lane = lane1 == 0, lane1 == LANES - 1
    top, bottom = depth == 0, depth == DEPTHS - 1

    def spread(values, y, k, rate):
        here = values[y][k]
        other = values[y][1 - k]
        before = jnp.where(first_lane, pltpu.roll(other, 1, 1), pltpu.roll(here, 1, 1))
        after = jnp.where(last_lane, pltpu.roll(other, LANES - 1, 1), pltpu.roll(here, LANES - 1, 1))
        lateral = values[y + 1][k] + values[y - 1][k] + before + after - 4.0 * here
        above = jnp.where(top, here, pltpu.roll(here, 1, 0))
        below = jnp.where(bottom, here, pltpu.roll(here, DEPTHS - 1, 0))
        return here + rate * lateral + depth_rate * (above + below - 2.0 * here)

    for step in range(1, BAKE_STEPS + 1):
        next_acid, next_quencher = list(acid), list(quencher)
        for y in range(step, HALO_ROWS - step):
            pair, loads = [], []
            for k in range(2):
                reaction = react_rate * acid[y][k] * quencher[y][k]
                new_acid = spread(acid, y, k, acid_rate) - reaction
                pair.append(new_acid)
                if step < BAKE_STEPS:
                    loads.append(spread(quencher, y, k, quench_rate) - reaction)
            if step < BAKE_STEPS:
                pair[1] = pair[1] * keep_tail
                loads[1] = loads[1] * keep_tail
                if y < BAKE_STEPS or y >= HALO_ROWS - BAKE_STEPS:
                    keep = keep_row(y)
                    pair = [v * keep for v in pair]
                    loads = [v * keep for v in loads]
            next_acid[y] = pair
            next_quencher[y] = loads
        acid, quencher = next_acid, next_quencher

    low64 = lane1 < 64
    for k in range(ROWS // 2):
        even_head, even_tail = acid[BAKE_STEPS + 2 * k]
        odd_head, odd_tail = (pltpu.roll(v, 64, 1) for v in acid[BAKE_STEPS + 2 * k + 1])
        base = 384 * k
        out_ref[:, base:base + 128] = even_head
        out_ref[:, base + 128:base + 256] = jnp.where(low64, even_tail, odd_head)
        out_ref[:, base + 256:base + 384] = jnp.where(low64, odd_head, odd_tail)


def vmem(n):
    return [pl.BlockSpec(memory_space=pltpu.VMEM)] * n


def smem(n):
    return [pl.BlockSpec(memory_space=pltpu.SMEM)] * n


def route(mesh_shape, half, turn):
    pairs = []
    for s in range(SECTORS):
        for t in range(TILES):
            upper, y = divmod(s, 4)
            target_tile = t
            if half:
                upper ^= 1
                target_tile = t ^ 16
            pairs.append((s * TILES + t, (upper * 4 + (y + turn) % 4) * TILES + target_tile))
    return pairs


def on_device(near_field, source_shift, source_weight, defocus, dose, quencher_load):
    both = ("src", "tile")
    near = near_field.reshape(2, CORE * CORE // LANES, LANES)
    own = jnp.concatenate(
        [source_shift.reshape(1, 4).astype(f32), jnp.sqrt(source_weight.reshape(1, 2)), jnp.zeros((1, 2), f32)], 1
    )
    other = lax.ppermute(own, both, route(None, True, 0))

    half = CORE // 4
    packed = jax.ShapeDtypeStruct((2, half, LANES), f32)
    right_edge, left_edge = pl.pallas_call(
        edges_kernel, out_shape=(packed, packed), in_specs=vmem(1), out_specs=tuple(vmem(2)), name="edges"
    )(near)
    up = [(i, i + 1) for i in range(TILES - 1)]
    down = [(j, i) for i, j in up]
    from_left = lax.ppermute(right_edge, "tile", up)
    from_right = lax.ppermute(left_edge, "tile", down)

    pair = jnp.concatenate([own, other], 0)
    points = [pair] + [lax.ppermute(pair, both, route(None, False, turn)) for turn in (1, 2, 3)]

    tables = [jnp.asarray(v) for v in (*forward_rows(), *forward_columns(), *inverse_columns(), inverse_rows())]
    edge = jax.ShapeDtypeStruct((DEPTHS, LANES), f32)
    acid, left, right = pl.pallas_call(
        image_kernel,
        out_shape=(jax.ShapeDtypeStruct((HALO_ROWS, DEPTHS, 256), f32), edge, edge),
        in_specs=vmem(3) + smem(6) + vmem(7),
        out_specs=tuple(vmem(3)),
        scratch_shapes=[
            pltpu.VMEM((2 * CORE, 512), bf16),
            pltpu.VMEM((2 * CORE, 512), bf16),
            pltpu.VMEM((4, SPEC_ROWS, LANES), f32),
            pltpu.VMEM((HALO_ROWS * DEPTHS, 256), bf16),
            pltpu.VMEM((HALO_ROWS * DEPTHS, 256), bf16),
            pltpu.VMEM((256, 256), bf16),
            pltpu.VMEM((256, 256), bf16),
            pltpu.VMEM((HALO_ROWS * DEPTHS, 384), f32),
            pltpu.SMEM((SECTORS * POINTS,), jnp.int32),
            pltpu.SMEM((SECTORS * POINTS,), jnp.int32),
            pltpu.SMEM((SECTORS * POINTS,), f32),
        ],
        name="image",
    )(near, from_left, from_right, *points, defocus, dose, *tables)
    from_left = lax.ppermute(right, "tile", up)
    from_right = lax.ppermute(left, "tile", down)
    out = pl.pallas_call(
        bake_kernel,
        out_shape=jax.ShapeDtypeStruct((DEPTHS, ROWS * CORE), f32),
        in_specs=vmem(3) + smem(1),
        out_specs=vmem(1)[0],
        name="bake",
    )(acid, from_left, from_right, quencher_load)
    return out.reshape(DEPTHS, 1, ROWS * CORE)


def solution(mesh):
    return jax.shard_map(
        on_device,
        mesh=mesh,
        in_specs=(P(None, "tile", None), P("src", None, None), P("src", None), P(), P(), P()),
        out_specs=P(None, "tile", "src"),
        check_vma=False,
    )
```

```python
import numpy as np

import jax
import jax.numpy as jnp
from jax import lax
from jax.experimental import pallas as pl
from jax.experimental.pallas import tpu as pltpu
from jax.sharding import PartitionSpec as P

CORE = 192
MARGIN = 32
LENGTH = CORE + 2 * MARGIN
RADIUS = 48
DEPTHS = 8
BAKE_STEPS = 4
SECTORS = 8
TILES = 32
POINTS = 2
ROWS = CORE // SECTORS
HALO_ROWS = ROWS + 2 * BAKE_STEPS
LOW = 88
SPEC_ROWS = 208
LANES = 128
UNROLL = 2

acid_rate = 0.24
quench_rate = 0.12
depth_rate = 0.02
react_rate = 0.8

bf16 = jnp.bfloat16
f32 = jnp.float32


def two_parts(table):
    table = table.astype(np.float32)
    high = table.astype(bf16)
    low = (table - high.astype(np.float32)).astype(bf16)
    return high, low


def waves(left, right):
    angle = 2.0 * np.pi / LENGTH * (np.outer(left, right) % LENGTH)
    return np.cos(angle), np.sin(angle)


def forward_rows():
    order = np.concatenate([np.arange(0, CORE, 2), np.arange(1, CORE, 2)])
    real, imag = waves(np.arange(SPEC_ROWS) - LOW, order + MARGIN)
    return two_parts(np.concatenate([real, -imag], 1))


def forward_columns():
    order = np.concatenate(
        [np.arange(CORE) + MARGIN, np.arange(MARGIN), np.arange(MARGIN) + MARGIN + CORE]
    )
    real, imag = waves(order, np.arange(256) - LOW)
    imag = -imag
    return two_parts(np.block([[real, imag], [-imag, real]]))


def inverse_columns():
    bins = np.arange(LANES) - RADIUS
    real, imag = waves(bins, np.arange(CORE) + MARGIN)
    keep = (np.abs(bins) <= RADIUS)[:, None] / LENGTH
    real, imag = real * keep, imag * keep
    top = np.concatenate([real[:, :128], imag[:, :128], real[:, 128:], imag[:, 128:]], 1)
    low = np.concatenate([-imag[:, :128], real[:, :128], -imag[:, 128:], real[:, 128:]], 1)
    return two_parts(np.concatenate([top, low], 0))


def inverse_rows():
    bins = np.arange(LANES) - RADIUS
    rows = np.arange(CORE + 2 * BAKE_STEPS) - BAKE_STEPS + MARGIN
    real, imag = waves(rows, bins)
    keep = (np.abs(bins) <= RADIUS)[None, :] / LENGTH
    return np.concatenate([real * keep, imag * keep], 1).astype(np.float32)


def split(values):
    high = values.astype(bf16)
    low = (values - high.astype(f32)).astype(bf16)
    return high, low


def product(left_high, left_low, right_high, right_low):
    def dot(a, b):
        return jnp.dot(a, b, preferred_element_type=f32)

    return dot(left_high, right_high) + (dot(left_low, right_high) + dot(left_high, right_low))


def lane_iota(shape):
    return lax.broadcasted_iota(jnp.int32, shape, len(shape) - 1)


def edges_kernel(near_ref, shift_ref, weight_ref, own_ref, cross_ref, points_ref):
    half = CORE // 4
    even_tile = lax.axis_index("tile") % 2 == 0
    lane = lane_iota((half, LANES))
    odd = lane >= 64
    second = (lane % 64) >= 32
    for part in range(2):
        def rows(start, offset):
            return near_ref[part, pl.ds(3 * start + offset, half, stride=3), :]

        def right(start):
            return jnp.where(odd, rows(start, 2), rows(start, 1))

        def left(start):
            return jnp.where(odd, rows(start, 1), rows(start, 0))

        right_edge = jnp.where(second, right(0), pltpu.roll(right(half), 96, 1))
        left_edge = jnp.where(second, pltpu.roll(left(half), 32, 1), left(0))
        own_ref[pl.ds(part * half, half), :] = jnp.where(even_tile, right_edge, left_edge)
        cross_ref[pl.ds(part * half, half), :] = jnp.where(even_tile, left_edge, right_edge)

    lane1 = lane_iota((8, LANES))
    values = jnp.zeros((8, LANES), f32)
    for j in range(POINTS):
        for axis in range(2):
            values = jnp.where(lane1 == 2 * j + axis, shift_ref[0, j, axis].astype(f32), values)
    weights = jnp.ones((8, LANES), f32)
    for j in range(POINTS):
        weights = jnp.where(lane1 == 4 + j, weight_ref[0, j], weights)
    values = jnp.where(lane1 < 4, values, jnp.sqrt(weights))
    own_ref[pl.ds(2 * half, 8), :] = values
    cross_ref[pl.ds(2 * half, 8), :] = values
    points_ref[...] = values


def by_depth(ref):
    depth = lax.broadcasted_iota(jnp.int32, (DEPTHS, LANES), 0)
    out = jnp.zeros((DEPTHS, LANES), f32)
    for d in range(DEPTHS):
        out = jnp.where(depth == d, ref[d], out)
    return out


def depth_phase(defocus_ref):
    bins = lane_iota((DEPTHS, LANES)) - RADIUS
    phase = by_depth(defocus_ref) * (bins * bins).astype(f32) / float(RADIUS * RADIUS)
    return jnp.cos(phase), jnp.sin(phase)


def spectrum(near_ref, own_ref, cross_ref, fyh_ref, fyl_ref, fxh_ref, fxl_ref, spec_ref, wh_ref, wl_ref):
    tile = lax.axis_index("tile")
    even_tile = tile % 2 == 0
    has_left = (tile > 0).astype(f32)
    has_right = (tile < TILES - 1).astype(f32)
    half = CORE // 4
    lane = lane_iota((half, LANES))
    low64 = lane < 64
    quarter = lane // 32

    for part in range(2):
        def put(row, col, high, low, negate):
            rows = pl.ds(row, half)
            cols = pl.ds(col, LANES)
            wh_ref[rows, cols] = -high if negate else high
            wl_ref[rows, cols] = -low if negate else low

        for piece in range(2):
            def rows(offset):
                return near_ref[part, pl.ds(3 * piece * half + offset, half, stride=3), :]

            a, b, c = rows(0), rows(1), rows(2)
            bt, ct = pltpu.roll(b, 64, 1), pltpu.roll(c, 64, 1)
            own, cross = own_ref[pl.ds(part * half, half), :], cross_ref[pl.ds(part * half, half), :]
            hl = jnp.where(even_tile, cross, own) * has_left
            hr = jnp.where(even_tile, own, cross) * has_right
            if piece == 0:
                even_tail = jnp.where(low64, b, jnp.where(quarter == 2, pltpu.roll(hl, 32, 1), pltpu.roll(hr, 96, 1)))
                odd_tail = jnp.where(low64, ct, jnp.where(quarter == 2, pltpu.roll(hl, 96, 1), pltpu.roll(hr, 32, 1)))
            else:
                even_tail = jnp.where(low64, b, jnp.where(quarter == 2, pltpu.roll(hl, 64, 1), pltpu.roll(hr, 64, 1)))
                odd_tail = jnp.where(low64, ct, jnp.where(quarter == 2, hl, hr))
            odd_head = jnp.where(low64, bt, ct)
            for base, head, tail in ((0, a, even_tail), (CORE // 2, odd_head, odd_tail)):
                row = base + piece * half
                for col, block in ((0, head), (LANES, tail)):
                    high, low = split(block)
                    if part == 0:
                        put(row, col, high, low, False)
                        put(CORE + row, 256 + col, high, low, False)
                    else:
                        put(row, 256 + col, high, low, False)
                        put(CORE + row, col, high, low, True)

    mixed = product(fyh_ref[...], fyl_ref[...], wh_ref[...], wl_ref[...])
    mixed_high, mixed_low = split(mixed)
    spec = product(mixed_high, mixed_low, fxh_ref[...], fxl_ref[...])
    for k in range(4):
        spec_ref[k] = spec[:, k * LANES:(k + 1) * LANES]


def row_tables(rows_ref, phase_real, phase_imag, lh_ref, ll_ref):
    me = lax.axis_index("src")
    table = rows_ref[pl.ds(pl.multiple_of(me * ROWS, 8), HALO_ROWS), :]
    table_real = table[:, None, :LANES]
    table_imag = table[:, None, LANES:]
    left_real = (table_real * phase_real - table_imag * phase_imag).reshape(HALO_ROWS * DEPTHS, LANES)
    left_imag = (table_real * phase_imag + table_imag * phase_real).reshape(HALO_ROWS * DEPTHS, LANES)
    for k, block in ((0, left_real), (1, left_imag)):
        high, low = split(block)
        lh_ref[:, k * LANES:(k + 1) * LANES] = high
        ll_ref[:, k * LANES:(k + 1) * LANES] = low


def image_points(q_ref, phase_real, phase_imag, spec_ref, lh_ref, ll_ref, th_ref, tl_ref, acc_ref):
    rowbin = lax.broadcasted_iota(jnp.int32, (LANES, LANES), 0) - RADIUS
    colbin = lane_iota((LANES, LANES)) - RADIUS
    inside = rowbin * rowbin + colbin * colbin <= RADIUS * RADIUS
    lane_full = lane_iota((LANES, LANES))

    def point(n, carry):
        row, j = n // POINTS, n % POINTS
        start = (LOW - RADIUS) - q_ref[row, 2 * j].astype(jnp.int32)
        shift = (LOW - RADIUS) - q_ref[row, 2 * j + 1].astype(jnp.int32)
        amp = q_ref[row, 4 + j]

        def shifted(k):
            first = spec_ref[k, pl.ds(start, LANES), :]
            second = spec_ref[k + 1, pl.ds(start, LANES), :]
            turn = LANES - shift
            moved = jnp.where(lane_full < turn, pltpu.roll(first, turn, 1), pltpu.roll(second, turn, 1))
            return jnp.where(inside, moved * amp, 0.0)

        real, imag = shifted(0), shifted(2)
        real_high, real_low = split(real)
        imag_high, imag_low = split(imag)
        zh = jnp.concatenate([jnp.concatenate([real_high, imag_high], 1), jnp.concatenate([-imag_high, real_high], 1)], 0)
        zl = jnp.concatenate([jnp.concatenate([real_low, imag_low], 1), jnp.concatenate([-imag_low, real_low], 1)], 0)
        middle = product(lh_ref[...], ll_ref[...], zh, zl)
        shape = (HALO_ROWS, DEPTHS, LANES)
        mid_real = middle[:, :LANES].reshape(shape)
        mid_imag = middle[:, LANES:].reshape(shape)
        out_real = (mid_real * phase_real - mid_imag * phase_imag).reshape(-1, LANES)
        out_imag = (mid_real * phase_imag + mid_imag * phase_real).reshape(-1, LANES)
        rh, rl = split(out_real)
        ih, il = split(out_imag)
        image = product(jnp.concatenate([rh, ih], 1), jnp.concatenate([rl, il], 1), th_ref[...], tl_ref[...])
        acc_ref[...] += image * image
        return carry

    lax.fori_loop(0, SECTORS // 2 * POINTS, point, 0, unroll=UNROLL)


def first_kernel(
    near_ref, own_ref, cross_ref, q_ref, defocus_ref,
    fyh_ref, fyl_ref, fxh_ref, fxl_ref, th_ref, tl_ref, rows_ref,
    spec_ref, lh_ref, ll_ref, acc_ref, wh_ref, wl_ref,
):
    spectrum(near_ref, own_ref, cross_ref, fyh_ref, fyl_ref, fxh_ref, fxl_ref, spec_ref, wh_ref, wl_ref)
    phase_real, phase_imag = depth_phase(defocus_ref)
    row_tables(rows_ref, phase_real, phase_imag, lh_ref, ll_ref)
    acc_ref[...] = jnp.zeros_like(acc_ref)
    image_points(q_ref, phase_real, phase_imag, spec_ref, lh_ref, ll_ref, th_ref, tl_ref, acc_ref)


def second_kernel(
    spec_ref, lh_ref, ll_ref, sum_ref, th_ref, tl_ref, q_ref, defocus_ref, dose_ref,
    acid_ref, own_ref, cross_ref, acc_ref,
):
    phase_real, phase_imag = depth_phase(defocus_ref)
    acc_ref[...] = sum_ref[...]
    image_points(q_ref, phase_real, phase_imag, spec_ref, lh_ref, ll_ref, th_ref, tl_ref, acc_ref)
    dose = by_depth(dose_ref)
    shape = (HALO_ROWS, DEPTHS, LANES)
    acc = acc_ref[...]
    head = (acc[:, :128] + acc[:, 128:256]).reshape(shape)
    tail = acc[:, 256:]
    tail = (tail + pltpu.roll(tail, 64, 1)).reshape(shape)
    acid_head = 1.0 - jnp.exp(-dose * head)
    acid_tail = 1.0 - jnp.exp(-dose * tail)
    acid_ref[:, :, :LANES] = acid_head
    acid_ref[:, :, LANES:] = acid_tail
    lane1 = lane_iota((DEPTHS, LANES))
    left = jnp.zeros((DEPTHS, LANES), f32)
    right = jnp.zeros((DEPTHS, LANES), f32)
    for y in range(HALO_ROWS):
        here = (lane1 >= 4 * y) & (lane1 < 4 * y + 4)
        left = jnp.where(here, pltpu.roll(acid_head[y], 4 * y, 1) if y else acid_head[y], left)
        turn = (4 * y - 60) % LANES
        right = jnp.where(here, pltpu.roll(acid_tail[y], turn, 1) if turn else acid_tail[y], right)
    even_tile = lax.axis_index("tile") % 2 == 0
    own_ref[...] = jnp.where(even_tile, right, left)
    cross_ref[...] = jnp.where(even_tile, left, right)


def bake_kernel(acid_ref, own_ref, cross_ref, load_ref, out_ref):
    me = lax.axis_index("src")
    tile = lax.axis_index("tile")
    lane1 = lane_iota((DEPTHS, LANES))
    depth = lax.broadcasted_iota(jnp.int32, (DEPTHS, LANES), 0)
    load = jnp.zeros((DEPTHS, LANES), f32)
    for d in range(DEPTHS):
        load = jnp.where(depth == d, load_ref[d], load)
    has_left = (tile > 0).astype(f32)
    has_right = (tile < TILES - 1).astype(f32)
    left_cells = lane1 >= 124
    right_cells = (lane1 >= 64) & (lane1 < 68)
    keep_tail = jnp.where(lane1 < 64, 1.0, jnp.where(left_cells, has_left, jnp.where(right_cells, has_right, 0.0)))

    def keep_row(y):
        row = me * ROWS - BAKE_STEPS + y
        return ((row >= 0) & (row < CORE)).astype(f32)

    even_tile = tile % 2 == 0
    own, cross = own_ref[...], cross_ref[...]
    from_left, from_right = jnp.where(even_tile, cross, own), jnp.where(even_tile, own, cross)
    acid, quencher = [], []
    for y in range(HALO_ROWS):
        tail = acid_ref[y, :, LANES:]
        turn_left, turn_right = (124 - 4 * y) % LANES, (64 - 4 * y) % LANES
        moved_left = pltpu.roll(from_left, turn_left, 1) if turn_left else from_left
        moved_right = pltpu.roll(from_right, turn_right, 1) if turn_right else from_right
        tail = jnp.where(lane1 < 64, tail, jnp.where(left_cells, moved_left, moved_right)) * keep_tail
        head = acid_ref[y, :, :LANES]
        pair = [head, tail]
        loads = [load, load * keep_tail]
        if y < BAKE_STEPS or y >= HALO_ROWS - BAKE_STEPS:
            keep = keep_row(y)
            pair = [v * keep for v in pair]
            loads = [v * keep for v in loads]
        acid.append(pair)
        quencher.append(loads)

    first_lane, last_lane = lane1 == 0, lane1 == LANES - 1
    top, bottom = depth == 0, depth == DEPTHS - 1

    def spread(values, y, k, rate):
        here = values[y][k]
        other = values[y][1 - k]
        before = jnp.where(first_lane, pltpu.roll(other, 1, 1), pltpu.roll(here, 1, 1))
        after = jnp.where(last_lane, pltpu.roll(other, LANES - 1, 1), pltpu.roll(here, LANES - 1, 1))
        lateral = values[y + 1][k] + values[y - 1][k] + before + after - 4.0 * here
        above = jnp.where(top, here, pltpu.roll(here, 1, 0))
        below = jnp.where(bottom, here, pltpu.roll(here, DEPTHS - 1, 0))
        return here + rate * lateral + depth_rate * (above + below - 2.0 * here)

    for step in range(1, BAKE_STEPS + 1):
        next_acid, next_quencher = list(acid), list(quencher)
        for y in range(step, HALO_ROWS - step):
            pair, loads = [], []
            for k in range(2):
                reaction = react_rate * acid[y][k] * quencher[y][k]
                new_acid = spread(acid, y, k, acid_rate) - reaction
                pair.append(new_acid)
                if step < BAKE_STEPS:
                    loads.append(spread(quencher, y, k, quench_rate) - reaction)
            if step < BAKE_STEPS:
                pair[1] = pair[1] * keep_tail
                loads[1] = loads[1] * keep_tail
                if y < BAKE_STEPS or y >= HALO_ROWS - BAKE_STEPS:
                    keep = keep_row(y)
                    pair = [v * keep for v in pair]
                    loads = [v * keep for v in loads]
            next_acid[y] = pair
            next_quencher[y] = loads
        acid, quencher = next_acid, next_quencher

    low64 = lane1 < 64
    for k in range(ROWS // 2):
        even_head, even_tail = acid[BAKE_STEPS + 2 * k]
        odd_head, odd_tail = (pltpu.roll(v, 64, 1) for v in acid[BAKE_STEPS + 2 * k + 1])
        base = 384 * k
        out_ref[:, 0, base:base + 128] = even_head
        out_ref[:, 0, base + 128:base + 256] = jnp.where(low64, even_tail, odd_head)
        out_ref[:, 0, base + 256:base + 384] = jnp.where(low64, odd_head, odd_tail)


def vmem(n):
    return [pl.BlockSpec(memory_space=pltpu.VMEM)] * n


def smem(n):
    return [pl.BlockSpec(memory_space=pltpu.SMEM)] * n


def same(tile):
    return tile


def own_chip(tile):
    return tile ^ 1


def across(tile):
    if tile in (0, TILES - 1):
        return tile
    return tile + 1 if tile % 2 else tile - 1


def nearer_half(tile):
    return tile ^ (TILES // 2)


def route(turn, move, flip=0):
    pairs = []
    for s in range(SECTORS):
        upper, y = divmod(s, 4)
        target = (upper ^ flip) * 4 + (y + turn) % 4
        pairs += [(s * TILES + t, target * TILES + move(t)) for t in range(TILES)]
    return pairs


def on_device(near_field, source_shift, source_weight, defocus, dose, quencher_load):
    both = ("src", "tile")
    near = near_field.reshape(2, CORE * CORE // LANES, LANES)
    packed = jax.ShapeDtypeStruct((CORE // 2 + 8, LANES), f32)
    edge = jax.ShapeDtypeStruct((DEPTHS, LANES), f32)
    own, cross, points = pl.pallas_call(
        edges_kernel, out_shape=(packed, packed, edge), in_specs=vmem(1) + smem(2), out_specs=tuple(vmem(3)), name="edges"
    )(near, source_shift, source_weight)
    from_own = lax.ppermute(own, both, route(1, own_chip))
    turned = lax.ppermute(points, both, route(2, same))
    from_cross = lax.ppermute(cross, both, route(3, across))
    last = CORE // 2
    half_points = jnp.concatenate(
        [points[:1, :8], turned[:1, :8], from_own[last:last + 1, :8], from_cross[last:last + 1, :8]], 0
    )
    other_points = lax.ppermute(half_points, both, route(0, nearer_half, 1))

    columns = [jnp.asarray(v) for v in inverse_columns()]
    tables = [jnp.asarray(v) for v in (*forward_rows(), *forward_columns())]
    left_rows = jax.ShapeDtypeStruct((HALO_ROWS * DEPTHS, 256), bf16)
    total = jax.ShapeDtypeStruct((HALO_ROWS * DEPTHS, 384), f32)
    spec, lh, ll, acc = pl.pallas_call(
        first_kernel,
        out_shape=(jax.ShapeDtypeStruct((4, SPEC_ROWS, LANES), f32), left_rows, left_rows, total),
        in_specs=vmem(3) + smem(2) + vmem(7),
        out_specs=tuple(vmem(4)),
        scratch_shapes=[pltpu.VMEM((2 * CORE, 512), bf16), pltpu.VMEM((2 * CORE, 512), bf16)],
        cost_estimate=pl.CostEstimate(flops=8_000_000_000, bytes_accessed=4_000_000, transcendentals=0),
        name="first",
    )(near, from_own, from_cross, half_points, defocus, *tables, *columns, jnp.asarray(inverse_rows()))
    acid, own, cross = pl.pallas_call(
        second_kernel,
        out_shape=(jax.ShapeDtypeStruct((HALO_ROWS, DEPTHS, 256), f32), edge, edge),
        in_specs=vmem(6) + smem(3),
        out_specs=tuple(vmem(3)),
        scratch_shapes=[pltpu.VMEM(total.shape, f32)],
        name="second",
    )(spec, lh, ll, acc, *columns, other_points, defocus, dose)
    from_own = lax.ppermute(own, both, route(0, own_chip))
    from_cross = lax.ppermute(cross, both, route(0, across))
    return pl.pallas_call(
        bake_kernel,
        out_shape=jax.ShapeDtypeStruct((DEPTHS, 1, ROWS * CORE), f32),
        in_specs=vmem(3) + smem(1),
        out_specs=vmem(1)[0],
        name="bake",
    )(acid, from_own, from_cross, quencher_load)


def solution(mesh):
    return jax.shard_map(
        on_device,
        mesh=mesh,
        in_specs=(P(None, "tile", None), P("src", None, None), P("src", None), P(), P(), P()),
        out_specs=P(None, "tile", "src"),
        check_vma=False,
    )
```

```python
import numpy as np

import jax
import jax.numpy as jnp
from jax import lax
from jax.experimental import pallas as pl
from jax.experimental.pallas import tpu as pltpu
from jax.sharding import PartitionSpec as P

CORE = 192
MARGIN = 32
LENGTH = CORE + 2 * MARGIN
RADIUS = 48
DEPTHS = 8
BAKE_STEPS = 4
SECTORS = 8
TILES = 32
POINTS = 2
ROWS = CORE // SECTORS
HALO_ROWS = ROWS + 2 * BAKE_STEPS
LOW = 88
SPEC_ROWS = 208
LANES = 128
GROUP_SHIFT = 8
GROUP = 8
CHUNK = 128
TOGETHER = 8

acid_rate = 0.24
quench_rate = 0.12
depth_rate = 0.02
react_rate = 0.8

bf16 = jnp.bfloat16
f32 = jnp.float32


def two_parts(table):
    table = table.astype(np.float32)
    high = table.astype(bf16)
    low = (table - high.astype(np.float32)).astype(bf16)
    return high, low


def waves(left, right):
    angle = 2.0 * np.pi / LENGTH * (np.outer(left, right) % LENGTH)
    return np.cos(angle), np.sin(angle)


def forward_rows():
    order = np.concatenate([np.arange(0, CORE, 2), np.arange(1, CORE, 2)])
    real, imag = waves(np.arange(SPEC_ROWS) - LOW, order + MARGIN)
    return two_parts(np.concatenate([real, -imag], 1))


def forward_columns():
    order = np.concatenate(
        [np.arange(CORE) + MARGIN, np.arange(MARGIN), np.arange(MARGIN) + MARGIN + CORE]
    )
    real, imag = waves(order, np.arange(256) - LOW)
    imag = -imag
    return two_parts(np.block([[real, imag], [-imag, real]]))


def inverse_columns():
    bins = np.arange(LANES) - RADIUS
    real, imag = waves(bins, np.arange(CORE) + MARGIN)
    keep = (np.abs(bins) <= RADIUS)[:, None] / LENGTH
    real, imag = real * keep, imag * keep
    top = np.concatenate([real[:, :128], imag[:, :128], real[:, 128:], imag[:, 128:]], 1)
    low = np.concatenate([-imag[:, :128], real[:, :128], -imag[:, 128:], real[:, 128:]], 1)
    return two_parts(np.concatenate([top, low], 0))


def inverse_rows():
    bins = np.arange(LANES) - RADIUS
    rows = np.arange(CORE + 2 * BAKE_STEPS) - BAKE_STEPS + MARGIN
    real, imag = waves(rows, bins)
    keep = (np.abs(bins) <= RADIUS)[None, :] / LENGTH
    return np.concatenate([real * keep, imag * keep], 1).astype(np.float32)


def split(values):
    high = values.astype(bf16)
    low = (values - high.astype(f32)).astype(bf16)
    return high, low


def product(left_high, left_low, right_high, right_low):
    def dot(a, b):
        return jnp.dot(a, b, preferred_element_type=f32)

    return dot(left_high, right_high) + (dot(left_low, right_high) + dot(left_high, right_low))


def lane_iota(shape):
    return lax.broadcasted_iota(jnp.int32, shape, len(shape) - 1)


def edges_kernel(near_ref, shift_ref, weight_ref, own_ref, cross_ref, points_ref):
    half = CORE // 4
    even_tile = lax.axis_index("tile") % 2 == 0
    lane = lane_iota((half, LANES))
    odd = lane >= 64
    second = (lane % 64) >= 32
    for part in range(2):
        def rows(start, offset):
            return near_ref[part, pl.ds(3 * start + offset, half, stride=3), :]

        def right(start):
            return jnp.where(odd, rows(start, 2), rows(start, 1))

        def left(start):
            return jnp.where(odd, rows(start, 1), rows(start, 0))

        right_edge = jnp.where(second, right(0), pltpu.roll(right(half), 96, 1))
        left_edge = jnp.where(second, pltpu.roll(left(half), 32, 1), left(0))
        own_ref[pl.ds(part * half, half), :] = jnp.where(even_tile, right_edge, left_edge)
        cross_ref[pl.ds(part * half, half), :] = jnp.where(even_tile, left_edge, right_edge)

    lane1 = lane_iota((8, LANES))
    values = jnp.zeros((8, LANES), f32)
    for j in range(POINTS):
        for axis in range(2):
            values = jnp.where(lane1 == 2 * j + axis, shift_ref[0, j, axis].astype(f32), values)
    weights = jnp.ones((8, LANES), f32)
    for j in range(POINTS):
        weights = jnp.where(lane1 == 4 + j, weight_ref[0, j], weights)
    values = jnp.where(lane1 < 4, values, jnp.sqrt(weights))
    own_ref[pl.ds(2 * half, 8), :] = values
    cross_ref[pl.ds(2 * half, 8), :] = values
    points_ref[...] = values


def by_depth(ref):
    depth = lax.broadcasted_iota(jnp.int32, (DEPTHS, LANES), 0)
    out = jnp.zeros((DEPTHS, LANES), f32)
    for d in range(DEPTHS):
        out = jnp.where(depth == d, ref[d], out)
    return out


def depth_phase(defocus_ref):
    bins = lane_iota((DEPTHS, LANES)) - RADIUS
    phase = by_depth(defocus_ref) * (bins * bins).astype(f32) / float(RADIUS * RADIUS)
    return jnp.cos(phase), jnp.sin(phase)


def spectrum(near_ref, own_ref, cross_ref, fyh_ref, fyl_ref, fxh_ref, fxl_ref, spec_ref, wh_ref, wl_ref):
    tile = lax.axis_index("tile")
    even_tile = tile % 2 == 0
    has_left = (tile > 0).astype(f32)
    has_right = (tile < TILES - 1).astype(f32)
    half = CORE // 4
    lane = lane_iota((half, LANES))
    low64 = lane < 64
    quarter = lane // 32

    for part in range(2):
        def put(row, col, high, low, negate):
            rows = pl.ds(row, half)
            cols = pl.ds(col, LANES)
            wh_ref[rows, cols] = -high if negate else high
            wl_ref[rows, cols] = -low if negate else low

        for piece in range(2):
            def rows(offset):
                return near_ref[part, pl.ds(3 * piece * half + offset, half, stride=3), :]

            a, b, c = rows(0), rows(1), rows(2)
            bt, ct = pltpu.roll(b, 64, 1), pltpu.roll(c, 64, 1)
            own, cross = own_ref[pl.ds(part * half, half), :], cross_ref[pl.ds(part * half, half), :]
            hl = jnp.where(even_tile, cross, own) * has_left
            hr = jnp.where(even_tile, own, cross) * has_right
            if piece == 0:
                even_tail = jnp.where(low64, b, jnp.where(quarter == 2, pltpu.roll(hl, 32, 1), pltpu.roll(hr, 96, 1)))
                odd_tail = jnp.where(low64, ct, jnp.where(quarter == 2, pltpu.roll(hl, 96, 1), pltpu.roll(hr, 32, 1)))
            else:
                even_tail = jnp.where(low64, b, jnp.where(quarter == 2, pltpu.roll(hl, 64, 1), pltpu.roll(hr, 64, 1)))
                odd_tail = jnp.where(low64, ct, jnp.where(quarter == 2, hl, hr))
            odd_head = jnp.where(low64, bt, ct)
            for base, head, tail in ((0, a, even_tail), (CORE // 2, odd_head, odd_tail)):
                row = base + piece * half
                for col, block in ((0, head), (LANES, tail)):
                    high, low = split(block)
                    if part == 0:
                        put(row, col, high, low, False)
                        put(CORE + row, 256 + col, high, low, False)
                    else:
                        put(row, 256 + col, high, low, False)
                        put(CORE + row, col, high, low, True)

    mixed = product(fyh_ref[...], fyl_ref[...], wh_ref[...], wl_ref[...])
    mixed_high, mixed_low = split(mixed)
    spec = product(mixed_high, mixed_low, fxh_ref[...], fxl_ref[...])
    for k in range(4):
        spec_ref[k] = spec[:, k * LANES:(k + 1) * LANES]


def row_tables(rows_ref, phase_real, phase_imag, left_ref):
    me = lax.axis_index("src")
    table = rows_ref[pl.ds(pl.multiple_of(me * ROWS, 8), HALO_ROWS), :]
    table_real = table[:, None, :LANES]
    table_imag = table[:, None, LANES:]
    left_real = (table_real * phase_real - table_imag * phase_imag).reshape(HALO_ROWS * DEPTHS, LANES)
    left_imag = (table_real * phase_imag + table_imag * phase_real).reshape(HALO_ROWS * DEPTHS, LANES)
    for k, block in ((0, left_real), (1, left_imag)):
        high, low = split(block)
        left_ref[:HALO_ROWS * DEPTHS, k * LANES:(k + 1) * LANES] = high
        left_ref[HALO_ROWS * DEPTHS:, k * LANES:(k + 1) * LANES] = low


def image_points(q_ref, phase_real, phase_imag, spec_ref, left_ref, columns_ref, shifted_ref, mid_ref):
    rowbin = lax.broadcasted_iota(jnp.int32, (LANES, LANES), 0) - RADIUS
    colbin = lane_iota((LANES, LANES)) - RADIUS
    inside = rowbin * rowbin + colbin * colbin <= RADIUS * RADIUS
    lane_full = lane_iota((LANES, LANES))
    rows = HALO_ROWS * DEPTHS
    shape = (HALO_ROWS, DEPTHS, LANES)

    def shift_spectrum(n):
        row, j = n // POINTS, n % POINTS
        start = (LOW - RADIUS) - q_ref[row, 2 * j].astype(jnp.int32)
        shift = (LOW - RADIUS) - q_ref[row, 2 * j + 1].astype(jnp.int32)
        amp = q_ref[row, 4 + j]
        turn = LANES - shift
        for k in range(2):
            first = spec_ref[2 * k, pl.ds(start, LANES), :]
            second = spec_ref[2 * k + 1, pl.ds(start, LANES), :]
            moved = jnp.where(lane_full < turn, pltpu.roll(first, turn, 1), pltpu.roll(second, turn, 1))
            for part, value in enumerate(split(jnp.where(inside, moved * amp, 0.0))):
                shifted_ref[n, part, :LANES, k * LANES:(k + 1) * LANES] = value
                shifted_ref[n, part, LANES:, (1 - k) * LANES:(2 - k) * LANES] = -value if k else value

    def transform_rows(n):
        both = jnp.dot(left_ref[...], shifted_ref[n, 0], preferred_element_type=f32)
        low = jnp.dot(left_ref[:rows, :], shifted_ref[n, 1], preferred_element_type=f32)
        middle = both[:rows] + (both[rows:] + low)
        mid_real = middle[:, :LANES].reshape(shape)
        mid_imag = middle[:, LANES:].reshape(shape)
        out_real = (mid_real * phase_real - mid_imag * phase_imag).reshape(rows, LANES)
        out_imag = (mid_real * phase_imag + mid_imag * phase_real).reshape(rows, LANES)
        for k, value in enumerate((out_real, out_imag)):
            high, low = split(value)
            mid_ref[n, :, k * LANES:(k + 1) * LANES] = high
            mid_ref[n, :, (2 + k) * LANES:(3 + k) * LANES] = low

    points = SECTORS // 2 * POINTS

    def in_groups(size, body):
        if size == points:
            for n in range(points):
                body(n)
        else:
            @pl.loop(0, points // size)
            def _(g):
                for n in range(size):
                    body(g * size + n)

    in_groups(GROUP_SHIFT, shift_spectrum)
    in_groups(GROUP, transform_rows)

    sums = []
    for c in range(rows // CHUNK):
        total = None
        for n in range(0, points, TOGETHER):
            part = mid_ref[n:n + TOGETHER, c * CHUNK:(c + 1) * CHUNK, :].reshape(TOGETHER * CHUNK, 512)
            part = jnp.concatenate([part, part[:, :256]], 1)
            image = jnp.dot(part, columns_ref[...], preferred_element_type=f32)
            power = (image * image).reshape(TOGETHER, CHUNK, 384)
            for k in range(TOGETHER):
                total = power[k] if total is None else total + power[k]
        sums.append(total)
    return sums


def first_kernel(
    near_ref, own_ref, cross_ref, q_ref, defocus_ref, fyh_ref, fyl_ref, fxh_ref, fxl_ref, columns_ref, rows_ref,
    spec_ref, left_ref, sum_ref, wh_ref, wl_ref, shifted_ref, mid_ref,
):
    spectrum(near_ref, own_ref, cross_ref, fyh_ref, fyl_ref, fxh_ref, fxl_ref, spec_ref, wh_ref, wl_ref)
    phase_real, phase_imag = depth_phase(defocus_ref)
    row_tables(rows_ref, phase_real, phase_imag, left_ref)
    for c, value in enumerate(image_points(q_ref, phase_real, phase_imag, spec_ref, left_ref, columns_ref, shifted_ref, mid_ref)):
        sum_ref[c * CHUNK:(c + 1) * CHUNK, :] = value


def second_kernel(
    spec_ref, left_ref, sum_ref, columns_ref, q_ref, defocus_ref, dose_ref, acid_ref, own_ref, cross_ref, shifted_ref, mid_ref
):
    phase_real, phase_imag = depth_phase(defocus_ref)
    sums = image_points(q_ref, phase_real, phase_imag, spec_ref, left_ref, columns_ref, shifted_ref, mid_ref)
    dose = by_depth(dose_ref)
    shape = (HALO_ROWS, DEPTHS, LANES)
    acc = jnp.concatenate([sum_ref[c * CHUNK:(c + 1) * CHUNK, :] + value for c, value in enumerate(sums)], 0)
    head = (acc[:, :128] + acc[:, 128:256]).reshape(shape)
    tail = acc[:, 256:]
    tail = (tail + pltpu.roll(tail, 64, 1)).reshape(shape)
    acid_head = 1.0 - jnp.exp(-dose * head)
    acid_tail = 1.0 - jnp.exp(-dose * tail)
    acid_ref[:, :, :LANES] = acid_head
    acid_ref[:, :, LANES:] = acid_tail
    lane1 = lane_iota((DEPTHS, LANES))
    left = jnp.zeros((DEPTHS, LANES), f32)
    right = jnp.zeros((DEPTHS, LANES), f32)
    for y in range(HALO_ROWS):
        here = (lane1 >= 4 * y) & (lane1 < 4 * y + 4)
        left = jnp.where(here, pltpu.roll(acid_head[y], 4 * y, 1) if y else acid_head[y], left)
        turn = (4 * y - 60) % LANES
        right = jnp.where(here, pltpu.roll(acid_tail[y], turn, 1) if turn else acid_tail[y], right)
    even_tile = lax.axis_index("tile") % 2 == 0
    own_ref[...] = jnp.where(even_tile, right, left)
    cross_ref[...] = jnp.where(even_tile, left, right)


def bake_kernel(acid_ref, own_ref, cross_ref, load_ref, out_ref):
    me = lax.axis_index("src")
    tile = lax.axis_index("tile")
    lane1 = lane_iota((DEPTHS, LANES))
    depth = lax.broadcasted_iota(jnp.int32, (DEPTHS, LANES), 0)
    load = jnp.zeros((DEPTHS, LANES), f32)
    for d in range(DEPTHS):
        load = jnp.where(depth == d, load_ref[d], load)
    has_left = (tile > 0).astype(f32)
    has_right = (tile < TILES - 1).astype(f32)
    left_cells = lane1 >= 124
    right_cells = (lane1 >= 64) & (lane1 < 68)
    keep_tail = jnp.where(lane1 < 64, 1.0, jnp.where(left_cells, has_left, jnp.where(right_cells, has_right, 0.0)))

    def keep_row(y):
        row = me * ROWS - BAKE_STEPS + y
        return ((row >= 0) & (row < CORE)).astype(f32)

    even_tile = tile % 2 == 0
    own, cross = own_ref[...], cross_ref[...]
    from_left, from_right = jnp.where(even_tile, cross, own), jnp.where(even_tile, own, cross)
    acid, quencher = [], []
    for y in range(HALO_ROWS):
        tail = acid_ref[y, :, LANES:]
        turn_left, turn_right = (124 - 4 * y) % LANES, (64 - 4 * y) % LANES
        moved_left = pltpu.roll(from_left, turn_left, 1) if turn_left else from_left
        moved_right = pltpu.roll(from_right, turn_right, 1) if turn_right else from_right
        tail = jnp.where(lane1 < 64, tail, jnp.where(left_cells, moved_left, moved_right)) * keep_tail
        head = acid_ref[y, :, :LANES]
        pair = [head, tail]
        loads = [load, load * keep_tail]
        if y < BAKE_STEPS or y >= HALO_ROWS - BAKE_STEPS:
            keep = keep_row(y)
            pair = [v * keep for v in pair]
            loads = [v * keep for v in loads]
        acid.append(pair)
        quencher.append(loads)

    first_lane, last_lane = lane1 == 0, lane1 == LANES - 1
    top, bottom = depth == 0, depth == DEPTHS - 1

    def spread(values, y, k, rate):
        here = values[y][k]
        other = values[y][1 - k]
        before = jnp.where(first_lane, pltpu.roll(other, 1, 1), pltpu.roll(here, 1, 1))
        after = jnp.where(last_lane, pltpu.roll(other, LANES - 1, 1), pltpu.roll(here, LANES - 1, 1))
        lateral = values[y + 1][k] + values[y - 1][k] + before + after - 4.0 * here
        above = jnp.where(top, here, pltpu.roll(here, 1, 0))
        below = jnp.where(bottom, here, pltpu.roll(here, DEPTHS - 1, 0))
        return here + rate * lateral + depth_rate * (above + below - 2.0 * here)

    for step in range(1, BAKE_STEPS + 1):
        next_acid, next_quencher = list(acid), list(quencher)
        for y in range(step, HALO_ROWS - step):
            pair, loads = [], []
            for k in range(2):
                reaction = react_rate * acid[y][k] * quencher[y][k]
                new_acid = spread(acid, y, k, acid_rate) - reaction
                pair.append(new_acid)
                if step < BAKE_STEPS:
                    loads.append(spread(quencher, y, k, quench_rate) - reaction)
            if step < BAKE_STEPS:
                pair[1] = pair[1] * keep_tail
                loads[1] = loads[1] * keep_tail
                if y < BAKE_STEPS or y >= HALO_ROWS - BAKE_STEPS:
                    keep = keep_row(y)
                    pair = [v * keep for v in pair]
                    loads = [v * keep for v in loads]
            next_acid[y] = pair
            next_quencher[y] = loads
        acid, quencher = next_acid, next_quencher

    low64 = lane1 < 64
    for k in range(ROWS // 2):
        even_head, even_tail = acid[BAKE_STEPS + 2 * k]
        odd_head, odd_tail = (pltpu.roll(v, 64, 1) for v in acid[BAKE_STEPS + 2 * k + 1])
        base = 384 * k
        out_ref[:, 0, base:base + 128] = even_head
        out_ref[:, 0, base + 128:base + 256] = jnp.where(low64, even_tail, odd_head)
        out_ref[:, 0, base + 256:base + 384] = jnp.where(low64, odd_head, odd_tail)


def vmem(n):
    return [pl.BlockSpec(memory_space=pltpu.VMEM)] * n


def smem(n):
    return [pl.BlockSpec(memory_space=pltpu.SMEM)] * n


def same(tile):
    return tile


def own_chip(tile):
    return tile ^ 1


def across(tile):
    if tile in (0, TILES - 1):
        return tile
    return tile + 1 if tile % 2 else tile - 1


def nearer_half(tile):
    return tile ^ (TILES // 2)


def route(turn, move, flip=0):
    pairs = []
    for s in range(SECTORS):
        upper, y = divmod(s, 4)
        target = (upper ^ flip) * 4 + (y + turn) % 4
        pairs += [(s * TILES + t, target * TILES + move(t)) for t in range(TILES)]
    return pairs


def on_device(near_field, source_shift, source_weight, defocus, dose, quencher_load):
    both = ("src", "tile")
    near = near_field.reshape(2, CORE * CORE // LANES, LANES)
    packed = jax.ShapeDtypeStruct((CORE // 2 + 8, LANES), f32)
    edge = jax.ShapeDtypeStruct((DEPTHS, LANES), f32)
    own, cross, points = pl.pallas_call(
        edges_kernel, out_shape=(packed, packed, edge), in_specs=vmem(1) + smem(2), out_specs=tuple(vmem(3)), name="edges"
    )(near, source_shift, source_weight)
    from_own = lax.ppermute(own, both, route(1, own_chip))
    turned = lax.ppermute(points, both, route(2, same))
    from_cross = lax.ppermute(cross, both, route(3, across))
    last = CORE // 2
    half_points = jnp.concatenate(
        [points[:1, :8], turned[:1, :8], from_own[last:last + 1, :8], from_cross[last:last + 1, :8]], 0
    )
    other_points = lax.ppermute(half_points, both, route(0, nearer_half, 1))

    high, low = inverse_columns()
    columns = jnp.asarray(np.concatenate([high, high, low], 0))
    tables = [jnp.asarray(v) for v in (*forward_rows(), *forward_columns())]
    rows = HALO_ROWS * DEPTHS
    total = jax.ShapeDtypeStruct((rows, 384), f32)
    shifted = pltpu.VMEM((SECTORS // 2 * POINTS, 2, 256, 256), bf16)
    middle = pltpu.VMEM((SECTORS // 2 * POINTS, rows, 512), bf16)
    spec, left, acc = pl.pallas_call(
        first_kernel,
        out_shape=(
            jax.ShapeDtypeStruct((4, SPEC_ROWS, LANES), f32), jax.ShapeDtypeStruct((2 * rows, 256), bf16), total
        ),
        in_specs=vmem(3) + smem(2) + vmem(6),
        out_specs=tuple(vmem(3)),
        scratch_shapes=[pltpu.VMEM((2 * CORE, 512), bf16), pltpu.VMEM((2 * CORE, 512), bf16), shifted, middle],
        cost_estimate=pl.CostEstimate(flops=8_000_000_000, bytes_accessed=4_000_000, transcendentals=0),
        name="first",
    )(near, from_own, from_cross, half_points, defocus, *tables, columns, jnp.asarray(inverse_rows()))
    acid, own, cross = pl.pallas_call(
        second_kernel,
        out_shape=(jax.ShapeDtypeStruct((HALO_ROWS, DEPTHS, 256), f32), edge, edge),
        in_specs=vmem(4) + smem(3),
        out_specs=tuple(vmem(3)),
        scratch_shapes=[shifted, middle],
        name="second",
    )(spec, left, acc, columns, other_points, defocus, dose)
    from_own = lax.ppermute(own, both, route(0, own_chip))
    from_cross = lax.ppermute(cross, both, route(0, across))
    return pl.pallas_call(
        bake_kernel,
        out_shape=jax.ShapeDtypeStruct((DEPTHS, 1, ROWS * CORE), f32),
        in_specs=vmem(3) + smem(1),
        out_specs=vmem(1)[0],
        name="bake",
    )(acid, from_own, from_cross, quencher_load)


def solution(mesh):
    return jax.shard_map(
        on_device,
        mesh=mesh,
        in_specs=(P(None, "tile", None), P("src", None, None), P("src", None), P(), P(), P()),
        out_specs=P(None, "tile", "src"),
        check_vma=False,
    )
```

```python
import numpy as np

import jax
import jax.numpy as jnp
from jax import lax
from jax.experimental import pallas as pl
from jax.experimental.pallas import tpu as pltpu
from jax.sharding import PartitionSpec as P

CORE = 192
MARGIN = 32
LENGTH = CORE + 2 * MARGIN
RADIUS = 48
DEPTHS = 8
BAKE_STEPS = 4
SECTORS = 8
TILES = 32
POINTS = 2
ROWS = CORE // SECTORS
HALO_ROWS = ROWS + 2 * BAKE_STEPS
LOW = 88
SPEC_ROWS = 208
LANES = 128
GROUP_SHIFT = 8
GROUP = 8
CHUNK = 128
TOGETHER = 8

acid_rate = 0.24
quench_rate = 0.12
depth_rate = 0.02
react_rate = 0.8

bf16 = jnp.bfloat16
f32 = jnp.float32


def two_parts(table):
    table = table.astype(np.float32)
    high = table.astype(bf16)
    low = (table - high.astype(np.float32)).astype(bf16)
    return high, low


def waves(left, right):
    angle = 2.0 * np.pi / LENGTH * (np.outer(left, right) % LENGTH)
    return np.cos(angle), np.sin(angle)


def forward_rows():
    order = np.concatenate([np.arange(0, CORE, 2), np.arange(1, CORE, 2)])
    real, imag = waves(np.arange(SPEC_ROWS) - LOW, order + MARGIN)
    return two_parts(np.concatenate([real, -imag], 1))


def forward_columns():
    order = np.concatenate(
        [np.arange(CORE) + MARGIN, np.arange(MARGIN), np.arange(MARGIN) + MARGIN + CORE]
    )
    real, imag = waves(order, np.arange(256) - LOW)
    imag = -imag
    return two_parts(np.block([[real, imag], [-imag, real]]))


def inverse_columns():
    bins = np.arange(LANES) - RADIUS
    real, imag = waves(bins, np.arange(CORE) + MARGIN)
    keep = (np.abs(bins) <= RADIUS)[:, None] / LENGTH
    real, imag = real * keep, imag * keep
    top = np.concatenate([real[:, :128], imag[:, :128], real[:, 128:], imag[:, 128:]], 1)
    low = np.concatenate([-imag[:, :128], real[:, :128], -imag[:, 128:], real[:, 128:]], 1)
    return two_parts(np.concatenate([top, low], 0))


def inverse_rows():
    bins = np.arange(LANES) - RADIUS
    rows = np.arange(CORE + 2 * BAKE_STEPS) - BAKE_STEPS + MARGIN
    real, imag = waves(rows, bins)
    keep = (np.abs(bins) <= RADIUS)[None, :] / LENGTH
    return np.concatenate([real * keep, imag * keep], 1).astype(np.float32)


def split(values):
    high = values.astype(bf16)
    low = (values - high.astype(f32)).astype(bf16)
    return high, low


def product(left_high, left_low, right_high, right_low):
    def dot(a, b):
        return jnp.dot(a, b, preferred_element_type=f32)

    return dot(left_high, right_high) + (dot(left_low, right_high) + dot(left_high, right_low))


def lane_iota(shape):
    return lax.broadcasted_iota(jnp.int32, shape, len(shape) - 1)


def edges_kernel(
    near_hbm, shift_hbm, weight_hbm, own_ref, cross_ref, points_ref, near_ref, shift_ref, weight_ref, sems
):
    copies = [
        pltpu.make_async_copy(source, target, sems.at[k])
        for k, (source, target) in enumerate(
            ((near_hbm, near_ref), (shift_hbm, shift_ref), (weight_hbm, weight_ref))
        )
    ]
    for copy in copies:
        copy.start()
    for copy in copies:
        copy.wait()
    half = CORE // 4
    even_tile = lax.axis_index("tile") % 2 == 0
    lane = lane_iota((half, LANES))
    odd = lane >= 64
    second = (lane % 64) >= 32
    for part in range(2):
        def rows(start, offset):
            return near_ref[part, pl.ds(3 * start + offset, half, stride=3), :]

        def right(start):
            return jnp.where(odd, rows(start, 2), rows(start, 1))

        def left(start):
            return jnp.where(odd, rows(start, 1), rows(start, 0))

        right_edge = jnp.where(second, right(0), pltpu.roll(right(half), 96, 1))
        left_edge = jnp.where(second, pltpu.roll(left(half), 32, 1), left(0))
        own_ref[pl.ds(part * half, half), :] = jnp.where(even_tile, right_edge, left_edge)
        cross_ref[pl.ds(part * half, half), :] = jnp.where(even_tile, left_edge, right_edge)

    lane1 = lane_iota((8, LANES))
    values = jnp.zeros((8, LANES), f32)
    for j in range(POINTS):
        for axis in range(2):
            values = jnp.where(lane1 == 2 * j + axis, shift_ref[0, j, axis].astype(f32), values)
    weights = jnp.ones((8, LANES), f32)
    for j in range(POINTS):
        weights = jnp.where(lane1 == 4 + j, weight_ref[0, j], weights)
    values = jnp.where(lane1 < 4, values, jnp.sqrt(weights))
    own_ref[pl.ds(2 * half, 8), :] = values
    cross_ref[pl.ds(2 * half, 8), :] = values
    points_ref[...] = values


def by_depth(ref):
    depth = lax.broadcasted_iota(jnp.int32, (DEPTHS, LANES), 0)
    out = jnp.zeros((DEPTHS, LANES), f32)
    for d in range(DEPTHS):
        out = jnp.where(depth == d, ref[d], out)
    return out


def depth_phase(defocus_ref):
    bins = lane_iota((DEPTHS, LANES)) - RADIUS
    phase = by_depth(defocus_ref) * (bins * bins).astype(f32) / float(RADIUS * RADIUS)
    return jnp.cos(phase), jnp.sin(phase)


def spectrum(near_ref, own_ref, cross_ref, fyh_ref, fyl_ref, fxh_ref, fxl_ref, spec_ref, wh_ref, wl_ref):
    tile = lax.axis_index("tile")
    even_tile = tile % 2 == 0
    has_left = (tile > 0).astype(f32)
    has_right = (tile < TILES - 1).astype(f32)
    half = CORE // 4
    lane = lane_iota((half, LANES))
    low64 = lane < 64
    quarter = lane // 32

    for part in range(2):
        def put(row, col, high, low, negate):
            rows = pl.ds(row, half)
            cols = pl.ds(col, LANES)
            wh_ref[rows, cols] = -high if negate else high
            wl_ref[rows, cols] = -low if negate else low

        for piece in range(2):
            def rows(offset):
                return near_ref[part, pl.ds(3 * piece * half + offset, half, stride=3), :]

            a, b, c = rows(0), rows(1), rows(2)
            bt, ct = pltpu.roll(b, 64, 1), pltpu.roll(c, 64, 1)
            own, cross = own_ref[pl.ds(part * half, half), :], cross_ref[pl.ds(part * half, half), :]
            hl = jnp.where(even_tile, cross, own) * has_left
            hr = jnp.where(even_tile, own, cross) * has_right
            if piece == 0:
                even_tail = jnp.where(low64, b, jnp.where(quarter == 2, pltpu.roll(hl, 32, 1), pltpu.roll(hr, 96, 1)))
                odd_tail = jnp.where(low64, ct, jnp.where(quarter == 2, pltpu.roll(hl, 96, 1), pltpu.roll(hr, 32, 1)))
            else:
                even_tail = jnp.where(low64, b, jnp.where(quarter == 2, pltpu.roll(hl, 64, 1), pltpu.roll(hr, 64, 1)))
                odd_tail = jnp.where(low64, ct, jnp.where(quarter == 2, hl, hr))
            odd_head = jnp.where(low64, bt, ct)
            for base, head, tail in ((0, a, even_tail), (CORE // 2, odd_head, odd_tail)):
                row = base + piece * half
                for col, block in ((0, head), (LANES, tail)):
                    high, low = split(block)
                    if part == 0:
                        put(row, col, high, low, False)
                        put(CORE + row, 256 + col, high, low, False)
                    else:
                        put(row, 256 + col, high, low, False)
                        put(CORE + row, col, high, low, True)

    mixed = product(fyh_ref[...], fyl_ref[...], wh_ref[...], wl_ref[...])
    mixed_high, mixed_low = split(mixed)
    spec = product(mixed_high, mixed_low, fxh_ref[...], fxl_ref[...])
    for k in range(4):
        spec_ref[k] = spec[:, k * LANES:(k + 1) * LANES]


def row_tables(rows_ref, phase_real, phase_imag, left_ref):
    me = lax.axis_index("src")
    table = rows_ref[pl.ds(pl.multiple_of(me * ROWS, 8), HALO_ROWS), :]
    table_real = table[:, None, :LANES]
    table_imag = table[:, None, LANES:]
    left_real = (table_real * phase_real - table_imag * phase_imag).reshape(HALO_ROWS * DEPTHS, LANES)
    left_imag = (table_real * phase_imag + table_imag * phase_real).reshape(HALO_ROWS * DEPTHS, LANES)
    for k, block in ((0, left_real), (1, left_imag)):
        high, low = split(block)
        left_ref[:HALO_ROWS * DEPTHS, k * LANES:(k + 1) * LANES] = high
        left_ref[HALO_ROWS * DEPTHS:, k * LANES:(k + 1) * LANES] = low


def image_points(q_ref, phase_real, phase_imag, spec_ref, left_ref, columns_ref, shifted_ref, mid_ref):
    rowbin = lax.broadcasted_iota(jnp.int32, (LANES, LANES), 0) - RADIUS
    colbin = lane_iota((LANES, LANES)) - RADIUS
    inside = rowbin * rowbin + colbin * colbin <= RADIUS * RADIUS
    lane_full = lane_iota((LANES, LANES))
    rows = HALO_ROWS * DEPTHS
    shape = (HALO_ROWS, DEPTHS, LANES)

    def shift_spectrum(n):
        row, j = n // POINTS, n % POINTS
        start = (LOW - RADIUS) - q_ref[row, 2 * j].astype(jnp.int32)
        shift = (LOW - RADIUS) - q_ref[row, 2 * j + 1].astype(jnp.int32)
        amp = q_ref[row, 4 + j]
        turn = LANES - shift
        for k in range(2):
            first = spec_ref[2 * k, pl.ds(start, LANES), :]
            second = spec_ref[2 * k + 1, pl.ds(start, LANES), :]
            moved = jnp.where(lane_full < turn, pltpu.roll(first, turn, 1), pltpu.roll(second, turn, 1))
            for part, value in enumerate(split(jnp.where(inside, moved * amp, 0.0))):
                shifted_ref[n, part, :LANES, k * LANES:(k + 1) * LANES] = value
                shifted_ref[n, part, LANES:, (1 - k) * LANES:(2 - k) * LANES] = -value if k else value

    def transform_rows(n):
        both = jnp.dot(left_ref[...], shifted_ref[n, 0], preferred_element_type=f32)
        low = jnp.dot(left_ref[:rows, :], shifted_ref[n, 1], preferred_element_type=f32)
        middle = both[:rows] + (both[rows:] + low)
        mid_real = middle[:, :LANES].reshape(shape)
        mid_imag = middle[:, LANES:].reshape(shape)
        out_real = (mid_real * phase_real - mid_imag * phase_imag).reshape(rows, LANES)
        out_imag = (mid_real * phase_imag + mid_imag * phase_real).reshape(rows, LANES)
        for k, value in enumerate((out_real, out_imag)):
            high, low = split(value)
            mid_ref[n, :, k * LANES:(k + 1) * LANES] = high
            mid_ref[n, :, (2 + k) * LANES:(3 + k) * LANES] = low

    points = SECTORS // 2 * POINTS

    def in_groups(size, body):
        if size == points:
            for n in range(points):
                body(n)
        else:
            @pl.loop(0, points // size)
            def _(g):
                for n in range(size):
                    body(g * size + n)

    in_groups(GROUP_SHIFT, shift_spectrum)
    in_groups(GROUP, transform_rows)

    sums = []
    for c in range(rows // CHUNK):
        total = None
        for n in range(0, points, TOGETHER):
            part = mid_ref[n:n + TOGETHER, c * CHUNK:(c + 1) * CHUNK, :].reshape(TOGETHER * CHUNK, 512)
            part = jnp.concatenate([part, part[:, :256]], 1)
            image = jnp.dot(part, columns_ref[...], preferred_element_type=f32)
            power = (image * image).reshape(TOGETHER, CHUNK, 384)
            for k in range(TOGETHER):
                total = power[k] if total is None else total + power[k]
        sums.append(total)
    return sums


def prepare_kernel(
    defocus_ref, dose_ref, load_ref, fyh_hbm, fyl_hbm, fxh_hbm, fxl_hbm, columns_hbm, rows_hbm,
    fyh_ref, fyl_ref, fxh_ref, fxl_ref, columns_ref, left_ref, depth_ref, rows_ref, sems,
):
    pairs = (
        (rows_hbm, rows_ref), (fyh_hbm, fyh_ref), (fyl_hbm, fyl_ref), (fxh_hbm, fxh_ref), (fxl_hbm, fxl_ref),
        (columns_hbm, columns_ref),
    )
    copies = [pltpu.make_async_copy(source, target, sems.at[k]) for k, (source, target) in enumerate(pairs)]
    for copy in copies:
        copy.start()
    phase_real, phase_imag = depth_phase(defocus_ref)
    depth_ref[0], depth_ref[1] = phase_real, phase_imag
    depth_ref[2], depth_ref[3] = by_depth(dose_ref), by_depth(load_ref)
    copies[0].wait()
    row_tables(rows_ref, phase_real, phase_imag, left_ref)
    for copy in copies[1:]:
        copy.wait()


def first_kernel(
    near_ref, own_ref, cross_ref, q_ref, depth_ref, fyh_ref, fyl_ref, fxh_ref, fxl_ref, columns_ref, left_ref,
    spec_ref, sum_ref, wh_ref, wl_ref, shifted_ref, mid_ref,
):
    spectrum(near_ref, own_ref, cross_ref, fyh_ref, fyl_ref, fxh_ref, fxl_ref, spec_ref, wh_ref, wl_ref)
    phases = depth_ref[0], depth_ref[1]
    sums = image_points(q_ref, *phases, spec_ref, left_ref, columns_ref, shifted_ref, mid_ref)
    for c, value in enumerate(sums):
        sum_ref[c * CHUNK:(c + 1) * CHUNK, :] = value


def second_kernel(
    spec_ref, left_ref, sum_ref, columns_ref, depth_ref, q_ref, acid_ref, own_ref, cross_ref, shifted_ref, mid_ref
):
    phases = depth_ref[0], depth_ref[1]
    sums = image_points(q_ref, *phases, spec_ref, left_ref, columns_ref, shifted_ref, mid_ref)
    dose = depth_ref[2]
    shape = (HALO_ROWS, DEPTHS, LANES)
    acc = jnp.concatenate([sum_ref[c * CHUNK:(c + 1) * CHUNK, :] + value for c, value in enumerate(sums)], 0)
    head = (acc[:, :128] + acc[:, 128:256]).reshape(shape)
    tail = acc[:, 256:]
    tail = (tail + pltpu.roll(tail, 64, 1)).reshape(shape)
    acid_head = 1.0 - jnp.exp(-dose * head)
    acid_tail = 1.0 - jnp.exp(-dose * tail)
    acid_ref[:, :, :LANES] = acid_head
    acid_ref[:, :, LANES:] = acid_tail
    lane1 = lane_iota((DEPTHS, LANES))
    left = jnp.zeros((DEPTHS, LANES), f32)
    right = jnp.zeros((DEPTHS, LANES), f32)
    for y in range(HALO_ROWS):
        here = (lane1 >= 4 * y) & (lane1 < 4 * y + 4)
        left = jnp.where(here, pltpu.roll(acid_head[y], 4 * y, 1) if y else acid_head[y], left)
        turn = (4 * y - 60) % LANES
        right = jnp.where(here, pltpu.roll(acid_tail[y], turn, 1) if turn else acid_tail[y], right)
    even_tile = lax.axis_index("tile") % 2 == 0
    own_ref[...] = jnp.where(even_tile, right, left)
    cross_ref[...] = jnp.where(even_tile, left, right)


def bake_kernel(acid_ref, own_ref, cross_ref, depth_ref, out_ref):
    me = lax.axis_index("src")
    tile = lax.axis_index("tile")
    lane1 = lane_iota((DEPTHS, LANES))
    depth = lax.broadcasted_iota(jnp.int32, (DEPTHS, LANES), 0)
    load = depth_ref[3]
    has_left = (tile > 0).astype(f32)
    has_right = (tile < TILES - 1).astype(f32)
    left_cells = lane1 >= 124
    right_cells = (lane1 >= 64) & (lane1 < 68)
    keep_tail = jnp.where(lane1 < 64, 1.0, jnp.where(left_cells, has_left, jnp.where(right_cells, has_right, 0.0)))

    def keep_row(y):
        row = me * ROWS - BAKE_STEPS + y
        return ((row >= 0) & (row < CORE)).astype(f32)

    even_tile = tile % 2 == 0
    own, cross = own_ref[...], cross_ref[...]
    from_left, from_right = jnp.where(even_tile, cross, own), jnp.where(even_tile, own, cross)
    acid, quencher = [], []
    for y in range(HALO_ROWS):
        tail = acid_ref[y, :, LANES:]
        turn_left, turn_right = (124 - 4 * y) % LANES, (64 - 4 * y) % LANES
        moved_left = pltpu.roll(from_left, turn_left, 1) if turn_left else from_left
        moved_right = pltpu.roll(from_right, turn_right, 1) if turn_right else from_right
        tail = jnp.where(lane1 < 64, tail, jnp.where(left_cells, moved_left, moved_right)) * keep_tail
        head = acid_ref[y, :, :LANES]
        pair = [head, tail]
        loads = [load, load * keep_tail]
        if y < BAKE_STEPS or y >= HALO_ROWS - BAKE_STEPS:
            keep = keep_row(y)
            pair = [v * keep for v in pair]
            loads = [v * keep for v in loads]
        acid.append(pair)
        quencher.append(loads)

    first_lane, last_lane = lane1 == 0, lane1 == LANES - 1
    top, bottom = depth == 0, depth == DEPTHS - 1

    def spread(values, y, k, rate):
        here = values[y][k]
        other = values[y][1 - k]
        before = jnp.where(first_lane, pltpu.roll(other, 1, 1), pltpu.roll(here, 1, 1))
        after = jnp.where(last_lane, pltpu.roll(other, LANES - 1, 1), pltpu.roll(here, LANES - 1, 1))
        lateral = values[y + 1][k] + values[y - 1][k] + before + after - 4.0 * here
        above = jnp.where(top, here, pltpu.roll(here, 1, 0))
        below = jnp.where(bottom, here, pltpu.roll(here, DEPTHS - 1, 0))
        return here + rate * lateral + depth_rate * (above + below - 2.0 * here)

    for step in range(1, BAKE_STEPS + 1):
        next_acid, next_quencher = list(acid), list(quencher)
        for y in range(step, HALO_ROWS - step):
            pair, loads = [], []
            for k in range(2):
                reaction = react_rate * acid[y][k] * quencher[y][k]
                new_acid = spread(acid, y, k, acid_rate) - reaction
                pair.append(new_acid)
                if step < BAKE_STEPS:
                    loads.append(spread(quencher, y, k, quench_rate) - reaction)
            if step < BAKE_STEPS:
                pair[1] = pair[1] * keep_tail
                loads[1] = loads[1] * keep_tail
                if y < BAKE_STEPS or y >= HALO_ROWS - BAKE_STEPS:
                    keep = keep_row(y)
                    pair = [v * keep for v in pair]
                    loads = [v * keep for v in loads]
            next_acid[y] = pair
            next_quencher[y] = loads
        acid, quencher = next_acid, next_quencher

    low64 = lane1 < 64
    for k in range(ROWS // 2):
        even_head, even_tail = acid[BAKE_STEPS + 2 * k]
        odd_head, odd_tail = (pltpu.roll(v, 64, 1) for v in acid[BAKE_STEPS + 2 * k + 1])
        base = 384 * k
        out_ref[:, 0, base:base + 128] = even_head
        out_ref[:, 0, base + 128:base + 256] = jnp.where(low64, even_tail, odd_head)
        out_ref[:, 0, base + 256:base + 384] = jnp.where(low64, odd_head, odd_tail)


def vmem(n):
    return [pl.BlockSpec(memory_space=pltpu.VMEM)] * n


def hbm(n):
    return [pl.BlockSpec(memory_space=pltpu.HBM)] * n


def in_hbm(values):
    return pltpu.with_memory_space_constraint(values, pltpu.HBM)


def grant(mib):
    return pltpu.CompilerParams(vmem_limit_bytes=mib * 2**20)


def smem(n):
    return [pl.BlockSpec(memory_space=pltpu.SMEM)] * n


def same(tile):
    return tile


def own_chip(tile):
    return tile ^ 1


def across(tile):
    if tile in (0, TILES - 1):
        return tile
    return tile + 1 if tile % 2 else tile - 1


def nearer_half(tile):
    return tile ^ (TILES // 2)


def route(turn, move, flip=0):
    pairs = []
    for s in range(SECTORS):
        upper, y = divmod(s, 4)
        target = (upper ^ flip) * 4 + (y + turn) % 4
        pairs += [(s * TILES + t, target * TILES + move(t)) for t in range(TILES)]
    return pairs


def on_device(near_field, source_shift, source_weight, defocus, dose, quencher_load):
    both = ("src", "tile")
    near = near_field.reshape(2, CORE * CORE // LANES, LANES)
    packed = jax.ShapeDtypeStruct((CORE // 2 + 8, LANES), f32)
    edge = jax.ShapeDtypeStruct((DEPTHS, LANES), f32)
    own, cross, points = pl.pallas_call(
        edges_kernel,
        out_shape=(packed, packed, edge),
        in_specs=hbm(3),
        out_specs=tuple(vmem(3)),
        scratch_shapes=[
            pltpu.VMEM(near.shape, f32),
            pltpu.SMEM(source_shift.shape, jnp.int32),
            pltpu.SMEM(source_weight.shape, f32),
            pltpu.SemaphoreType.DMA((3,)),
        ],
        compiler_params=grant(8),
        name="edges",
    )(in_hbm(near), in_hbm(source_shift), in_hbm(source_weight))
    from_own = lax.ppermute(own, both, route(1, own_chip))
    turned = lax.ppermute(points, both, route(2, same))
    from_cross = lax.ppermute(cross, both, route(3, across))
    last = CORE // 2
    half_points = jnp.concatenate(
        [points[:1, :8], turned[:1, :8], from_own[last:last + 1, :8], from_cross[last:last + 1, :8]], 0
    )
    other_points = lax.ppermute(half_points, both, route(0, nearer_half, 1))

    high, low = inverse_columns()
    tables = [*forward_rows(), *forward_columns(), np.concatenate([high, high, low], 0)]
    rows = HALO_ROWS * DEPTHS
    *tables, left, depth = pl.pallas_call(
        prepare_kernel,
        out_shape=(
            *(jax.ShapeDtypeStruct(v.shape, bf16) for v in tables),
            jax.ShapeDtypeStruct((2 * rows, 256), bf16),
            jax.ShapeDtypeStruct((4, DEPTHS, LANES), f32),
        ),
        in_specs=smem(3) + hbm(6),
        out_specs=tuple(vmem(7)),
        scratch_shapes=[pltpu.VMEM((CORE + 2 * BAKE_STEPS, 256), f32), pltpu.SemaphoreType.DMA((6,))],
        compiler_params=grant(4),
        cost_estimate=pl.CostEstimate(flops=1_000_000, bytes_accessed=5_000_000, transcendentals=0),
        name="prepare",
    )(defocus, dose, quencher_load, *(in_hbm(jnp.asarray(v)) for v in (*tables, inverse_rows())))
    columns = tables[-1]
    total = jax.ShapeDtypeStruct((rows, 384), f32)
    shifted = pltpu.VMEM((SECTORS // 2 * POINTS, 2, 256, 256), bf16)
    middle = pltpu.VMEM((SECTORS // 2 * POINTS, rows, 512), bf16)
    window = pltpu.VMEM((2 * CORE, 512), bf16)
    spec, acc = pl.pallas_call(
        first_kernel,
        out_shape=(jax.ShapeDtypeStruct((4, SPEC_ROWS, LANES), f32), total),
        in_specs=vmem(3) + smem(1) + vmem(7),
        out_specs=tuple(vmem(2)),
        scratch_shapes=[window, window, shifted, middle],
        cost_estimate=pl.CostEstimate(flops=8_000_000_000, bytes_accessed=4_000_000, transcendentals=0),
        compiler_params=grant(24),
        name="first",
    )(near, from_own, from_cross, half_points, depth, *tables, left)
    acid, own, cross = pl.pallas_call(
        second_kernel,
        out_shape=(jax.ShapeDtypeStruct((HALO_ROWS, DEPTHS, 256), f32), edge, edge),
        in_specs=vmem(5) + smem(1),
        out_specs=tuple(vmem(3)),
        scratch_shapes=[shifted, middle],
        compiler_params=grant(24),
        name="second",
    )(spec, left, acc, columns, depth, other_points)
    from_own = lax.ppermute(own, both, route(0, own_chip))
    from_cross = lax.ppermute(cross, both, route(0, across))
    return pl.pallas_call(
        bake_kernel,
        out_shape=jax.ShapeDtypeStruct((DEPTHS, 1, ROWS * CORE), f32),
        in_specs=vmem(4),
        out_specs=vmem(1)[0],
        compiler_params=grant(8),
        name="bake",
    )(acid, from_own, from_cross, depth)


def solution(mesh):
    return jax.shard_map(
        on_device,
        mesh=mesh,
        in_specs=(P(None, "tile", None), P("src", None, None), P("src", None), P(), P(), P()),
        out_specs=P(None, "tile", "src"),
        check_vma=False,
    )
```

```python
import numpy as np

import jax
import jax.numpy as jnp
from jax import lax
from jax.experimental import pallas as pl
from jax.experimental.pallas import tpu as pltpu
from jax.sharding import PartitionSpec as P

CORE = 192
MARGIN = 32
LENGTH = CORE + 2 * MARGIN
RADIUS = 48
DEPTHS = 8
BAKE_STEPS = 4
SECTORS = 8
TILES = 32
POINTS = 2
ROWS = CORE // SECTORS
HALO_ROWS = ROWS + 2 * BAKE_STEPS
LOW = 88
SPEC_ROWS = 208
LANES = 128
GROUP_SHIFT = 8
GROUP = 8
CHUNK = 128
TOGETHER = 8

acid_rate = 0.24
quench_rate = 0.12
depth_rate = 0.02
react_rate = 0.8

bf16 = jnp.bfloat16
f32 = jnp.float32


def two_parts(table):
    table = table.astype(np.float32)
    high = table.astype(bf16)
    low = (table - high.astype(np.float32)).astype(bf16)
    return high, low


def waves(left, right):
    angle = 2.0 * np.pi / LENGTH * (np.outer(left, right) % LENGTH)
    return np.cos(angle), np.sin(angle)


def forward_rows():
    order = np.concatenate([np.arange(0, CORE, 2), np.arange(1, CORE, 2)])
    real, imag = waves(np.arange(SPEC_ROWS) - LOW, order + MARGIN)
    return two_parts(np.concatenate([real, -imag], 1))


def forward_columns():
    order = np.concatenate(
        [np.arange(CORE) + MARGIN, np.arange(MARGIN), np.arange(MARGIN) + MARGIN + CORE]
    )
    real, imag = waves(order, np.arange(256) - LOW)
    imag = -imag
    return two_parts(np.block([[real, imag], [-imag, real]]))


def inverse_columns():
    bins = np.arange(LANES) - RADIUS
    real, imag = waves(bins, np.arange(CORE) + MARGIN)
    keep = (np.abs(bins) <= RADIUS)[:, None] / LENGTH
    real, imag = real * keep, imag * keep
    top = np.concatenate([real[:, :128], imag[:, :128], real[:, 128:], imag[:, 128:]], 1)
    low = np.concatenate([-imag[:, :128], real[:, :128], -imag[:, 128:], real[:, 128:]], 1)
    return two_parts(np.concatenate([top, low], 0))


def inverse_rows():
    bins = np.arange(LANES) - RADIUS
    rows = np.arange(CORE + 2 * BAKE_STEPS) - BAKE_STEPS + MARGIN
    real, imag = waves(rows, bins)
    keep = (np.abs(bins) <= RADIUS)[None, :] / LENGTH
    return np.concatenate([real * keep, imag * keep], 1).astype(np.float32)


def split(values):
    high = values.astype(bf16)
    low = (values - high.astype(f32)).astype(bf16)
    return high, low


def product(left_high, left_low, right_high, right_low):
    def dot(a, b):
        return jnp.dot(a, b, preferred_element_type=f32)

    return dot(left_high, right_high) + (dot(left_low, right_high) + dot(left_high, right_low))


def lane_iota(shape):
    return lax.broadcasted_iota(jnp.int32, shape, len(shape) - 1)


def edges_kernel(
    near_hbm, shift_hbm, weight_hbm, own_ref, cross_ref, points_ref, near_ref, shift_ref, weight_ref, sems
):
    copies = [
        pltpu.make_async_copy(source, target, sems.at[k])
        for k, (source, target) in enumerate(
            ((near_hbm, near_ref), (shift_hbm, shift_ref), (weight_hbm, weight_ref))
        )
    ]
    for copy in copies:
        copy.start()
    for copy in copies:
        copy.wait()
    half = CORE // 4
    even_tile = lax.axis_index("tile") % 2 == 0
    lane = lane_iota((half, LANES))
    odd = lane >= 64
    second = (lane % 64) >= 32
    for part in range(2):
        def rows(start, offset):
            return near_ref[part, pl.ds(3 * start + offset, half, stride=3), :]

        def right(start):
            return jnp.where(odd, rows(start, 2), rows(start, 1))

        def left(start):
            return jnp.where(odd, rows(start, 1), rows(start, 0))

        right_edge = jnp.where(second, right(0), pltpu.roll(right(half), 96, 1))
        left_edge = jnp.where(second, pltpu.roll(left(half), 32, 1), left(0))
        own_ref[pl.ds(part * half, half), :] = jnp.where(even_tile, right_edge, left_edge)
        cross_ref[pl.ds(part * half, half), :] = jnp.where(even_tile, left_edge, right_edge)

    lane1 = lane_iota((8, LANES))
    values = jnp.zeros((8, LANES), f32)
    for j in range(POINTS):
        for axis in range(2):
            values = jnp.where(lane1 == 2 * j + axis, shift_ref[0, j, axis].astype(f32), values)
    weights = jnp.ones((8, LANES), f32)
    for j in range(POINTS):
        weights = jnp.where(lane1 == 4 + j, weight_ref[0, j], weights)
    values = jnp.where(lane1 < 4, values, jnp.sqrt(weights))
    own_ref[pl.ds(2 * half, 8), :] = values
    cross_ref[pl.ds(2 * half, 8), :] = values
    points_ref[...] = values


def by_depth(ref):
    depth = lax.broadcasted_iota(jnp.int32, (DEPTHS, LANES), 0)
    out = jnp.zeros((DEPTHS, LANES), f32)
    for d in range(DEPTHS):
        out = jnp.where(depth == d, ref[d], out)
    return out


def depth_phase(defocus_ref):
    bins = lane_iota((DEPTHS, LANES)) - RADIUS
    phase = by_depth(defocus_ref) * (bins * bins).astype(f32) / float(RADIUS * RADIUS)
    return jnp.cos(phase), jnp.sin(phase)


def spectrum(near_ref, own_ref, cross_ref, fyh_ref, fyl_ref, fxh_ref, fxl_ref, spec_ref, wh_ref, wl_ref):
    tile = lax.axis_index("tile")
    even_tile = tile % 2 == 0
    has_left = (tile > 0).astype(f32)
    has_right = (tile < TILES - 1).astype(f32)
    half = CORE // 4
    lane = lane_iota((half, LANES))
    low64 = lane < 64
    quarter = lane // 32

    for part in range(2):
        def put(row, col, high, low, negate):
            rows = pl.ds(row, half)
            cols = pl.ds(col, LANES)
            wh_ref[rows, cols] = -high if negate else high
            wl_ref[rows, cols] = -low if negate else low

        for piece in range(2):
            def rows(offset):
                return near_ref[part, pl.ds(3 * piece * half + offset, half, stride=3), :]

            a, b, c = rows(0), rows(1), rows(2)
            bt, ct = pltpu.roll(b, 64, 1), pltpu.roll(c, 64, 1)
            own, cross = own_ref[pl.ds(part * half, half), :], cross_ref[pl.ds(part * half, half), :]
            hl = jnp.where(even_tile, cross, own) * has_left
            hr = jnp.where(even_tile, own, cross) * has_right
            if piece == 0:
                even_tail = jnp.where(low64, b, jnp.where(quarter == 2, pltpu.roll(hl, 32, 1), pltpu.roll(hr, 96, 1)))
                odd_tail = jnp.where(low64, ct, jnp.where(quarter == 2, pltpu.roll(hl, 96, 1), pltpu.roll(hr, 32, 1)))
            else:
                even_tail = jnp.where(low64, b, jnp.where(quarter == 2, pltpu.roll(hl, 64, 1), pltpu.roll(hr, 64, 1)))
                odd_tail = jnp.where(low64, ct, jnp.where(quarter == 2, hl, hr))
            odd_head = jnp.where(low64, bt, ct)
            for base, head, tail in ((0, a, even_tail), (CORE // 2, odd_head, odd_tail)):
                row = base + piece * half
                for col, block in ((0, head), (LANES, tail)):
                    high, low = split(block)
                    if part == 0:
                        put(row, col, high, low, False)
                        put(CORE + row, 256 + col, high, low, False)
                    else:
                        put(row, 256 + col, high, low, False)
                        put(CORE + row, col, high, low, True)

    mixed = product(fyh_ref[...], fyl_ref[...], wh_ref[...], wl_ref[...])
    mixed_high, mixed_low = split(mixed)
    spec = product(mixed_high, mixed_low, fxh_ref[...], fxl_ref[...])
    for k in range(4):
        spec_ref[k] = spec[:, k * LANES:(k + 1) * LANES]


def row_tables(rows_ref, phase_real, phase_imag, left_ref):
    me = lax.axis_index("src")
    table = rows_ref[pl.ds(pl.multiple_of(me * ROWS, 8), HALO_ROWS), :]
    table_real = table[:, None, :LANES]
    table_imag = table[:, None, LANES:]
    left_real = (table_real * phase_real - table_imag * phase_imag).reshape(HALO_ROWS * DEPTHS, LANES)
    left_imag = (table_real * phase_imag + table_imag * phase_real).reshape(HALO_ROWS * DEPTHS, LANES)
    for k, block in ((0, left_real), (1, left_imag)):
        high, low = split(block)
        left_ref[:HALO_ROWS * DEPTHS, k * LANES:(k + 1) * LANES] = high
        left_ref[HALO_ROWS * DEPTHS:, k * LANES:(k + 1) * LANES] = low


def image_points(q_ref, phase_real, phase_imag, spec_ref, left_ref, columns_ref, shifted_ref, mid_ref):
    rowbin = lax.broadcasted_iota(jnp.int32, (LANES, LANES), 0) - RADIUS
    colbin = lane_iota((LANES, LANES)) - RADIUS
    inside = rowbin * rowbin + colbin * colbin <= RADIUS * RADIUS
    lane_full = lane_iota((LANES, LANES))
    rows = HALO_ROWS * DEPTHS
    shape = (HALO_ROWS, DEPTHS, LANES)

    def shift_spectrum(n):
        row, j = n // POINTS, n % POINTS
        start = (LOW - RADIUS) - q_ref[row, 2 * j].astype(jnp.int32)
        shift = (LOW - RADIUS) - q_ref[row, 2 * j + 1].astype(jnp.int32)
        amp = q_ref[row, 4 + j]
        turn = LANES - shift
        for k in range(2):
            first = spec_ref[2 * k, pl.ds(start, LANES), :]
            second = spec_ref[2 * k + 1, pl.ds(start, LANES), :]
            moved = jnp.where(lane_full < turn, pltpu.roll(first, turn, 1), pltpu.roll(second, turn, 1))
            for part, value in enumerate(split(jnp.where(inside, moved * amp, 0.0))):
                shifted_ref[n, part, :LANES, k * LANES:(k + 1) * LANES] = value
                shifted_ref[n, part, LANES:, (1 - k) * LANES:(2 - k) * LANES] = -value if k else value

    def transform_rows(n):
        both = jnp.dot(left_ref[...], shifted_ref[n, 0], preferred_element_type=f32)
        low = jnp.dot(left_ref[:rows, :], shifted_ref[n, 1], preferred_element_type=f32)
        middle = both[:rows] + (both[rows:] + low)
        mid_real = middle[:, :LANES].reshape(shape)
        mid_imag = middle[:, LANES:].reshape(shape)
        out_real = (mid_real * phase_real - mid_imag * phase_imag).reshape(rows, LANES)
        out_imag = (mid_real * phase_imag + mid_imag * phase_real).reshape(rows, LANES)
        for k, value in enumerate((out_real, out_imag)):
            high, low = split(value)
            mid_ref[n, :, k * LANES:(k + 1) * LANES] = high
            mid_ref[n, :, (2 + k) * LANES:(3 + k) * LANES] = low

    points = SECTORS // 2 * POINTS

    def in_groups(size, body):
        if size == points:
            for n in range(points):
                body(n)
        else:
            @pl.loop(0, points // size)
            def _(g):
                for n in range(size):
                    body(g * size + n)

    in_groups(GROUP_SHIFT, shift_spectrum)
    in_groups(GROUP, transform_rows)

    sums = []
    for c in range(rows // CHUNK):
        total = None
        for n in range(0, points, TOGETHER):
            part = mid_ref[n:n + TOGETHER, c * CHUNK:(c + 1) * CHUNK, :].reshape(TOGETHER * CHUNK, 512)
            part = jnp.concatenate([part, part[:, :256]], 1)
            image = jnp.dot(part, columns_ref[...], preferred_element_type=f32)
            power = (image * image).reshape(TOGETHER, CHUNK, 384)
            for k in range(TOGETHER):
                total = power[k] if total is None else total + power[k]
        sums.append(total)
    return sums


def prepare_kernel(
    defocus_ref, dose_ref, load_ref, fyh_hbm, fyl_hbm, fxh_hbm, fxl_hbm, columns_hbm, rows_hbm,
    fyh_ref, fyl_ref, fxh_ref, fxl_ref, columns_ref, left_ref, depth_ref, rows_ref, sems,
):
    pairs = (
        (rows_hbm, rows_ref), (fyh_hbm, fyh_ref), (fyl_hbm, fyl_ref), (fxh_hbm, fxh_ref), (fxl_hbm, fxl_ref),
        (columns_hbm, columns_ref),
    )
    copies = [pltpu.make_async_copy(source, target, sems.at[k]) for k, (source, target) in enumerate(pairs)]
    for copy in copies:
        copy.start()
    phase_real, phase_imag = depth_phase(defocus_ref)
    depth_ref[0], depth_ref[1] = phase_real, phase_imag
    depth_ref[2], depth_ref[3] = by_depth(dose_ref), by_depth(load_ref)
    copies[0].wait()
    row_tables(rows_ref, phase_real, phase_imag, left_ref)
    for copy in copies[1:]:
        copy.wait()


def first_kernel(
    near_ref, own_ref, cross_ref, q_ref, depth_ref, fyh_ref, fyl_ref, fxh_ref, fxl_ref, columns_ref, left_ref,
    spec_ref, sum_ref, wh_ref, wl_ref, shifted_ref, mid_ref,
):
    spectrum(near_ref, own_ref, cross_ref, fyh_ref, fyl_ref, fxh_ref, fxl_ref, spec_ref, wh_ref, wl_ref)
    phases = depth_ref[0], depth_ref[1]
    sums = image_points(q_ref, *phases, spec_ref, left_ref, columns_ref, shifted_ref, mid_ref)
    for c, value in enumerate(sums):
        sum_ref[c * CHUNK:(c + 1) * CHUNK, :] = value


def second_kernel(
    spec_ref, left_ref, sum_ref, columns_ref, depth_ref, q_ref, acid_ref, own_ref, cross_ref, shifted_ref, mid_ref
):
    phases = depth_ref[0], depth_ref[1]
    sums = image_points(q_ref, *phases, spec_ref, left_ref, columns_ref, shifted_ref, mid_ref)
    dose = depth_ref[2]
    shape = (HALO_ROWS, DEPTHS, LANES)
    acc = jnp.concatenate([sum_ref[c * CHUNK:(c + 1) * CHUNK, :] + value for c, value in enumerate(sums)], 0)
    head = (acc[:, :128] + acc[:, 128:256]).reshape(shape)
    tail = acc[:, 256:]
    tail = (tail + pltpu.roll(tail, 64, 1)).reshape(shape)
    acid_head = 1.0 - jnp.exp(-dose * head)
    acid_tail = 1.0 - jnp.exp(-dose * tail)
    acid_ref[:, :, :LANES] = acid_head
    acid_ref[:, :, LANES:] = acid_tail
    lane1 = lane_iota((DEPTHS, LANES))
    left = jnp.zeros((DEPTHS, LANES), f32)
    right = jnp.zeros((DEPTHS, LANES), f32)
    for y in range(HALO_ROWS):
        here = (lane1 >= 4 * y) & (lane1 < 4 * y + 4)
        left = jnp.where(here, pltpu.roll(acid_head[y], 4 * y, 1) if y else acid_head[y], left)
        turn = (4 * y - 60) % LANES
        right = jnp.where(here, pltpu.roll(acid_tail[y], turn, 1) if turn else acid_tail[y], right)
    even_tile = lax.axis_index("tile") % 2 == 0
    own_ref[...] = jnp.where(even_tile, right, left)
    cross_ref[...] = jnp.where(even_tile, left, right)


def bake_kernel(acid_ref, own_ref, cross_ref, depth_ref, out_ref):
    me = lax.axis_index("src")
    tile = lax.axis_index("tile")
    lane1 = lane_iota((DEPTHS, LANES))
    depth = lax.broadcasted_iota(jnp.int32, (DEPTHS, LANES), 0)
    load = depth_ref[3]
    has_left = (tile > 0).astype(f32)
    has_right = (tile < TILES - 1).astype(f32)
    left_cells = lane1 >= 124
    right_cells = (lane1 >= 64) & (lane1 < 68)
    keep_tail = jnp.where(lane1 < 64, 1.0, jnp.where(left_cells, has_left, jnp.where(right_cells, has_right, 0.0)))

    def keep_row(y):
        row = me * ROWS - BAKE_STEPS + y
        return ((row >= 0) & (row < CORE)).astype(f32)

    even_tile = tile % 2 == 0
    own, cross = own_ref[...], cross_ref[...]
    from_left, from_right = jnp.where(even_tile, cross, own), jnp.where(even_tile, own, cross)
    acid, quencher = [], []
    for y in range(HALO_ROWS):
        tail = acid_ref[y, :, LANES:]
        turn_left, turn_right = (124 - 4 * y) % LANES, (64 - 4 * y) % LANES
        moved_left = pltpu.roll(from_left, turn_left, 1) if turn_left else from_left
        moved_right = pltpu.roll(from_right, turn_right, 1) if turn_right else from_right
        tail = jnp.where(lane1 < 64, tail, jnp.where(left_cells, moved_left, moved_right)) * keep_tail
        head = acid_ref[y, :, :LANES]
        pair = [head, tail]
        loads = [load, load * keep_tail]
        if y < BAKE_STEPS or y >= HALO_ROWS - BAKE_STEPS:
            keep = keep_row(y)
            pair = [v * keep for v in pair]
            loads = [v * keep for v in loads]
        acid.append(pair)
        quencher.append(loads)

    first_lane, last_lane = lane1 == 0, lane1 == LANES - 1
    top, bottom = depth == 0, depth == DEPTHS - 1

    def spread(values, y, k, rate):
        here = values[y][k]
        other = values[y][1 - k]
        before = jnp.where(first_lane, pltpu.roll(other, 1, 1), pltpu.roll(here, 1, 1))
        after = jnp.where(last_lane, pltpu.roll(other, LANES - 1, 1), pltpu.roll(here, LANES - 1, 1))
        lateral = values[y + 1][k] + values[y - 1][k] + (before + after)
        above = jnp.where(top, here, pltpu.roll(here, 1, 0))
        below = jnp.where(bottom, here, pltpu.roll(here, DEPTHS - 1, 0))
        spread_value = rate * lateral + depth_rate * (above + below)
        rest = round(1.0 - 4.0 * rate - 2.0 * depth_rate, 12)
        return spread_value + rest * here if rest else spread_value

    for step in range(1, BAKE_STEPS + 1):
        next_acid, next_quencher = list(acid), list(quencher)
        for y in range(step, HALO_ROWS - step):
            pair, loads = [], []
            for k in range(2):
                reaction = react_rate * acid[y][k] * quencher[y][k]
                new_acid = spread(acid, y, k, acid_rate) - reaction
                pair.append(new_acid)
                if step < BAKE_STEPS:
                    loads.append(spread(quencher, y, k, quench_rate) - reaction)
            if step < BAKE_STEPS:
                pair[1] = pair[1] * keep_tail
                loads[1] = loads[1] * keep_tail
                if y < BAKE_STEPS or y >= HALO_ROWS - BAKE_STEPS:
                    keep = keep_row(y)
                    pair = [v * keep for v in pair]
                    loads = [v * keep for v in loads]
            next_acid[y] = pair
            next_quencher[y] = loads
        acid, quencher = next_acid, next_quencher

    low64 = lane1 < 64
    for k in range(ROWS // 2):
        even_head, even_tail = acid[BAKE_STEPS + 2 * k]
        odd_head, odd_tail = (pltpu.roll(v, 64, 1) for v in acid[BAKE_STEPS + 2 * k + 1])
        base = 384 * k
        out_ref[:, 0, base:base + 128] = even_head
        out_ref[:, 0, base + 128:base + 256] = jnp.where(low64, even_tail, odd_head)
        out_ref[:, 0, base + 256:base + 384] = jnp.where(low64, odd_head, odd_tail)


def vmem(n):
    return [pl.BlockSpec(memory_space=pltpu.VMEM)] * n


def hbm(n):
    return [pl.BlockSpec(memory_space=pltpu.HBM)] * n


def in_hbm(values):
    return pltpu.with_memory_space_constraint(values, pltpu.HBM)


def grant(mib):
    return pltpu.CompilerParams(vmem_limit_bytes=mib * 2**20)


def smem(n):
    return [pl.BlockSpec(memory_space=pltpu.SMEM)] * n


def same(tile):
    return tile


def own_chip(tile):
    return tile ^ 1


def across(tile):
    if tile in (0, TILES - 1):
        return tile
    return tile + 1 if tile % 2 else tile - 1


def nearer_half(tile):
    return tile ^ (TILES // 2)


def route(turn, move, flip=0):
    pairs = []
    for s in range(SECTORS):
        upper, y = divmod(s, 4)
        target = (upper ^ flip) * 4 + (y + turn) % 4
        for t in range(TILES):
            source, place = s * TILES + t, target * TILES + move(t)
            pairs.append((source, (s ^ 1) * TILES + t if place == source else place))
    return pairs


def on_device(near_field, source_shift, source_weight, defocus, dose, quencher_load):
    both = ("src", "tile")
    near = near_field.reshape(2, CORE * CORE // LANES, LANES)
    packed = jax.ShapeDtypeStruct((CORE // 2 + 8, LANES), f32)
    edge = jax.ShapeDtypeStruct((DEPTHS, LANES), f32)
    own, cross, points = pl.pallas_call(
        edges_kernel,
        out_shape=(packed, packed, edge),
        in_specs=hbm(3),
        out_specs=tuple(vmem(3)),
        scratch_shapes=[
            pltpu.VMEM(near.shape, f32),
            pltpu.SMEM(source_shift.shape, jnp.int32),
            pltpu.SMEM(source_weight.shape, f32),
            pltpu.SemaphoreType.DMA((3,)),
        ],
        compiler_params=grant(8),
        name="edges",
    )(in_hbm(near), in_hbm(source_shift), in_hbm(source_weight))
    from_own = lax.ppermute(own, both, route(1, own_chip))
    turned = lax.ppermute(points, both, route(2, same))
    from_cross = lax.ppermute(cross, both, route(3, across))
    last = CORE // 2
    half_points = jnp.concatenate(
        [points[:1, :8], turned[:1, :8], from_own[last:last + 1, :8], from_cross[last:last + 1, :8]], 0
    )
    other_points = lax.ppermute(half_points, both, route(0, nearer_half, 1))

    high, low = inverse_columns()
    tables = [*forward_rows(), *forward_columns(), np.concatenate([high, high, low], 0)]
    rows = HALO_ROWS * DEPTHS
    *tables, left, depth = pl.pallas_call(
        prepare_kernel,
        out_shape=(
            *(jax.ShapeDtypeStruct(v.shape, bf16) for v in tables),
            jax.ShapeDtypeStruct((2 * rows, 256), bf16),
            jax.ShapeDtypeStruct((4, DEPTHS, LANES), f32),
        ),
        in_specs=smem(3) + hbm(6),
        out_specs=tuple(vmem(7)),
        scratch_shapes=[pltpu.VMEM((CORE + 2 * BAKE_STEPS, 256), f32), pltpu.SemaphoreType.DMA((6,))],
        compiler_params=grant(4),
        cost_estimate=pl.CostEstimate(flops=1_000_000, bytes_accessed=5_000_000, transcendentals=0),
        name="prepare",
    )(defocus, dose, quencher_load, *(in_hbm(jnp.asarray(v)) for v in (*tables, inverse_rows())))
    columns = tables[-1]
    total = jax.ShapeDtypeStruct((rows, 384), f32)
    shifted = pltpu.VMEM((SECTORS // 2 * POINTS, 2, 256, 256), bf16)
    middle = pltpu.VMEM((SECTORS // 2 * POINTS, rows, 512), bf16)
    window = pltpu.VMEM((2 * CORE, 512), bf16)
    spec, acc = pl.pallas_call(
        first_kernel,
        out_shape=(jax.ShapeDtypeStruct((4, SPEC_ROWS, LANES), f32), total),
        in_specs=vmem(3) + smem(1) + vmem(7),
        out_specs=tuple(vmem(2)),
        scratch_shapes=[window, window, shifted, middle],
        cost_estimate=pl.CostEstimate(flops=8_000_000_000, bytes_accessed=4_000_000, transcendentals=0),
        compiler_params=grant(24),
        name="first",
    )(near, from_own, from_cross, half_points, depth, *tables, left)
    acid, own, cross = pl.pallas_call(
        second_kernel,
        out_shape=(jax.ShapeDtypeStruct((HALO_ROWS, DEPTHS, 256), f32), edge, edge),
        in_specs=vmem(5) + smem(1),
        out_specs=tuple(vmem(3)),
        scratch_shapes=[shifted, middle],
        compiler_params=grant(24),
        name="second",
    )(spec, left, acc, columns, depth, other_points)
    from_own = lax.ppermute(own, both, route(0, own_chip))
    from_cross = lax.ppermute(cross, both, route(0, across))
    return pl.pallas_call(
        bake_kernel,
        out_shape=jax.ShapeDtypeStruct((DEPTHS, 1, ROWS * CORE), f32),
        in_specs=vmem(4),
        out_specs=vmem(1)[0],
        compiler_params=grant(8),
        name="bake",
    )(acid, from_own, from_cross, depth)


def solution(mesh):
    return jax.shard_map(
        on_device,
        mesh=mesh,
        in_specs=(P(None, "tile", None), P("src", None, None), P("src", None), P(), P(), P()),
        out_specs=P(None, "tile", "src"),
        check_vma=False,
    )
```

```python
import numpy as np

import jax
import jax.numpy as jnp
from jax import lax
from jax.experimental import pallas as pl
from jax.experimental.pallas import tpu as pltpu
from jax.sharding import PartitionSpec as P

CORE = 192
MARGIN = 32
LENGTH = CORE + 2 * MARGIN
RADIUS = 48
DEPTHS = 8
BAKE_STEPS = 4
SECTORS = 8
TILES = 32
POINTS = 2
ROWS = CORE // SECTORS
HALO_ROWS = ROWS + 2 * BAKE_STEPS
LOW = 88
SPEC_ROWS = 208
LANES = 128
GROUP_SHIFT = 8
GROUP = 8
CHUNK = 128
TOGETHER = 8

acid_rate = 0.24
quench_rate = 0.12
depth_rate = 0.02
react_rate = 0.8

bf16 = jnp.bfloat16
f32 = jnp.float32


def two_parts(table):
    table = table.astype(np.float32)
    high = table.astype(bf16)
    low = (table - high.astype(np.float32)).astype(bf16)
    return high, low


def waves(left, right):
    angle = 2.0 * np.pi / LENGTH * (np.outer(left, right) % LENGTH)
    return np.cos(angle), np.sin(angle)


def forward_rows():
    order = np.concatenate([np.arange(0, CORE, 2), np.arange(1, CORE, 2)])
    real, imag = waves(np.arange(SPEC_ROWS) - LOW, order + MARGIN)
    return two_parts(np.concatenate([real, -imag], 1))


def forward_columns():
    order = np.concatenate(
        [np.arange(CORE) + MARGIN, np.arange(MARGIN), np.arange(MARGIN) + MARGIN + CORE]
    )
    real, imag = waves(order, np.arange(256) - LOW)
    imag = -imag
    return two_parts(np.block([[real, imag], [-imag, real]]))


def inverse_columns():
    bins = np.arange(LANES) - RADIUS
    real, imag = waves(bins, np.arange(CORE) + MARGIN)
    keep = (np.abs(bins) <= RADIUS)[:, None] / LENGTH
    real, imag = real * keep, imag * keep
    top = np.concatenate([real[:, :128], imag[:, :128], real[:, 128:], imag[:, 128:]], 1)
    low = np.concatenate([-imag[:, :128], real[:, :128], -imag[:, 128:], real[:, 128:]], 1)
    return two_parts(np.concatenate([top, low], 0))


def inverse_rows():
    bins = np.arange(LANES) - RADIUS
    rows = np.arange(CORE + 2 * BAKE_STEPS) - BAKE_STEPS + MARGIN
    real, imag = waves(rows, bins)
    keep = (np.abs(bins) <= RADIUS)[None, :] / LENGTH
    return np.concatenate([real * keep, imag * keep], 1).astype(np.float32)


def split(values):
    high = values.astype(bf16)
    low = (values - high.astype(f32)).astype(bf16)
    return high, low


def product(left_high, left_low, right_high, right_low):
    def dot(a, b):
        return jnp.dot(a, b, preferred_element_type=f32)

    return dot(left_high, right_high) + (dot(left_low, right_high) + dot(left_high, right_low))


def lane_iota(shape):
    return lax.broadcasted_iota(jnp.int32, shape, len(shape) - 1)


def edges_kernel(
    near_hbm, shift_hbm, weight_hbm, own_ref, cross_ref, points_ref, near_ref, shift_ref, weight_ref, sems
):
    copies = [
        pltpu.make_async_copy(source, target, sems.at[k])
        for k, (source, target) in enumerate(
            ((near_hbm, near_ref), (shift_hbm, shift_ref), (weight_hbm, weight_ref))
        )
    ]
    for copy in copies:
        copy.start()
    for copy in copies:
        copy.wait()
    half = CORE // 4
    even_tile = lax.axis_index("tile") % 2 == 0
    lane = lane_iota((half, LANES))
    odd = lane >= 64
    second = (lane % 64) >= 32
    for part in range(2):
        def rows(start, offset):
            return near_ref[part, pl.ds(3 * start + offset, half, stride=3), :]

        def right(start):
            return jnp.where(odd, rows(start, 2), rows(start, 1))

        def left(start):
            return jnp.where(odd, rows(start, 1), rows(start, 0))

        right_edge = jnp.where(second, right(0), pltpu.roll(right(half), 96, 1))
        left_edge = jnp.where(second, pltpu.roll(left(half), 32, 1), left(0))
        own_ref[pl.ds(part * half, half), :] = jnp.where(even_tile, right_edge, left_edge)
        cross_ref[pl.ds(part * half, half), :] = jnp.where(even_tile, left_edge, right_edge)

    lane1 = lane_iota((8, LANES))
    values = jnp.zeros((8, LANES), f32)
    for j in range(POINTS):
        for axis in range(2):
            values = jnp.where(lane1 == 2 * j + axis, shift_ref[0, j, axis].astype(f32), values)
    weights = jnp.ones((8, LANES), f32)
    for j in range(POINTS):
        weights = jnp.where(lane1 == 4 + j, weight_ref[0, j], weights)
    values = jnp.where(lane1 < 4, values, jnp.sqrt(weights))
    own_ref[pl.ds(2 * half, 8), :] = values
    cross_ref[pl.ds(2 * half, 8), :] = values
    points_ref[...] = values


def by_depth(ref):
    depth = lax.broadcasted_iota(jnp.int32, (DEPTHS, LANES), 0)
    out = jnp.zeros((DEPTHS, LANES), f32)
    for d in range(DEPTHS):
        out = jnp.where(depth == d, ref[d], out)
    return out


def depth_phase(defocus_ref):
    bins = lane_iota((DEPTHS, LANES)) - RADIUS
    phase = by_depth(defocus_ref) * (bins * bins).astype(f32) / float(RADIUS * RADIUS)
    return jnp.cos(phase), jnp.sin(phase)


def spectrum(near_ref, own_ref, cross_ref, fyh_ref, fyl_ref, fxh_ref, fxl_ref, spec_ref, wh_ref, wl_ref):
    tile = lax.axis_index("tile")
    even_tile = tile % 2 == 0
    has_left = (tile > 0).astype(f32)
    has_right = (tile < TILES - 1).astype(f32)
    half = CORE // 4
    lane = lane_iota((half, LANES))
    low64 = lane < 64
    quarter = lane // 32

    for part in range(2):
        def put(row, col, high, low, negate):
            rows = pl.ds(row, half)
            cols = pl.ds(col, LANES)
            wh_ref[rows, cols] = -high if negate else high
            wl_ref[rows, cols] = -low if negate else low

        for piece in range(2):
            def rows(offset):
                return near_ref[part, pl.ds(3 * piece * half + offset, half, stride=3), :]

            a, b, c = rows(0), rows(1), rows(2)
            bt, ct = pltpu.roll(b, 64, 1), pltpu.roll(c, 64, 1)
            own, cross = own_ref[pl.ds(part * half, half), :], cross_ref[pl.ds(part * half, half), :]
            hl = jnp.where(even_tile, cross, own) * has_left
            hr = jnp.where(even_tile, own, cross) * has_right
            if piece == 0:
                even_tail = jnp.where(low64, b, jnp.where(quarter == 2, pltpu.roll(hl, 32, 1), pltpu.roll(hr, 96, 1)))
                odd_tail = jnp.where(low64, ct, jnp.where(quarter == 2, pltpu.roll(hl, 96, 1), pltpu.roll(hr, 32, 1)))
            else:
                even_tail = jnp.where(low64, b, jnp.where(quarter == 2, pltpu.roll(hl, 64, 1), pltpu.roll(hr, 64, 1)))
                odd_tail = jnp.where(low64, ct, jnp.where(quarter == 2, hl, hr))
            odd_head = jnp.where(low64, bt, ct)
            for base, head, tail in ((0, a, even_tail), (CORE // 2, odd_head, odd_tail)):
                row = base + piece * half
                for col, block in ((0, head), (LANES, tail)):
                    high, low = split(block)
                    if part == 0:
                        put(row, col, high, low, False)
                        put(CORE + row, 256 + col, high, low, False)
                    else:
                        put(row, 256 + col, high, low, False)
                        put(CORE + row, col, high, low, True)

    mixed = product(fyh_ref[...], fyl_ref[...], wh_ref[...], wl_ref[...])
    mixed_high, mixed_low = split(mixed)
    spec = product(mixed_high, mixed_low, fxh_ref[...], fxl_ref[...])
    for k in range(4):
        spec_ref[k] = spec[:, k * LANES:(k + 1) * LANES]


def row_tables(rows_ref, phase_real, phase_imag, left_ref):
    me = lax.axis_index("src")
    table = rows_ref[pl.ds(pl.multiple_of(me * ROWS, 8), HALO_ROWS), :]
    table_real = table[:, None, :LANES]
    table_imag = table[:, None, LANES:]
    left_real = (table_real * phase_real - table_imag * phase_imag).reshape(HALO_ROWS * DEPTHS, LANES)
    left_imag = (table_real * phase_imag + table_imag * phase_real).reshape(HALO_ROWS * DEPTHS, LANES)
    for k, block in ((0, left_real), (1, left_imag)):
        high, low = split(block)
        left_ref[:HALO_ROWS * DEPTHS, k * LANES:(k + 1) * LANES] = high
        left_ref[HALO_ROWS * DEPTHS:, k * LANES:(k + 1) * LANES] = low


def image_points(q_ref, phase_real, phase_imag, spec_ref, left_ref, columns_ref, shifted_ref, mid_ref):
    rowbin = lax.broadcasted_iota(jnp.int32, (LANES, LANES), 0) - RADIUS
    colbin = lane_iota((LANES, LANES)) - RADIUS
    inside = rowbin * rowbin + colbin * colbin <= RADIUS * RADIUS
    lane_full = lane_iota((LANES, LANES))
    rows = HALO_ROWS * DEPTHS
    shape = (HALO_ROWS, DEPTHS, LANES)

    def shift_spectrum(n):
        row, j = n // POINTS, n % POINTS
        start = (LOW - RADIUS) - q_ref[row, 2 * j].astype(jnp.int32)
        shift = (LOW - RADIUS) - q_ref[row, 2 * j + 1].astype(jnp.int32)
        amp = q_ref[row, 4 + j]
        turn = LANES - shift
        for k in range(2):
            first = spec_ref[2 * k, pl.ds(start, LANES), :]
            second = spec_ref[2 * k + 1, pl.ds(start, LANES), :]
            moved = jnp.where(lane_full < turn, pltpu.roll(first, turn, 1), pltpu.roll(second, turn, 1))
            for part, value in enumerate(split(jnp.where(inside, moved * amp, 0.0))):
                shifted_ref[n, part, :LANES, k * LANES:(k + 1) * LANES] = value
                shifted_ref[n, part, LANES:, (1 - k) * LANES:(2 - k) * LANES] = -value if k else value

    def transform_rows(n):
        both = jnp.dot(left_ref[...], shifted_ref[n, 0], preferred_element_type=f32)
        low = jnp.dot(left_ref[:rows, :], shifted_ref[n, 1], preferred_element_type=f32)
        middle = both[:rows] + (both[rows:] + low)
        mid_real = middle[:, :LANES].reshape(shape)
        mid_imag = middle[:, LANES:].reshape(shape)
        out_real = (mid_real * phase_real - mid_imag * phase_imag).reshape(rows, LANES)
        out_imag = (mid_real * phase_imag + mid_imag * phase_real).reshape(rows, LANES)
        for k, value in enumerate((out_real, out_imag)):
            high, low = split(value)
            mid_ref[n, :, k * LANES:(k + 1) * LANES] = high
            mid_ref[n, :, (2 + k) * LANES:(3 + k) * LANES] = low

    points = SECTORS // 2 * POINTS

    def in_groups(size, body):
        if size == points:
            for n in range(points):
                body(n)
        else:
            @pl.loop(0, points // size)
            def _(g):
                for n in range(size):
                    body(g * size + n)

    in_groups(GROUP_SHIFT, shift_spectrum)
    in_groups(GROUP, transform_rows)

    sums = []
    for c in range(rows // CHUNK):
        total = None
        for n in range(0, points, TOGETHER):
            part = mid_ref[n:n + TOGETHER, c * CHUNK:(c + 1) * CHUNK, :].reshape(TOGETHER * CHUNK, 512)
            part = jnp.concatenate([part, part[:, :256]], 1)
            image = jnp.dot(part, columns_ref[...], preferred_element_type=f32)
            power = (image * image).reshape(TOGETHER, CHUNK, 384)
            for k in range(TOGETHER):
                total = power[k] if total is None else total + power[k]
        sums.append(total)
    return sums


def prepare_kernel(
    defocus_ref, dose_ref, load_ref, fyh_hbm, fyl_hbm, fxh_hbm, fxl_hbm, columns_hbm, rows_hbm,
    fyh_ref, fyl_ref, fxh_ref, fxl_ref, columns_ref, left_ref, depth_ref, rows_ref, sems,
):
    pairs = (
        (rows_hbm, rows_ref), (fyh_hbm, fyh_ref), (fyl_hbm, fyl_ref), (fxh_hbm, fxh_ref), (fxl_hbm, fxl_ref),
        (columns_hbm, columns_ref),
    )
    copies = [pltpu.make_async_copy(source, target, sems.at[k]) for k, (source, target) in enumerate(pairs)]
    for copy in copies:
        copy.start()
    phase_real, phase_imag = depth_phase(defocus_ref)
    depth_ref[0], depth_ref[1] = phase_real, phase_imag
    depth_ref[2], depth_ref[3] = by_depth(dose_ref), by_depth(load_ref)
    copies[0].wait()
    row_tables(rows_ref, phase_real, phase_imag, left_ref)
    for copy in copies[1:]:
        copy.wait()


def first_kernel(
    near_ref, own_ref, cross_ref, q_ref, depth_ref, fyh_ref, fyl_ref, fxh_ref, fxl_ref, columns_ref, left_ref,
    spec_ref, sum_ref, wh_ref, wl_ref, shifted_ref, mid_ref,
):
    spectrum(near_ref, own_ref, cross_ref, fyh_ref, fyl_ref, fxh_ref, fxl_ref, spec_ref, wh_ref, wl_ref)
    phases = depth_ref[0], depth_ref[1]
    sums = image_points(q_ref, *phases, spec_ref, left_ref, columns_ref, shifted_ref, mid_ref)
    for c, value in enumerate(sums):
        sum_ref[c * CHUNK:(c + 1) * CHUNK, :] = value


def second_kernel(
    spec_ref, left_ref, sum_ref, columns_ref, depth_ref, q_ref, acid_ref, cross_ref, own_ref, shifted_ref, mid_ref
):
    phases = depth_ref[0], depth_ref[1]
    sums = image_points(q_ref, *phases, spec_ref, left_ref, columns_ref, shifted_ref, mid_ref)
    dose = depth_ref[2]
    shape = (HALO_ROWS, DEPTHS, LANES)
    acc = jnp.concatenate([sum_ref[c * CHUNK:(c + 1) * CHUNK, :] + value for c, value in enumerate(sums)], 0)
    head = (acc[:, :128] + acc[:, 128:256]).reshape(shape)
    tail = acc[:, 256:]
    tail = (tail + pltpu.roll(tail, 64, 1)).reshape(shape)
    acid_head = 1.0 - jnp.exp(-dose * head)
    acid_tail = 1.0 - jnp.exp(-dose * tail)
    acid_ref[:, :, :LANES] = acid_head
    acid_ref[:, :, LANES:] = acid_tail
    lane1 = lane_iota((DEPTHS, LANES))
    left = jnp.zeros((DEPTHS, LANES), f32)
    right = jnp.zeros((DEPTHS, LANES), f32)
    for y in range(HALO_ROWS):
        here = (lane1 >= 4 * y) & (lane1 < 4 * y + 4)
        left = jnp.where(here, pltpu.roll(acid_head[y], 4 * y, 1) if y else acid_head[y], left)
        turn = (4 * y - 60) % LANES
        right = jnp.where(here, pltpu.roll(acid_tail[y], turn, 1) if turn else acid_tail[y], right)
    even_tile = lax.axis_index("tile") % 2 == 0
    own_ref[...] = jnp.where(even_tile, right, left)
    cross_ref[...] = jnp.where(even_tile, left, right)


def bake_kernel(acid_ref, cross_ref, own_ref, depth_ref, out_ref):
    me = lax.axis_index("src")
    tile = lax.axis_index("tile")
    lane1 = lane_iota((DEPTHS, LANES))
    depth = lax.broadcasted_iota(jnp.int32, (DEPTHS, LANES), 0)
    load = depth_ref[3]
    has_left = (tile > 0).astype(f32)
    has_right = (tile < TILES - 1).astype(f32)
    left_cells = lane1 >= 124
    right_cells = (lane1 >= 64) & (lane1 < 68)
    keep_tail = jnp.where(lane1 < 64, 1.0, jnp.where(left_cells, has_left, jnp.where(right_cells, has_right, 0.0)))

    def keep_row(y):
        row = me * ROWS - BAKE_STEPS + y
        return ((row >= 0) & (row < CORE)).astype(f32)

    even_tile = tile % 2 == 0
    own, cross = own_ref[...], cross_ref[...]
    from_left, from_right = jnp.where(even_tile, cross, own), jnp.where(even_tile, own, cross)
    acid, quencher = [], []
    for y in range(HALO_ROWS):
        tail = acid_ref[y, :, LANES:]
        turn_left, turn_right = (124 - 4 * y) % LANES, (64 - 4 * y) % LANES
        moved_left = pltpu.roll(from_left, turn_left, 1) if turn_left else from_left
        moved_right = pltpu.roll(from_right, turn_right, 1) if turn_right else from_right
        tail = jnp.where(lane1 < 64, tail, jnp.where(left_cells, moved_left, moved_right)) * keep_tail
        head = acid_ref[y, :, :LANES]
        pair = [head, tail]
        loads = [load, load * keep_tail]
        if y < BAKE_STEPS or y >= HALO_ROWS - BAKE_STEPS:
            keep = keep_row(y)
            pair = [v * keep for v in pair]
            loads = [v * keep for v in loads]
        acid.append(pair)
        quencher.append(loads)

    first_lane, last_lane = lane1 == 0, lane1 == LANES - 1
    top, bottom = depth == 0, depth == DEPTHS - 1

    def spread(values, y, k, rate):
        here = values[y][k]
        other = values[y][1 - k]
        before = jnp.where(first_lane, pltpu.roll(other, 1, 1), pltpu.roll(here, 1, 1))
        after = jnp.where(last_lane, pltpu.roll(other, LANES - 1, 1), pltpu.roll(here, LANES - 1, 1))
        lateral = values[y + 1][k] + values[y - 1][k] + (before + after)
        above = jnp.where(top, here, pltpu.roll(here, 1, 0))
        below = jnp.where(bottom, here, pltpu.roll(here, DEPTHS - 1, 0))
        spread_value = rate * lateral + depth_rate * (above + below)
        rest = round(1.0 - 4.0 * rate - 2.0 * depth_rate, 12)
        return spread_value + rest * here if rest else spread_value

    for step in range(1, BAKE_STEPS + 1):
        next_acid, next_quencher = list(acid), list(quencher)
        for y in range(step, HALO_ROWS - step):
            pair, loads = [], []
            for k in range(2):
                reaction = react_rate * acid[y][k] * quencher[y][k]
                new_acid = spread(acid, y, k, acid_rate) - reaction
                pair.append(new_acid)
                if step < BAKE_STEPS:
                    loads.append(spread(quencher, y, k, quench_rate) - reaction)
            if step < BAKE_STEPS:
                pair[1] = pair[1] * keep_tail
                loads[1] = loads[1] * keep_tail
                if y < BAKE_STEPS or y >= HALO_ROWS - BAKE_STEPS:
                    keep = keep_row(y)
                    pair = [v * keep for v in pair]
                    loads = [v * keep for v in loads]
            next_acid[y] = pair
            next_quencher[y] = loads
        acid, quencher = next_acid, next_quencher

    low64 = lane1 < 64
    for k in range(ROWS // 2):
        even_head, even_tail = acid[BAKE_STEPS + 2 * k]
        odd_head, odd_tail = (pltpu.roll(v, 64, 1) for v in acid[BAKE_STEPS + 2 * k + 1])
        base = 384 * k
        out_ref[:, 0, base:base + 128] = even_head
        out_ref[:, 0, base + 128:base + 256] = jnp.where(low64, even_tail, odd_head)
        out_ref[:, 0, base + 256:base + 384] = jnp.where(low64, odd_head, odd_tail)


def vmem(n):
    return [pl.BlockSpec(memory_space=pltpu.VMEM)] * n


def hbm(n):
    return [pl.BlockSpec(memory_space=pltpu.HBM)] * n


def in_hbm(values):
    return pltpu.with_memory_space_constraint(values, pltpu.HBM)


def grant(mib):
    return pltpu.CompilerParams(vmem_limit_bytes=mib * 2**20)


def smem(n):
    return [pl.BlockSpec(memory_space=pltpu.SMEM)] * n


def same(tile):
    return tile


def own_chip(tile):
    return tile ^ 1


def across(tile):
    if tile in (0, TILES - 1):
        return tile
    return tile + 1 if tile % 2 else tile - 1


def nearer_half(tile):
    return tile ^ (TILES // 2)


def route(turn, move, flip=0):
    pairs = []
    for s in range(SECTORS):
        upper, y = divmod(s, 4)
        target = (upper ^ flip) * 4 + (y + turn) % 4
        for t in range(TILES):
            source, place = s * TILES + t, target * TILES + move(t)
            pairs.append((source, (s ^ 1) * TILES + t if place == source else place))
    return pairs


def on_device(near_field, source_shift, source_weight, defocus, dose, quencher_load):
    both = ("src", "tile")
    near = near_field.reshape(2, CORE * CORE // LANES, LANES)
    packed = jax.ShapeDtypeStruct((CORE // 2 + 8, LANES), f32)
    edge = jax.ShapeDtypeStruct((DEPTHS, LANES), f32)
    own, cross, points = pl.pallas_call(
        edges_kernel,
        out_shape=(packed, packed, edge),
        in_specs=hbm(3),
        out_specs=tuple(vmem(3)),
        scratch_shapes=[
            pltpu.VMEM(near.shape, f32),
            pltpu.SMEM(source_shift.shape, jnp.int32),
            pltpu.SMEM(source_weight.shape, f32),
            pltpu.SemaphoreType.DMA((3,)),
        ],
        compiler_params=grant(8),
        name="edges",
    )(in_hbm(near), in_hbm(source_shift), in_hbm(source_weight))
    from_own = lax.ppermute(own, both, route(1, own_chip))
    turned = lax.ppermute(points, both, route(2, same))
    from_cross = lax.ppermute(cross, both, route(3, across))
    last = CORE // 2
    half_points = jnp.concatenate(
        [points[:1, :8], turned[:1, :8], from_own[last:last + 1, :8], from_cross[last:last + 1, :8]], 0
    )
    other_points = lax.ppermute(half_points, both, route(0, nearer_half, 1))

    high, low = inverse_columns()
    tables = [*forward_rows(), *forward_columns(), np.concatenate([high, high, low], 0)]
    rows = HALO_ROWS * DEPTHS
    *tables, left, depth = pl.pallas_call(
        prepare_kernel,
        out_shape=(
            *(jax.ShapeDtypeStruct(v.shape, bf16) for v in tables),
            jax.ShapeDtypeStruct((2 * rows, 256), bf16),
            jax.ShapeDtypeStruct((4, DEPTHS, LANES), f32),
        ),
        in_specs=smem(3) + hbm(6),
        out_specs=tuple(vmem(7)),
        scratch_shapes=[pltpu.VMEM((CORE + 2 * BAKE_STEPS, 256), f32), pltpu.SemaphoreType.DMA((6,))],
        compiler_params=grant(4),
        cost_estimate=pl.CostEstimate(flops=1_000_000, bytes_accessed=5_000_000, transcendentals=0),
        name="prepare",
    )(defocus, dose, quencher_load, *(in_hbm(jnp.asarray(v)) for v in (*tables, inverse_rows())))
    columns = tables[-1]
    total = jax.ShapeDtypeStruct((rows, 384), f32)
    shifted = pltpu.VMEM((SECTORS // 2 * POINTS, 2, 256, 256), bf16)
    middle = pltpu.VMEM((SECTORS // 2 * POINTS, rows, 512), bf16)
    window = pltpu.VMEM((2 * CORE, 512), bf16)
    spec, acc = pl.pallas_call(
        first_kernel,
        out_shape=(jax.ShapeDtypeStruct((4, SPEC_ROWS, LANES), f32), total),
        in_specs=vmem(3) + smem(1) + vmem(7),
        out_specs=tuple(vmem(2)),
        scratch_shapes=[window, window, shifted, middle],
        cost_estimate=pl.CostEstimate(flops=8_000_000_000, bytes_accessed=4_000_000, transcendentals=0),
        compiler_params=grant(24),
        name="first",
    )(near, from_own, from_cross, half_points, depth, *tables, left)
    acid, cross, own = pl.pallas_call(
        second_kernel,
        out_shape=(jax.ShapeDtypeStruct((HALO_ROWS, DEPTHS, 256), f32), edge, edge),
        in_specs=vmem(5) + smem(1),
        out_specs=tuple(vmem(3)),
        scratch_shapes=[shifted, middle],
        compiler_params=grant(24),
        name="second",
    )(spec, left, acc, columns, depth, other_points)
    from_cross = lax.ppermute(cross, both, route(0, across))
    from_own = lax.ppermute(own, both, route(0, own_chip))
    return pl.pallas_call(
        bake_kernel,
        out_shape=jax.ShapeDtypeStruct((DEPTHS, 1, ROWS * CORE), f32),
        in_specs=vmem(4),
        out_specs=vmem(1)[0],
        compiler_params=grant(8),
        name="bake",
    )(acid, from_cross, from_own, depth)


def solution(mesh):
    return jax.shard_map(
        on_device,
        mesh=mesh,
        in_specs=(P(None, "tile", None), P("src", None, None), P("src", None), P(), P(), P()),
        out_specs=P(None, "tile", "src"),
        check_vma=False,
    )
```

```python
import numpy as np

import jax
import jax.numpy as jnp
from jax import lax
from jax.experimental import pallas as pl
from jax.experimental.pallas import tpu as pltpu
from jax.sharding import PartitionSpec as P

CORE = 192
MARGIN = 32
LENGTH = CORE + 2 * MARGIN
RADIUS = 48
DEPTHS = 8
BAKE_STEPS = 4
SECTORS = 8
TILES = 32
POINTS = 2
ROWS = CORE // SECTORS
HALO_ROWS = ROWS + 2 * BAKE_STEPS
LOW = 88
SPEC_ROWS = 208
LANES = 128
GROUP_SHIFT = 8
GROUP = 8
CHUNK = 128
TOGETHER = 8

acid_rate = 0.24
quench_rate = 0.12
depth_rate = 0.02
react_rate = 0.8

bf16 = jnp.bfloat16
f32 = jnp.float32


def two_parts(table):
    table = table.astype(np.float32)
    high = table.astype(bf16)
    low = (table - high.astype(np.float32)).astype(bf16)
    return high, low


def waves(left, right):
    angle = 2.0 * np.pi / LENGTH * (np.outer(left, right) % LENGTH)
    return np.cos(angle), np.sin(angle)


def forward_rows():
    order = np.concatenate([np.arange(0, CORE, 2), np.arange(1, CORE, 2)])
    real, imag = waves(np.arange(SPEC_ROWS) - LOW, order + MARGIN)
    return two_parts(np.concatenate([real, -imag], 1))


def forward_columns():
    order = np.concatenate(
        [np.arange(CORE) + MARGIN, np.arange(MARGIN), np.arange(MARGIN) + MARGIN + CORE]
    )
    real, imag = waves(order, np.arange(256) - LOW)
    imag = -imag
    return two_parts(np.block([[real, imag], [-imag, real]]))


def inverse_columns():
    bins = np.arange(LANES) - RADIUS
    real, imag = waves(bins, np.arange(CORE) + MARGIN)
    keep = (np.abs(bins) <= RADIUS)[:, None] / LENGTH
    real, imag = real * keep, imag * keep
    top = np.concatenate([real[:, :128], imag[:, :128], real[:, 128:], imag[:, 128:]], 1)
    low = np.concatenate([-imag[:, :128], real[:, :128], -imag[:, 128:], real[:, 128:]], 1)
    return two_parts(np.concatenate([top, low], 0))


def inverse_rows():
    bins = np.arange(LANES) - RADIUS
    rows = np.arange(CORE + 2 * BAKE_STEPS) - BAKE_STEPS + MARGIN
    real, imag = waves(rows, bins)
    keep = (np.abs(bins) <= RADIUS)[None, :] / LENGTH
    return np.concatenate([real * keep, imag * keep], 1).astype(np.float32)


def split(values):
    high = values.astype(bf16)
    low = (values - high.astype(f32)).astype(bf16)
    return high, low


def product(left_high, left_low, right_high, right_low):
    def dot(a, b):
        return jnp.dot(a, b, preferred_element_type=f32)

    return dot(left_high, right_high) + (dot(left_low, right_high) + dot(left_high, right_low))


def lane_iota(shape):
    return lax.broadcasted_iota(jnp.int32, shape, len(shape) - 1)


def edges_kernel(
    near_hbm, shift_hbm, weight_hbm, cross_ref, own_ref, points_ref, near_ref, shift_ref, weight_ref, sems
):
    copies = [
        pltpu.make_async_copy(source, target, sems.at[k])
        for k, (source, target) in enumerate(
            ((near_hbm, near_ref), (shift_hbm, shift_ref), (weight_hbm, weight_ref))
        )
    ]
    for copy in copies:
        copy.start()
    for copy in copies:
        copy.wait()
    half = CORE // 4
    even_tile = lax.axis_index("tile") % 2 == 0
    lane = lane_iota((half, LANES))
    odd = lane >= 64
    second = (lane % 64) >= 32
    for part in range(2):
        def rows(start, offset):
            return near_ref[part, pl.ds(3 * start + offset, half, stride=3), :]

        def right(start):
            return jnp.where(odd, rows(start, 2), rows(start, 1))

        def left(start):
            return jnp.where(odd, rows(start, 1), rows(start, 0))

        right_edge = jnp.where(second, right(0), pltpu.roll(right(half), 96, 1))
        left_edge = jnp.where(second, pltpu.roll(left(half), 32, 1), left(0))
        own_ref[pl.ds(part * half, half), :] = jnp.where(even_tile, right_edge, left_edge)
        cross_ref[pl.ds(part * half, half), :] = jnp.where(even_tile, left_edge, right_edge)

    lane1 = lane_iota((8, LANES))
    values = jnp.zeros((8, LANES), f32)
    for j in range(POINTS):
        for axis in range(2):
            values = jnp.where(lane1 == 2 * j + axis, shift_ref[0, j, axis].astype(f32), values)
    weights = jnp.ones((8, LANES), f32)
    for j in range(POINTS):
        weights = jnp.where(lane1 == 4 + j, weight_ref[0, j], weights)
    values = jnp.where(lane1 < 4, values, jnp.sqrt(weights))
    own_ref[pl.ds(2 * half, 8), :] = values
    cross_ref[pl.ds(2 * half, 8), :] = values
    points_ref[...] = values


def by_depth(ref):
    depth = lax.broadcasted_iota(jnp.int32, (DEPTHS, LANES), 0)
    out = jnp.zeros((DEPTHS, LANES), f32)
    for d in range(DEPTHS):
        out = jnp.where(depth == d, ref[d], out)
    return out


def depth_phase(defocus_ref):
    bins = lane_iota((DEPTHS, LANES)) - RADIUS
    phase = by_depth(defocus_ref) * (bins * bins).astype(f32) / float(RADIUS * RADIUS)
    return jnp.cos(phase), jnp.sin(phase)


def spectrum(near_ref, own_ref, cross_ref, fyh_ref, fyl_ref, fxh_ref, fxl_ref, spec_ref, wh_ref, wl_ref):
    tile = lax.axis_index("tile")
    even_tile = tile % 2 == 0
    has_left = (tile > 0).astype(f32)
    has_right = (tile < TILES - 1).astype(f32)
    half = CORE // 4
    lane = lane_iota((half, LANES))
    low64 = lane < 64
    quarter = lane // 32

    for part in range(2):
        def put(row, col, high, low, negate):
            rows = pl.ds(row, half)
            cols = pl.ds(col, LANES)
            wh_ref[rows, cols] = -high if negate else high
            wl_ref[rows, cols] = -low if negate else low

        for piece in range(2):
            def rows(offset):
                return near_ref[part, pl.ds(3 * piece * half + offset, half, stride=3), :]

            a, b, c = rows(0), rows(1), rows(2)
            bt, ct = pltpu.roll(b, 64, 1), pltpu.roll(c, 64, 1)
            own, cross = own_ref[pl.ds(part * half, half), :], cross_ref[pl.ds(part * half, half), :]
            hl = jnp.where(even_tile, cross, own) * has_left
            hr = jnp.where(even_tile, own, cross) * has_right
            if piece == 0:
                even_tail = jnp.where(low64, b, jnp.where(quarter == 2, pltpu.roll(hl, 32, 1), pltpu.roll(hr, 96, 1)))
                odd_tail = jnp.where(low64, ct, jnp.where(quarter == 2, pltpu.roll(hl, 96, 1), pltpu.roll(hr, 32, 1)))
            else:
                even_tail = jnp.where(low64, b, jnp.where(quarter == 2, pltpu.roll(hl, 64, 1), pltpu.roll(hr, 64, 1)))
                odd_tail = jnp.where(low64, ct, jnp.where(quarter == 2, hl, hr))
            odd_head = jnp.where(low64, bt, ct)
            for base, head, tail in ((0, a, even_tail), (CORE // 2, odd_head, odd_tail)):
                row = base + piece * half
                for col, block in ((0, head), (LANES, tail)):
                    high, low = split(block)
                    if part == 0:
                        put(row, col, high, low, False)
                        put(CORE + row, 256 + col, high, low, False)
                    else:
                        put(row, 256 + col, high, low, False)
                        put(CORE + row, col, high, low, True)

    mixed = product(fyh_ref[...], fyl_ref[...], wh_ref[...], wl_ref[...])
    mixed_high, mixed_low = split(mixed)
    spec = product(mixed_high, mixed_low, fxh_ref[...], fxl_ref[...])
    for k in range(4):
        spec_ref[k] = spec[:, k * LANES:(k + 1) * LANES]


def row_tables(rows_ref, phase_real, phase_imag, left_ref):
    me = lax.axis_index("src")
    table = rows_ref[pl.ds(pl.multiple_of(me * ROWS, 8), HALO_ROWS), :]
    table_real = table[:, None, :LANES]
    table_imag = table[:, None, LANES:]
    left_real = (table_real * phase_real - table_imag * phase_imag).reshape(HALO_ROWS * DEPTHS, LANES)
    left_imag = (table_real * phase_imag + table_imag * phase_real).reshape(HALO_ROWS * DEPTHS, LANES)
    for k, block in ((0, left_real), (1, left_imag)):
        high, low = split(block)
        left_ref[:HALO_ROWS * DEPTHS, k * LANES:(k + 1) * LANES] = high
        left_ref[HALO_ROWS * DEPTHS:, k * LANES:(k + 1) * LANES] = low


def image_points(q_ref, phase_real, phase_imag, spec_ref, left_ref, columns_ref, shifted_ref, mid_ref):
    rowbin = lax.broadcasted_iota(jnp.int32, (LANES, LANES), 0) - RADIUS
    colbin = lane_iota((LANES, LANES)) - RADIUS
    inside = rowbin * rowbin + colbin * colbin <= RADIUS * RADIUS
    lane_full = lane_iota((LANES, LANES))
    rows = HALO_ROWS * DEPTHS
    shape = (HALO_ROWS, DEPTHS, LANES)

    def shift_spectrum(n):
        row, j = n // POINTS, n % POINTS
        start = (LOW - RADIUS) - q_ref[row, 2 * j].astype(jnp.int32)
        shift = (LOW - RADIUS) - q_ref[row, 2 * j + 1].astype(jnp.int32)
        turn = LANES - shift
        for k in range(2):
            first = spec_ref[2 * k, pl.ds(start, LANES), :]
            second = spec_ref[2 * k + 1, pl.ds(start, LANES), :]
            moved = jnp.where(lane_full < turn, pltpu.roll(first, turn, 1), pltpu.roll(second, turn, 1))
            for part, value in enumerate(split(jnp.where(inside, moved, 0.0))):
                shifted_ref[n, part, :LANES, k * LANES:(k + 1) * LANES] = value
                shifted_ref[n, part, LANES:, (1 - k) * LANES:(2 - k) * LANES] = -value if k else value

    def transform_rows(n):
        amp = q_ref[n // POINTS, 4 + n % POINTS]
        turn_real, turn_imag = phase_real * amp, phase_imag * amp
        both = jnp.dot(left_ref[...], shifted_ref[n, 0], preferred_element_type=f32)
        low = jnp.dot(left_ref[:rows, :], shifted_ref[n, 1], preferred_element_type=f32)
        middle = both[:rows] + (both[rows:] + low)
        mid_real = middle[:, :LANES].reshape(shape)
        mid_imag = middle[:, LANES:].reshape(shape)
        out_real = (mid_real * turn_real - mid_imag * turn_imag).reshape(rows, LANES)
        out_imag = (mid_real * turn_imag + mid_imag * turn_real).reshape(rows, LANES)
        for k, value in enumerate((out_real, out_imag)):
            high, low = split(value)
            mid_ref[n, :, k * LANES:(k + 1) * LANES] = high
            mid_ref[n, :, (2 + k) * LANES:(3 + k) * LANES] = low

    points = SECTORS // 2 * POINTS

    def in_groups(size, body):
        if size == points:
            for n in range(points):
                body(n)
        else:
            @pl.loop(0, points // size)
            def _(g):
                for n in range(size):
                    body(g * size + n)

    in_groups(GROUP_SHIFT, shift_spectrum)
    in_groups(GROUP, transform_rows)

    sums = []
    for c in range(rows // CHUNK):
        total = None
        for n in range(0, points, TOGETHER):
            part = mid_ref[n:n + TOGETHER, c * CHUNK:(c + 1) * CHUNK, :].reshape(TOGETHER * CHUNK, 512)
            part = jnp.concatenate([part, part[:, :256]], 1)
            image = jnp.dot(part, columns_ref[...], preferred_element_type=f32)
            power = (image * image).reshape(TOGETHER, CHUNK, 384)
            for k in range(TOGETHER):
                total = power[k] if total is None else total + power[k]
        sums.append(total)
    return sums


def prepare_kernel(
    defocus_ref, dose_ref, load_ref, fyh_hbm, fyl_hbm, fxh_hbm, fxl_hbm, columns_hbm, rows_hbm,
    fyh_ref, fyl_ref, fxh_ref, fxl_ref, columns_ref, left_ref, depth_ref, rows_ref, sems,
):
    pairs = (
        (rows_hbm, rows_ref), (fyh_hbm, fyh_ref), (fyl_hbm, fyl_ref), (fxh_hbm, fxh_ref), (fxl_hbm, fxl_ref),
        (columns_hbm, columns_ref),
    )
    copies = [pltpu.make_async_copy(source, target, sems.at[k]) for k, (source, target) in enumerate(pairs)]
    for copy in copies:
        copy.start()
    phase_real, phase_imag = depth_phase(defocus_ref)
    depth_ref[0], depth_ref[1] = phase_real, phase_imag
    depth_ref[2], depth_ref[3] = by_depth(dose_ref), by_depth(load_ref)
    copies[0].wait()
    row_tables(rows_ref, phase_real, phase_imag, left_ref)
    for copy in copies[1:]:
        copy.wait()


def first_kernel(
    near_ref, cross_ref, own_ref, q_ref, depth_ref, fyh_ref, fyl_ref, fxh_ref, fxl_ref, columns_ref, left_ref,
    spec_ref, sum_ref, wh_ref, wl_ref, shifted_ref, mid_ref,
):
    spectrum(near_ref, own_ref, cross_ref, fyh_ref, fyl_ref, fxh_ref, fxl_ref, spec_ref, wh_ref, wl_ref)
    phases = depth_ref[0], depth_ref[1]
    sums = image_points(q_ref, *phases, spec_ref, left_ref, columns_ref, shifted_ref, mid_ref)
    for c, value in enumerate(sums):
        sum_ref[c * CHUNK:(c + 1) * CHUNK, :] = value


def second_kernel(
    spec_ref, left_ref, sum_ref, columns_ref, depth_ref, q_ref, acid_ref, cross_ref, own_ref, shifted_ref, mid_ref
):
    phases = depth_ref[0], depth_ref[1]
    sums = image_points(q_ref, *phases, spec_ref, left_ref, columns_ref, shifted_ref, mid_ref)
    dose = depth_ref[2]
    shape = (HALO_ROWS, DEPTHS, LANES)
    acc = jnp.concatenate([sum_ref[c * CHUNK:(c + 1) * CHUNK, :] + value for c, value in enumerate(sums)], 0)
    head = (acc[:, :128] + acc[:, 128:256]).reshape(shape)
    tail = acc[:, 256:]
    tail = (tail + pltpu.roll(tail, 64, 1)).reshape(shape)
    acid_head = 1.0 - jnp.exp(-dose * head)
    acid_tail = 1.0 - jnp.exp(-dose * tail)
    acid_ref[:, :, :LANES] = acid_head
    acid_ref[:, :, LANES:] = acid_tail
    lane1 = lane_iota((DEPTHS, LANES))
    left = jnp.zeros((DEPTHS, LANES), f32)
    right = jnp.zeros((DEPTHS, LANES), f32)
    for y in range(HALO_ROWS):
        here = (lane1 >= 4 * y) & (lane1 < 4 * y + 4)
        left = jnp.where(here, pltpu.roll(acid_head[y], 4 * y, 1) if y else acid_head[y], left)
        turn = (4 * y - 60) % LANES
        right = jnp.where(here, pltpu.roll(acid_tail[y], turn, 1) if turn else acid_tail[y], right)
    even_tile = lax.axis_index("tile") % 2 == 0
    own_ref[...] = jnp.where(even_tile, right, left)
    cross_ref[...] = jnp.where(even_tile, left, right)


def bake_kernel(acid_ref, cross_ref, own_ref, depth_ref, out_ref):
    me = lax.axis_index("src")
    tile = lax.axis_index("tile")
    lane1 = lane_iota((DEPTHS, LANES))
    depth = lax.broadcasted_iota(jnp.int32, (DEPTHS, LANES), 0)
    load = depth_ref[3]
    has_left = (tile > 0).astype(f32)
    has_right = (tile < TILES - 1).astype(f32)
    left_cells = lane1 >= 124
    right_cells = (lane1 >= 64) & (lane1 < 68)
    keep_tail = jnp.where(lane1 < 64, 1.0, jnp.where(left_cells, has_left, jnp.where(right_cells, has_right, 0.0)))

    def keep_row(y):
        row = me * ROWS - BAKE_STEPS + y
        return ((row >= 0) & (row < CORE)).astype(f32)

    even_tile = tile % 2 == 0
    own, cross = own_ref[...], cross_ref[...]
    from_left, from_right = jnp.where(even_tile, cross, own), jnp.where(even_tile, own, cross)
    acid, quencher = [], []
    for y in range(HALO_ROWS):
        tail = acid_ref[y, :, LANES:]
        turn_left, turn_right = (124 - 4 * y) % LANES, (64 - 4 * y) % LANES
        moved_left = pltpu.roll(from_left, turn_left, 1) if turn_left else from_left
        moved_right = pltpu.roll(from_right, turn_right, 1) if turn_right else from_right
        tail = jnp.where(lane1 < 64, tail, jnp.where(left_cells, moved_left, moved_right)) * keep_tail
        head = acid_ref[y, :, :LANES]
        pair = [head, tail]
        loads = [load, load * keep_tail]
        if y < BAKE_STEPS or y >= HALO_ROWS - BAKE_STEPS:
            keep = keep_row(y)
            pair = [v * keep for v in pair]
            loads = [v * keep for v in loads]
        acid.append(pair)
        quencher.append(loads)

    first_lane, last_lane = lane1 == 0, lane1 == LANES - 1
    top, bottom = depth == 0, depth == DEPTHS - 1

    def spread(values, y, k, rate):
        here = values[y][k]
        other = values[y][1 - k]
        before = jnp.where(first_lane, pltpu.roll(other, 1, 1), pltpu.roll(here, 1, 1))
        after = jnp.where(last_lane, pltpu.roll(other, LANES - 1, 1), pltpu.roll(here, LANES - 1, 1))
        lateral = values[y + 1][k] + values[y - 1][k] + (before + after)
        above = jnp.where(top, here, pltpu.roll(here, 1, 0))
        below = jnp.where(bottom, here, pltpu.roll(here, DEPTHS - 1, 0))
        spread_value = rate * lateral + depth_rate * (above + below)
        rest = round(1.0 - 4.0 * rate - 2.0 * depth_rate, 12)
        return spread_value + rest * here if rest else spread_value

    for step in range(1, BAKE_STEPS + 1):
        next_acid, next_quencher = list(acid), list(quencher)
        for y in range(step, HALO_ROWS - step):
            pair, loads = [], []
            for k in range(2):
                reaction = react_rate * acid[y][k] * quencher[y][k]
                new_acid = spread(acid, y, k, acid_rate) - reaction
                pair.append(new_acid)
                if step < BAKE_STEPS:
                    loads.append(spread(quencher, y, k, quench_rate) - reaction)
            if step < BAKE_STEPS:
                pair[1] = pair[1] * keep_tail
                loads[1] = loads[1] * keep_tail
                if y < BAKE_STEPS or y >= HALO_ROWS - BAKE_STEPS:
                    keep = keep_row(y)
                    pair = [v * keep for v in pair]
                    loads = [v * keep for v in loads]
            next_acid[y] = pair
            next_quencher[y] = loads
        acid, quencher = next_acid, next_quencher

    low64 = lane1 < 64
    for k in range(ROWS // 2):
        even_head, even_tail = acid[BAKE_STEPS + 2 * k]
        odd_head, odd_tail = (pltpu.roll(v, 64, 1) for v in acid[BAKE_STEPS + 2 * k + 1])
        base = 384 * k
        out_ref[:, 0, base:base + 128] = even_head
        out_ref[:, 0, base + 128:base + 256] = jnp.where(low64, even_tail, odd_head)
        out_ref[:, 0, base + 256:base + 384] = jnp.where(low64, odd_head, odd_tail)


def vmem(n):
    return [pl.BlockSpec(memory_space=pltpu.VMEM)] * n


def hbm(n):
    return [pl.BlockSpec(memory_space=pltpu.HBM)] * n


def in_hbm(values):
    return pltpu.with_memory_space_constraint(values, pltpu.HBM)


def grant(mib):
    return pltpu.CompilerParams(vmem_limit_bytes=mib * 2**20)


def smem(n):
    return [pl.BlockSpec(memory_space=pltpu.SMEM)] * n


def same(tile):
    return tile


def own_chip(tile):
    return tile ^ 1


def across(tile):
    if tile in (0, TILES - 1):
        return tile
    return tile + 1 if tile % 2 else tile - 1


def nearer_half(tile):
    return tile ^ (TILES // 2)


def route(turn, move, flip=0):
    pairs = []
    for s in range(SECTORS):
        upper, y = divmod(s, 4)
        target = (upper ^ flip) * 4 + (y + turn) % 4
        for t in range(TILES):
            source, place = s * TILES + t, target * TILES + move(t)
            pairs.append((source, (s ^ 1) * TILES + t if place == source else place))
    return pairs


def on_device(near_field, source_shift, source_weight, defocus, dose, quencher_load):
    both = ("src", "tile")
    near = near_field.reshape(2, CORE * CORE // LANES, LANES)
    packed = jax.ShapeDtypeStruct((CORE // 2 + 8, LANES), f32)
    edge = jax.ShapeDtypeStruct((DEPTHS, LANES), f32)
    cross, own, points = pl.pallas_call(
        edges_kernel,
        out_shape=(packed, packed, edge),
        in_specs=hbm(3),
        out_specs=tuple(vmem(3)),
        scratch_shapes=[
            pltpu.VMEM(near.shape, f32),
            pltpu.SMEM(source_shift.shape, jnp.int32),
            pltpu.SMEM(source_weight.shape, f32),
            pltpu.SemaphoreType.DMA((3,)),
        ],
        compiler_params=grant(8),
        name="edges",
    )(in_hbm(near), in_hbm(source_shift), in_hbm(source_weight))
    from_cross = lax.ppermute(cross, both, route(3, across))
    from_own = lax.ppermute(own, both, route(1, own_chip))
    turned = lax.ppermute(points, both, route(2, same))
    last = CORE // 2
    half_points = jnp.concatenate(
        [points[:1, :8], from_cross[last:last + 1, :8], from_own[last:last + 1, :8], turned[:1, :8]], 0
    )
    other_points = lax.ppermute(half_points, both, route(0, nearer_half, 1))

    high, low = inverse_columns()
    tables = [*forward_rows(), *forward_columns(), np.concatenate([high, high, low], 0)]
    rows = HALO_ROWS * DEPTHS
    *tables, left, depth = pl.pallas_call(
        prepare_kernel,
        out_shape=(
            *(jax.ShapeDtypeStruct(v.shape, bf16) for v in tables),
            jax.ShapeDtypeStruct((2 * rows, 256), bf16),
            jax.ShapeDtypeStruct((4, DEPTHS, LANES), f32),
        ),
        in_specs=smem(3) + hbm(6),
        out_specs=tuple(vmem(7)),
        scratch_shapes=[pltpu.VMEM((CORE + 2 * BAKE_STEPS, 256), f32), pltpu.SemaphoreType.DMA((6,))],
        compiler_params=grant(4),
        cost_estimate=pl.CostEstimate(flops=1_000_000, bytes_accessed=5_000_000, transcendentals=0),
        name="prepare",
    )(defocus, dose, quencher_load, *(in_hbm(jnp.asarray(v)) for v in (*tables, inverse_rows())))
    columns = tables[-1]
    total = jax.ShapeDtypeStruct((rows, 384), f32)
    shifted = pltpu.VMEM((SECTORS // 2 * POINTS, 2, 256, 256), bf16)
    middle = pltpu.VMEM((SECTORS // 2 * POINTS, rows, 512), bf16)
    window = pltpu.VMEM((2 * CORE, 512), bf16)
    spec, acc = pl.pallas_call(
        first_kernel,
        out_shape=(jax.ShapeDtypeStruct((4, SPEC_ROWS, LANES), f32), total),
        in_specs=vmem(3) + smem(1) + vmem(7),
        out_specs=tuple(vmem(2)),
        scratch_shapes=[window, window, shifted, middle],
        cost_estimate=pl.CostEstimate(flops=8_000_000_000, bytes_accessed=4_000_000, transcendentals=0),
        compiler_params=grant(24),
        name="first",
    )(near, from_cross, from_own, half_points, depth, *tables, left)
    acid, cross, own = pl.pallas_call(
        second_kernel,
        out_shape=(jax.ShapeDtypeStruct((HALO_ROWS, DEPTHS, 256), f32), edge, edge),
        in_specs=vmem(5) + smem(1),
        out_specs=tuple(vmem(3)),
        scratch_shapes=[shifted, middle],
        compiler_params=grant(24),
        name="second",
    )(spec, left, acc, columns, depth, other_points)
    from_cross = lax.ppermute(cross, both, route(0, across))
    from_own = lax.ppermute(own, both, route(0, own_chip))
    return pl.pallas_call(
        bake_kernel,
        out_shape=jax.ShapeDtypeStruct((DEPTHS, 1, ROWS * CORE), f32),
        in_specs=vmem(4),
        out_specs=vmem(1)[0],
        compiler_params=grant(8),
        name="bake",
    )(acid, from_cross, from_own, depth)


def solution(mesh):
    return jax.shard_map(
        on_device,
        mesh=mesh,
        in_specs=(P(None, "tile", None), P("src", None, None), P("src", None), P(), P(), P()),
        out_specs=P(None, "tile", "src"),
        check_vma=False,
    )
```

```python
import numpy as np

import jax
import jax.numpy as jnp
from jax import lax
from jax.experimental import pallas as pl
from jax.experimental.pallas import tpu as pltpu
from jax.sharding import PartitionSpec as P

CORE = 192
MARGIN = 32
LENGTH = CORE + 2 * MARGIN
RADIUS = 48
SHIFT_MAX = 38
DEPTHS = 8
BAKE_STEPS = 4
SECTORS = 8
TILES = 32
POINTS = 2
ROWS = CORE // SECTORS
HALO_ROWS = ROWS + 2 * BAKE_STEPS
LOW = 88
SPEC_ROWS = 208
LANES = 128
GROUP_SHIFT = 8
GROUP = 8
CHUNK = 128

acid_rate = 0.24
quench_rate = 0.12
depth_rate = 0.02
react_rate = 0.8

bf16 = jnp.bfloat16
f32 = jnp.float32


def two_parts(table):
    table = table.astype(np.float32)
    high = table.astype(bf16)
    low = (table - high.astype(np.float32)).astype(bf16)
    return high, low


def waves(left, right):
    angle = 2.0 * np.pi / LENGTH * (np.outer(left, right) % LENGTH)
    return np.cos(angle), np.sin(angle)


def forward_rows():
    order = np.concatenate([np.arange(0, CORE, 2), np.arange(1, CORE, 2)])
    real, imag = waves(np.arange(SPEC_ROWS) - LOW, order + MARGIN)
    return two_parts(np.concatenate([real, -imag], 1))


def forward_columns():
    order = np.concatenate(
        [np.arange(CORE) + MARGIN, np.arange(MARGIN), np.arange(MARGIN) + MARGIN + CORE]
    )
    bins = np.arange(LANES) - SHIFT_MAX
    real, imag = waves(order, np.concatenate([bins, -bins]))
    imag = -imag
    return two_parts(np.block([[real, imag], [-imag, real]]))


def inverse_columns():
    bins = np.arange(64)
    real, imag = waves(bins, np.arange(256) + MARGIN)
    keep = np.where(bins <= RADIUS, np.where(bins == 0, 0.5, 1.0), 0.0)[:, None] / LENGTH
    keep = keep * (np.arange(256) < CORE)[None, :]
    return two_parts(np.concatenate([real * keep, imag * keep], 0))


def inverse_rows():
    bins = np.arange(LANES) - RADIUS
    rows = np.arange(CORE + 2 * BAKE_STEPS) - BAKE_STEPS + MARGIN
    real, imag = waves(rows, bins)
    keep = (np.abs(bins) <= RADIUS)[None, :] / LENGTH
    return np.concatenate([real * keep, imag * keep], 1).astype(np.float32)


def split(values):
    high = values.astype(bf16)
    low = (values - high.astype(f32)).astype(bf16)
    return high, low


def product(left, right_high, right_low):
    rows = left.shape[0] // 2
    both = jnp.dot(left, right_high, preferred_element_type=f32)
    low = jnp.dot(left[:rows], right_low, preferred_element_type=f32)
    return both[:rows] + (both[rows:] + low)


def lane_iota(shape):
    return lax.broadcasted_iota(jnp.int32, shape, len(shape) - 1)


def edges_kernel(
    near_hbm, shift_hbm, weight_hbm, cross_ref, own_ref, points_ref, near_ref, shift_ref, weight_ref, sems
):
    copies = [
        pltpu.make_async_copy(source, target, sems.at[k])
        for k, (source, target) in enumerate(
            ((near_hbm, near_ref), (shift_hbm, shift_ref), (weight_hbm, weight_ref))
        )
    ]
    for copy in copies:
        copy.start()
    for copy in copies:
        copy.wait()
    half = CORE // 4
    even_tile = lax.axis_index("tile") % 2 == 0
    lane = lane_iota((half, LANES))
    odd = lane >= 64
    second = (lane % 64) >= 32
    for part in range(2):
        def rows(start, offset):
            return near_ref[part, pl.ds(3 * start + offset, half, stride=3), :]

        def right(start):
            return jnp.where(odd, rows(start, 2), rows(start, 1))

        def left(start):
            return jnp.where(odd, rows(start, 1), rows(start, 0))

        right_edge = jnp.where(second, right(0), pltpu.roll(right(half), 96, 1))
        left_edge = jnp.where(second, pltpu.roll(left(half), 32, 1), left(0))
        own_ref[pl.ds(part * half, half), :] = jnp.where(even_tile, right_edge, left_edge)
        cross_ref[pl.ds(part * half, half), :] = jnp.where(even_tile, left_edge, right_edge)

    lane1 = lane_iota((8, LANES))
    values = jnp.zeros((8, LANES), f32)
    for j in range(POINTS):
        for axis in range(2):
            values = jnp.where(lane1 == 2 * j + axis, shift_ref[0, j, axis].astype(f32), values)
    weights = jnp.ones((8, LANES), f32)
    for j in range(POINTS):
        weights = jnp.where(lane1 == 4 + j, weight_ref[0, j], weights)
    values = jnp.where(lane1 < 4, values, jnp.sqrt(weights))
    own_ref[pl.ds(2 * half, 8), :] = values
    cross_ref[pl.ds(2 * half, 8), :] = values
    points_ref[...] = values


def by_depth(ref):
    depth = lax.broadcasted_iota(jnp.int32, (DEPTHS, LANES), 0)
    out = jnp.zeros((DEPTHS, LANES), f32)
    for d in range(DEPTHS):
        out = jnp.where(depth == d, ref[d], out)
    return out


def depth_phase(defocus_ref, bins):
    phase = by_depth(defocus_ref) * (bins * bins).astype(f32) / float(RADIUS * RADIUS)
    return jnp.cos(phase), jnp.sin(phase)


def spectrum(near_ref, own_ref, cross_ref, rows_ref, fxh_ref, fxl_ref, spec_ref, wh_ref, wl_ref):
    tile = lax.axis_index("tile")
    even_tile = tile % 2 == 0
    has_left = (tile > 0).astype(f32)
    has_right = (tile < TILES - 1).astype(f32)
    half = CORE // 4
    lane = lane_iota((half, LANES))
    low64 = lane < 64
    quarter = lane // 32

    for part in range(2):
        def put(row, col, high, low, negate):
            rows = pl.ds(row, half)
            cols = pl.ds(col, LANES)
            wh_ref[rows, cols] = -high if negate else high
            wl_ref[rows, cols] = -low if negate else low

        for piece in range(2):
            def rows(offset):
                return near_ref[part, pl.ds(3 * piece * half + offset, half, stride=3), :]

            a, b, c = rows(0), rows(1), rows(2)
            bt, ct = pltpu.roll(b, 64, 1), pltpu.roll(c, 64, 1)
            own, cross = own_ref[pl.ds(part * half, half), :], cross_ref[pl.ds(part * half, half), :]
            hl = jnp.where(even_tile, cross, own) * has_left
            hr = jnp.where(even_tile, own, cross) * has_right
            if piece == 0:
                even_tail = jnp.where(low64, b, jnp.where(quarter == 2, pltpu.roll(hl, 32, 1), pltpu.roll(hr, 96, 1)))
                odd_tail = jnp.where(low64, ct, jnp.where(quarter == 2, pltpu.roll(hl, 96, 1), pltpu.roll(hr, 32, 1)))
            else:
                even_tail = jnp.where(low64, b, jnp.where(quarter == 2, pltpu.roll(hl, 64, 1), pltpu.roll(hr, 64, 1)))
                odd_tail = jnp.where(low64, ct, jnp.where(quarter == 2, hl, hr))
            odd_head = jnp.where(low64, bt, ct)
            for base, head, tail in ((0, a, even_tail), (CORE // 2, odd_head, odd_tail)):
                row = base + piece * half
                for col, block in ((0, head), (LANES, tail)):
                    high, low = split(block)
                    if part == 0:
                        put(row, col, high, low, False)
                        put(CORE + row, 256 + col, high, low, False)
                    else:
                        put(row, 256 + col, high, low, False)
                        put(CORE + row, col, high, low, True)

    mixed = product(rows_ref[...], wh_ref[...], wl_ref[...])
    spec = product(jnp.concatenate(split(mixed), 0), fxh_ref[...], fxl_ref[...])
    ahead_real, back_real, ahead_imag, back_imag = (spec[:, k * LANES:(k + 1) * LANES] for k in range(4))
    for k, value in enumerate((ahead_real, back_real, ahead_imag, back_imag)):
        spec_ref[k] = value
    for k, value in enumerate((-ahead_imag, back_imag, ahead_real, -back_real)):
        spec_ref[4 + k] = pltpu.roll(value, 64, 1)


def row_tables(rows_ref, phase_real, phase_imag, left_ref):
    me = lax.axis_index("src")
    table = rows_ref[pl.ds(pl.multiple_of(me * ROWS, 8), HALO_ROWS), :]
    table_real = table[:, None, :LANES]
    table_imag = table[:, None, LANES:]
    left_real = (table_real * phase_real - table_imag * phase_imag).reshape(HALO_ROWS * DEPTHS, LANES)
    left_imag = (table_real * phase_imag + table_imag * phase_real).reshape(HALO_ROWS * DEPTHS, LANES)
    for k, block in ((0, left_real), (1, left_imag)):
        high, low = split(block)
        left_ref[:HALO_ROWS * DEPTHS, k * LANES:(k + 1) * LANES] = high
        left_ref[HALO_ROWS * DEPTHS:, k * LANES:(k + 1) * LANES] = low


def image_points(q_ref, phase_real, phase_imag, spec_ref, left_ref, columns_ref, shifted_ref, mid_ref, before_ref, sum_ref):
    rowbin = lax.broadcasted_iota(jnp.int32, (LANES, LANES), 0) - RADIUS
    colbin = lane_iota((LANES, LANES)) % 64
    inside = rowbin * rowbin + colbin * colbin <= RADIUS * RADIUS
    rows = HALO_ROWS * DEPTHS
    shape = (HALO_ROWS, DEPTHS, LANES)

    def shift_spectrum(n):
        row, j = n // POINTS, n % POINTS
        start = (LOW - RADIUS) - q_ref[row, 2 * j].astype(jnp.int32)
        shift = q_ref[row, 2 * j + 1].astype(jnp.int32)

        lane = lane_iota((LANES, LANES))

        def moved(k, first):
            near = ((lane - first) & (LANES - 1)) < 64
            rows_here = pl.ds(start, LANES)
            value = jnp.where(near, spec_ref[k, rows_here, :], spec_ref[4 + k, rows_here, :])
            return pltpu.roll(value, LANES - first, 1)

        ahead, back = SHIFT_MAX - shift, SHIFT_MAX + shift
        folded = [moved(k, ahead) + moved(k + 1, back) for k in (0, 2)]
        for k in range(2):
            for part, value in enumerate(split(jnp.where(inside, folded[k], 0.0))):
                shifted_ref[n, part, :LANES, k * LANES:(k + 1) * LANES] = value
                shifted_ref[n, part, LANES:, (1 - k) * LANES:(2 - k) * LANES] = -value if k else value

    def transform_rows(n):
        amp = q_ref[n // POINTS, 4 + n % POINTS]
        turn_real, turn_imag = phase_real * amp, phase_imag * amp
        both = jnp.dot(left_ref[...], shifted_ref[n, 0], preferred_element_type=f32)
        low = jnp.dot(left_ref[:rows, :], shifted_ref[n, 1], preferred_element_type=f32)
        middle = both[:rows] + (both[rows:] + low)
        mid_real = middle[:, :LANES].reshape(shape)
        mid_imag = middle[:, LANES:].reshape(shape)
        out_real = (mid_real * turn_real - mid_imag * turn_imag).reshape(rows, LANES)
        out_imag = (mid_real * turn_imag + mid_imag * turn_real).reshape(rows, LANES)
        for k, value in enumerate((out_real, out_imag)):
            high, low = split(value)
            mid_ref[k, n, :, :LANES] = high
            mid_ref[k, n, :, LANES:] = low

    points = SECTORS // 2 * POINTS

    def in_groups(size, body):
        if size == points:
            for n in range(points):
                body(n)
        else:
            @pl.loop(0, points // size)
            def _(g):
                for n in range(size):
                    body(g * size + n)

    in_groups(GROUP_SHIFT, shift_spectrum)
    in_groups(GROUP, transform_rows)

    for c in range(rows // CHUNK):
        here = slice(c * CHUNK, (c + 1) * CHUNK)
        total = None if before_ref is None else before_ref[here, :]
        for k in range(2):
            part = mid_ref[k, :, here, :].reshape(points * CHUNK, 256)
            part = jnp.concatenate([part, part[:, :LANES]], 1)
            image = jnp.dot(part, columns_ref[...], preferred_element_type=f32)
            power = (image * image).reshape(points, CHUNK, 256)
            for n in range(points):
                total = power[n] if total is None else total + power[n]
        sum_ref[here, :] = total


def prepare_kernel(
    defocus_ref, dose_ref, load_ref, fy_hbm, fxh_hbm, fxl_hbm, columns_hbm, rows_hbm,
    fy_ref, fxh_ref, fxl_ref, columns_ref, left_ref, depth_ref, rows_ref, sems,
):
    pairs = (
        (rows_hbm, rows_ref), (fy_hbm, fy_ref), (fxh_hbm, fxh_ref), (fxl_hbm, fxl_ref),
        (columns_hbm, columns_ref),
    )
    copies = [pltpu.make_async_copy(source, target, sems.at[k]) for k, (source, target) in enumerate(pairs)]
    for copy in copies:
        copy.start()
    lane = lane_iota((DEPTHS, LANES))
    depth_ref[0], depth_ref[1] = depth_phase(defocus_ref, lane % 64)
    phase_real, phase_imag = depth_phase(defocus_ref, lane - RADIUS)
    depth_ref[2], depth_ref[3] = by_depth(dose_ref), by_depth(load_ref)
    copies[0].wait()
    row_tables(rows_ref, phase_real, phase_imag, left_ref)
    for copy in copies[1:]:
        copy.wait()


def first_kernel(
    near_ref, cross_ref, own_ref, q_ref, depth_ref, fy_ref, fxh_ref, fxl_ref, columns_ref, left_ref,
    spec_ref, sum_ref, wh_ref, wl_ref, shifted_ref, mid_ref,
):
    spectrum(near_ref, own_ref, cross_ref, fy_ref, fxh_ref, fxl_ref, spec_ref, wh_ref, wl_ref)
    phases = depth_ref[0], depth_ref[1]
    image_points(q_ref, *phases, spec_ref, left_ref, columns_ref, shifted_ref, mid_ref, None, sum_ref)


def second_kernel(
    spec_ref, left_ref, sum_ref, columns_ref, depth_ref, q_ref, acid_ref, cross_ref, own_ref, shifted_ref, mid_ref, acc_ref
):
    phases = depth_ref[0], depth_ref[1]
    image_points(q_ref, *phases, spec_ref, left_ref, columns_ref, shifted_ref, mid_ref, sum_ref, acc_ref)
    dose = depth_ref[2]
    shape = (HALO_ROWS, DEPTHS, LANES)
    head = acc_ref[:, :LANES].reshape(shape)
    tail = acc_ref[:, LANES:].reshape(shape)
    acid_head = 1.0 - jnp.exp(-dose * head)
    acid_tail = 1.0 - jnp.exp(-dose * tail)
    acid_ref[:, :, :LANES] = acid_head
    acid_ref[:, :, LANES:] = acid_tail
    lane1 = lane_iota((DEPTHS, LANES))
    left = jnp.zeros((DEPTHS, LANES), f32)
    right = jnp.zeros((DEPTHS, LANES), f32)
    for y in range(HALO_ROWS):
        here = (lane1 >= 4 * y) & (lane1 < 4 * y + 4)
        left = jnp.where(here, pltpu.roll(acid_head[y], 4 * y, 1) if y else acid_head[y], left)
        turn = (4 * y - 60) % LANES
        right = jnp.where(here, pltpu.roll(acid_tail[y], turn, 1) if turn else acid_tail[y], right)
    even_tile = lax.axis_index("tile") % 2 == 0
    own_ref[...] = jnp.where(even_tile, right, left)
    cross_ref[...] = jnp.where(even_tile, left, right)


def bake_kernel(acid_ref, cross_ref, own_ref, depth_ref, out_ref):
    me = lax.axis_index("src")
    tile = lax.axis_index("tile")
    lane1 = lane_iota((DEPTHS, LANES))
    depth = lax.broadcasted_iota(jnp.int32, (DEPTHS, LANES), 0)
    load = depth_ref[3]
    has_left = (tile > 0).astype(f32)
    has_right = (tile < TILES - 1).astype(f32)
    left_cells = lane1 >= 124
    right_cells = (lane1 >= 64) & (lane1 < 68)
    keep_tail = jnp.where(lane1 < 64, 1.0, jnp.where(left_cells, has_left, jnp.where(right_cells, has_right, 0.0)))

    def keep_row(y):
        row = me * ROWS - BAKE_STEPS + y
        return ((row >= 0) & (row < CORE)).astype(f32)

    even_tile = tile % 2 == 0
    own, cross = own_ref[...], cross_ref[...]
    from_left, from_right = jnp.where(even_tile, cross, own), jnp.where(even_tile, own, cross)
    acid, quencher = [], []
    for y in range(HALO_ROWS):
        tail = acid_ref[y, :, LANES:]
        turn_left, turn_right = (124 - 4 * y) % LANES, (64 - 4 * y) % LANES
        moved_left = pltpu.roll(from_left, turn_left, 1) if turn_left else from_left
        moved_right = pltpu.roll(from_right, turn_right, 1) if turn_right else from_right
        tail = jnp.where(lane1 < 64, tail, jnp.where(left_cells, moved_left, moved_right)) * keep_tail
        head = acid_ref[y, :, :LANES]
        pair = [head, tail]
        loads = [load, load * keep_tail]
        if y < BAKE_STEPS or y >= HALO_ROWS - BAKE_STEPS:
            keep = keep_row(y)
            pair = [v * keep for v in pair]
            loads = [v * keep for v in loads]
        acid.append(pair)
        quencher.append(loads)

    first_lane, last_lane = lane1 == 0, lane1 == LANES - 1
    top, bottom = depth == 0, depth == DEPTHS - 1

    def spread(values, y, k, rate):
        here = values[y][k]
        other = values[y][1 - k]
        before = jnp.where(first_lane, pltpu.roll(other, 1, 1), pltpu.roll(here, 1, 1))
        after = jnp.where(last_lane, pltpu.roll(other, LANES - 1, 1), pltpu.roll(here, LANES - 1, 1))
        lateral = values[y + 1][k] + values[y - 1][k] + (before + after)
        above = jnp.where(top, here, pltpu.roll(here, 1, 0))
        below = jnp.where(bottom, here, pltpu.roll(here, DEPTHS - 1, 0))
        spread_value = rate * lateral + depth_rate * (above + below)
        rest = round(1.0 - 4.0 * rate - 2.0 * depth_rate, 12)
        return spread_value + rest * here if rest else spread_value

    for step in range(1, BAKE_STEPS + 1):
        next_acid, next_quencher = list(acid), list(quencher)
        for y in range(step, HALO_ROWS - step):
            pair, loads = [], []
            for k in range(2):
                reaction = react_rate * acid[y][k] * quencher[y][k]
                new_acid = spread(acid, y, k, acid_rate) - reaction
                pair.append(new_acid)
                if step < BAKE_STEPS:
                    loads.append(spread(quencher, y, k, quench_rate) - reaction)
            if step < BAKE_STEPS:
                pair[1] = pair[1] * keep_tail
                loads[1] = loads[1] * keep_tail
                if y < BAKE_STEPS or y >= HALO_ROWS - BAKE_STEPS:
                    keep = keep_row(y)
                    pair = [v * keep for v in pair]
                    loads = [v * keep for v in loads]
            next_acid[y] = pair
            next_quencher[y] = loads
        acid, quencher = next_acid, next_quencher

    low64 = lane1 < 64
    for k in range(ROWS // 2):
        even_head, even_tail = acid[BAKE_STEPS + 2 * k]
        odd_head, odd_tail = (pltpu.roll(v, 64, 1) for v in acid[BAKE_STEPS + 2 * k + 1])
        base = 384 * k
        out_ref[:, 0, base:base + 128] = even_head
        out_ref[:, 0, base + 128:base + 256] = jnp.where(low64, even_tail, odd_head)
        out_ref[:, 0, base + 256:base + 384] = jnp.where(low64, odd_head, odd_tail)


def vmem(n):
    return [pl.BlockSpec(memory_space=pltpu.VMEM)] * n


def hbm(n):
    return [pl.BlockSpec(memory_space=pltpu.HBM)] * n


def in_hbm(values):
    return pltpu.with_memory_space_constraint(values, pltpu.HBM)


def grant(mib):
    return pltpu.CompilerParams(vmem_limit_bytes=mib * 2**20)


def smem(n):
    return [pl.BlockSpec(memory_space=pltpu.SMEM)] * n


def same(tile):
    return tile


def own_chip(tile):
    return tile ^ 1


def across(tile):
    if tile in (0, TILES - 1):
        return tile
    return tile + 1 if tile % 2 else tile - 1


def nearer_half(tile):
    return tile ^ (TILES // 2)


def route(turn, move, flip=0):
    pairs = []
    for s in range(SECTORS):
        upper, y = divmod(s, 4)
        target = (upper ^ flip) * 4 + (y + turn) % 4
        for t in range(TILES):
            source, place = s * TILES + t, target * TILES + move(t)
            pairs.append((source, (s ^ 1) * TILES + t if place == source else place))
    return pairs


def on_device(near_field, source_shift, source_weight, defocus, dose, quencher_load):
    both = ("src", "tile")
    near = near_field.reshape(2, CORE * CORE // LANES, LANES)
    packed = jax.ShapeDtypeStruct((CORE // 2 + 8, LANES), f32)
    edge = jax.ShapeDtypeStruct((DEPTHS, LANES), f32)
    cross, own, points = pl.pallas_call(
        edges_kernel,
        out_shape=(packed, packed, edge),
        in_specs=hbm(3),
        out_specs=tuple(vmem(3)),
        scratch_shapes=[
            pltpu.VMEM(near.shape, f32),
            pltpu.SMEM(source_shift.shape, jnp.int32),
            pltpu.SMEM(source_weight.shape, f32),
            pltpu.SemaphoreType.DMA((3,)),
        ],
        compiler_params=grant(8),
        name="edges",
    )(in_hbm(near), in_hbm(source_shift), in_hbm(source_weight))
    from_cross = lax.ppermute(cross, both, route(3, across))
    from_own = lax.ppermute(own, both, route(1, own_chip))
    turned = lax.ppermute(points, both, route(2, same))
    last = CORE // 2
    half_points = jnp.concatenate(
        [points[:1, :8], from_cross[last:last + 1, :8], from_own[last:last + 1, :8], turned[:1, :8]], 0
    )
    other_points = lax.ppermute(half_points, both, route(0, nearer_half, 1))

    high, low = inverse_columns()
    tables = [np.concatenate(forward_rows(), 0), *forward_columns(), np.concatenate([high, high, low], 0)]
    rows = HALO_ROWS * DEPTHS
    *tables, left, depth = pl.pallas_call(
        prepare_kernel,
        out_shape=(
            *(jax.ShapeDtypeStruct(v.shape, bf16) for v in tables),
            jax.ShapeDtypeStruct((2 * rows, 256), bf16),
            jax.ShapeDtypeStruct((4, DEPTHS, LANES), f32),
        ),
        in_specs=smem(3) + hbm(5),
        out_specs=tuple(vmem(6)),
        scratch_shapes=[pltpu.VMEM((CORE + 2 * BAKE_STEPS, 256), f32), pltpu.SemaphoreType.DMA((5,))],
        compiler_params=grant(4),
        cost_estimate=pl.CostEstimate(flops=1_000_000, bytes_accessed=5_000_000, transcendentals=0),
        name="prepare",
    )(defocus, dose, quencher_load, *(in_hbm(jnp.asarray(v)) for v in (*tables, inverse_rows())))
    columns = tables[-1]
    total = jax.ShapeDtypeStruct((rows, 256), f32)
    shifted = pltpu.VMEM((SECTORS // 2 * POINTS, 2, 256, 256), bf16)
    middle = pltpu.VMEM((2, SECTORS // 2 * POINTS, rows, 256), bf16)
    window = pltpu.VMEM((2 * CORE, 512), bf16)
    spec, acc = pl.pallas_call(
        first_kernel,
        out_shape=(jax.ShapeDtypeStruct((8, SPEC_ROWS, LANES), f32), total),
        in_specs=vmem(3) + smem(1) + vmem(6),
        out_specs=tuple(vmem(2)),
        scratch_shapes=[window, window, shifted, middle],
        cost_estimate=pl.CostEstimate(flops=8_000_000_000, bytes_accessed=4_000_000, transcendentals=0),
        compiler_params=grant(24),
        name="first",
    )(near, from_cross, from_own, half_points, depth, *tables, left)
    acid, cross, own = pl.pallas_call(
        second_kernel,
        out_shape=(jax.ShapeDtypeStruct((HALO_ROWS, DEPTHS, 256), f32), edge, edge),
        in_specs=vmem(5) + smem(1),
        out_specs=tuple(vmem(3)),
        scratch_shapes=[shifted, middle, pltpu.VMEM(total.shape, f32)],
        compiler_params=grant(24),
        name="second",
    )(spec, left, acc, columns, depth, other_points)
    from_cross = lax.ppermute(cross, both, route(0, across))
    from_own = lax.ppermute(own, both, route(0, own_chip))
    return pl.pallas_call(
        bake_kernel,
        out_shape=jax.ShapeDtypeStruct((DEPTHS, 1, ROWS * CORE), f32),
        in_specs=vmem(4),
        out_specs=vmem(1)[0],
        compiler_params=grant(8),
        name="bake",
    )(acid, from_cross, from_own, depth)


def solution(mesh):
    return jax.shard_map(
        on_device,
        mesh=mesh,
        in_specs=(P(None, "tile", None), P("src", None, None), P("src", None), P(), P(), P()),
        out_specs=P(None, "tile", "src"),
        check_vma=False,
    )
```

```python
import numpy as np

import jax
import jax.numpy as jnp
from jax import lax
from jax.experimental import pallas as pl
from jax.experimental.pallas import tpu as pltpu
from jax.sharding import PartitionSpec as P


CORE = 192
MARGIN = 32
LENGTH = CORE + 2 * MARGIN
RADIUS = 48
SHIFT_MAX = 38
DEPTHS = 8
BAKE_STEPS = 4
SECTORS = 8
TILES = 32
POINTS = 2
ROWS = CORE // SECTORS
HALO_ROWS = ROWS + 2 * BAKE_STEPS
LOW = 88
SPEC_ROWS = 208
LANES = 128
GROUP_SHIFT = 8
GROUP = 8
CHUNK = 128

acid_rate = 0.24
quench_rate = 0.12
depth_rate = 0.02
react_rate = 0.8

bf16 = jnp.bfloat16
f32 = jnp.float32


def two_parts(table):
    table = table.astype(np.float32)
    high = table.astype(bf16)
    low = (table - high.astype(np.float32)).astype(bf16)
    return high, low


def waves(left, right):
    angle = 2.0 * np.pi / LENGTH * (np.outer(left, right) % LENGTH)
    return np.cos(angle), np.sin(angle)


def forward_rows():
    order = np.concatenate([np.arange(0, CORE, 2), np.arange(1, CORE, 2)])
    real, imag = waves(np.arange(SPEC_ROWS) - LOW, order + MARGIN)
    return two_parts(np.concatenate([real, -imag], 1))


def forward_columns():
    order = np.concatenate(
        [np.arange(CORE) + MARGIN, np.arange(MARGIN), np.arange(MARGIN) + MARGIN + CORE]
    )
    bins = np.arange(LANES) - SHIFT_MAX
    real, imag = waves(order, np.concatenate([bins, -bins]))
    imag = -imag
    return two_parts(np.block([[real, imag], [-imag, real]]))


def inverse_columns():
    bins = np.arange(64)
    real, imag = waves(bins, np.arange(256) + MARGIN)
    keep = np.where(bins <= RADIUS, np.where(bins == 0, 0.5, 1.0), 0.0)[:, None] / LENGTH
    keep = keep * (np.arange(256) < CORE)[None, :]
    return two_parts(np.concatenate([real * keep, imag * keep], 0))


def inverse_rows():
    bins = np.arange(LANES) - RADIUS
    rows = np.arange(CORE + 2 * BAKE_STEPS) - BAKE_STEPS + MARGIN
    real, imag = waves(rows, bins)
    keep = (np.abs(bins) <= RADIUS)[None, :] / LENGTH
    return np.concatenate([real * keep, imag * keep], 1).astype(np.float32)


def split(values):
    high = values.astype(bf16)
    low = (values - high.astype(f32)).astype(bf16)
    return high, low


def product(left, right_high, right_low):
    rows = left.shape[0] // 2
    both = jnp.dot(left, right_high, preferred_element_type=f32)
    low = jnp.dot(left[:rows], right_low, preferred_element_type=f32)
    return both[:rows] + (both[rows:] + low)


def lane_iota(shape):
    return lax.broadcasted_iota(jnp.int32, shape, len(shape) - 1)


def points_kernel(shift_hbm, weight_hbm, points_ref, shift_ref, weight_ref, sems):
    copies = [
        pltpu.make_async_copy(source, target, sems.at[k])
        for k, (source, target) in enumerate(((shift_hbm, shift_ref), (weight_hbm, weight_ref)))
    ]
    for copy in copies:
        copy.start()
    for copy in copies:
        copy.wait()
    lane1 = lane_iota((8, LANES))
    values = jnp.zeros((8, LANES), f32)
    for j in range(POINTS):
        for axis in range(2):
            values = jnp.where(lane1 == 2 * j + axis, shift_ref[0, j, axis].astype(f32), values)
    weights = jnp.ones((8, LANES), f32)
    for j in range(POINTS):
        weights = jnp.where(lane1 == 4 + j, weight_ref[0, j], weights)
    points_ref[...] = jnp.where(lane1 < 4, values, jnp.sqrt(weights))


def edges_kernel(near_hbm, points_ref, cross_ref, own_ref, near_ref, sem):
    copy = pltpu.make_async_copy(near_hbm, near_ref, sem)
    copy.start()
    copy.wait()
    half = CORE // 4
    even_tile = lax.axis_index("tile") % 2 == 0
    lane = lane_iota((half, LANES))
    odd = lane >= 64
    second = (lane % 64) >= 32
    for part in range(2):
        def rows(start, offset):
            return near_ref[part, pl.ds(3 * start + offset, half, stride=3), :]

        def right(start):
            return jnp.where(odd, rows(start, 2), rows(start, 1))

        def left(start):
            return jnp.where(odd, rows(start, 1), rows(start, 0))

        right_edge = jnp.where(second, right(0), pltpu.roll(right(half), 96, 1))
        left_edge = jnp.where(second, pltpu.roll(left(half), 32, 1), left(0))
        own_ref[pl.ds(part * half, half), :] = jnp.where(even_tile, right_edge, left_edge)
        cross_ref[pl.ds(part * half, half), :] = jnp.where(even_tile, left_edge, right_edge)

    own_ref[pl.ds(2 * half, 8), :] = points_ref[...]
    cross_ref[pl.ds(2 * half, 8), :] = points_ref[...]


def by_depth(ref):
    depth = lax.broadcasted_iota(jnp.int32, (DEPTHS, LANES), 0)
    out = jnp.zeros((DEPTHS, LANES), f32)
    for d in range(DEPTHS):
        out = jnp.where(depth == d, ref[d], out)
    return out


def depth_phase(defocus_ref, bins):
    phase = by_depth(defocus_ref) * (bins * bins).astype(f32) / float(RADIUS * RADIUS)
    return jnp.cos(phase), jnp.sin(phase)


def spectrum(near_ref, own_ref, cross_ref, rows_ref, fxh_ref, fxl_ref, spec_ref, wh_ref, wl_ref):
    tile = lax.axis_index("tile")
    even_tile = tile % 2 == 0
    has_left = (tile > 0).astype(f32)
    has_right = (tile < TILES - 1).astype(f32)
    half = CORE // 4
    lane = lane_iota((half, LANES))
    low64 = lane < 64
    quarter = lane // 32

    for part in range(2):
        def put(row, col, high, low, negate):
            rows = pl.ds(row, half)
            cols = pl.ds(col, LANES)
            wh_ref[rows, cols] = -high if negate else high
            wl_ref[rows, cols] = -low if negate else low

        for piece in range(2):
            def rows(offset):
                return near_ref[part, pl.ds(3 * piece * half + offset, half, stride=3), :]

            a, b, c = rows(0), rows(1), rows(2)
            bt, ct = pltpu.roll(b, 64, 1), pltpu.roll(c, 64, 1)
            own, cross = own_ref[pl.ds(part * half, half), :], cross_ref[pl.ds(part * half, half), :]
            hl = jnp.where(even_tile, cross, own) * has_left
            hr = jnp.where(even_tile, own, cross) * has_right
            if piece == 0:
                even_tail = jnp.where(low64, b, jnp.where(quarter == 2, pltpu.roll(hl, 32, 1), pltpu.roll(hr, 96, 1)))
                odd_tail = jnp.where(low64, ct, jnp.where(quarter == 2, pltpu.roll(hl, 96, 1), pltpu.roll(hr, 32, 1)))
            else:
                even_tail = jnp.where(low64, b, jnp.where(quarter == 2, pltpu.roll(hl, 64, 1), pltpu.roll(hr, 64, 1)))
                odd_tail = jnp.where(low64, ct, jnp.where(quarter == 2, hl, hr))
            odd_head = jnp.where(low64, bt, ct)
            for base, head, tail in ((0, a, even_tail), (CORE // 2, odd_head, odd_tail)):
                row = base + piece * half
                for col, block in ((0, head), (LANES, tail)):
                    high, low = split(block)
                    if part == 0:
                        put(row, col, high, low, False)
                        put(CORE + row, 256 + col, high, low, False)
                    else:
                        put(row, 256 + col, high, low, False)
                        put(CORE + row, col, high, low, True)

    mixed = product(rows_ref[...], wh_ref[...], wl_ref[...])
    spec = product(jnp.concatenate(split(mixed), 0), fxh_ref[...], fxl_ref[...])
    ahead_real, back_real, ahead_imag, back_imag = (spec[:, k * LANES:(k + 1) * LANES] for k in range(4))
    for k, value in enumerate((ahead_real, back_real, ahead_imag, back_imag)):
        spec_ref[k] = value
    for k, value in enumerate((-ahead_imag, back_imag, ahead_real, -back_real)):
        spec_ref[4 + k] = pltpu.roll(value, 64, 1)


def row_tables(rows_ref, phase_real, phase_imag, left_ref):
    me = lax.axis_index("src")
    table = rows_ref[pl.ds(pl.multiple_of(me * ROWS, 8), HALO_ROWS), :]
    table_real = table[:, None, :LANES]
    table_imag = table[:, None, LANES:]
    left_real = (table_real * phase_real - table_imag * phase_imag).reshape(HALO_ROWS * DEPTHS, LANES)
    left_imag = (table_real * phase_imag + table_imag * phase_real).reshape(HALO_ROWS * DEPTHS, LANES)
    for k, block in ((0, left_real), (1, left_imag)):
        high, low = split(block)
        left_ref[:HALO_ROWS * DEPTHS, k * LANES:(k + 1) * LANES] = high
        left_ref[HALO_ROWS * DEPTHS:, k * LANES:(k + 1) * LANES] = low


def image_points(q_ref, phase_real, phase_imag, spec_ref, left_ref, columns_ref, shifted_ref, mid_ref, before_ref, sum_ref):
    rowbin = lax.broadcasted_iota(jnp.int32, (LANES, LANES), 0) - RADIUS
    colbin = lane_iota((LANES, LANES)) % 64
    inside = rowbin * rowbin + colbin * colbin <= RADIUS * RADIUS
    rows = HALO_ROWS * DEPTHS
    shape = (HALO_ROWS, DEPTHS, LANES)

    def shift_spectrum(n):
        row, j = n // POINTS, n % POINTS
        start = (LOW - RADIUS) - q_ref[row, 2 * j].astype(jnp.int32)
        shift = q_ref[row, 2 * j + 1].astype(jnp.int32)

        lane = lane_iota((LANES, LANES))

        def moved(k, first):
            near = ((lane - first) & (LANES - 1)) < 64
            rows_here = pl.ds(start, LANES)
            value = jnp.where(near, spec_ref[k, rows_here, :], spec_ref[4 + k, rows_here, :])
            return pltpu.roll(value, LANES - first, 1)

        ahead, back = SHIFT_MAX - shift, SHIFT_MAX + shift
        folded = [moved(k, ahead) + moved(k + 1, back) for k in (0, 2)]
        for k in range(2):
            for part, value in enumerate(split(jnp.where(inside, folded[k], 0.0))):
                shifted_ref[n, part, :LANES, k * LANES:(k + 1) * LANES] = value
                shifted_ref[n, part, LANES:, (1 - k) * LANES:(2 - k) * LANES] = -value if k else value

    def transform_rows(n):
        amp = q_ref[n // POINTS, 4 + n % POINTS]
        turn_real, turn_imag = phase_real * amp, phase_imag * amp
        both = jnp.dot(left_ref[...], shifted_ref[n, 0], preferred_element_type=f32)
        low = jnp.dot(left_ref[:rows, :], shifted_ref[n, 1], preferred_element_type=f32)
        middle = both[:rows] + (both[rows:] + low)
        mid_real = middle[:, :LANES].reshape(shape)
        mid_imag = middle[:, LANES:].reshape(shape)
        out_real = (mid_real * turn_real - mid_imag * turn_imag).reshape(rows, LANES)
        out_imag = (mid_real * turn_imag + mid_imag * turn_real).reshape(rows, LANES)
        for k, value in enumerate((out_real, out_imag)):
            high, low = split(value)
            mid_ref[k, n, :, :LANES] = high
            mid_ref[k, n, :, LANES:] = low

    points = SECTORS // 2 * POINTS

    def in_groups(size, body):
        if size == points:
            for n in range(points):
                body(n)
        else:
            @pl.loop(0, points // size)
            def _(g):
                for n in range(size):
                    body(g * size + n)

    in_groups(GROUP_SHIFT, shift_spectrum)
    in_groups(GROUP, transform_rows)

    for c in range(rows // CHUNK):
        here = slice(c * CHUNK, (c + 1) * CHUNK)
        total = None if before_ref is None else before_ref[here, :]
        for k in range(2):
            part = mid_ref[k, :, here, :].reshape(points * CHUNK, 256)
            part = jnp.concatenate([part, part[:, :LANES]], 1)
            image = jnp.dot(part, columns_ref[...], preferred_element_type=f32)
            power = (image * image).reshape(points, CHUNK, 256)
            for n in range(points):
                total = power[n] if total is None else total + power[n]
        sum_ref[here, :] = total


def prepare_kernel(
    defocus_ref, dose_ref, load_ref, fy_hbm, fxh_hbm, fxl_hbm, columns_hbm, rows_hbm,
    fy_ref, fxh_ref, fxl_ref, columns_ref, left_ref, depth_ref, rows_ref, sems,
):
    pairs = (
        (rows_hbm, rows_ref), (fy_hbm, fy_ref), (fxh_hbm, fxh_ref), (fxl_hbm, fxl_ref),
        (columns_hbm, columns_ref),
    )
    copies = [pltpu.make_async_copy(source, target, sems.at[k]) for k, (source, target) in enumerate(pairs)]
    for copy in copies:
        copy.start()
    lane = lane_iota((DEPTHS, LANES))
    depth_ref[0], depth_ref[1] = depth_phase(defocus_ref, lane % 64)
    phase_real, phase_imag = depth_phase(defocus_ref, lane - RADIUS)
    depth_ref[2], depth_ref[3] = by_depth(dose_ref), by_depth(load_ref)
    copies[0].wait()
    row_tables(rows_ref, phase_real, phase_imag, left_ref)
    for copy in copies[1:]:
        copy.wait()


def first_kernel(
    near_ref, cross_ref, own_ref, q_ref, depth_ref, fy_ref, fxh_ref, fxl_ref, columns_ref, left_ref,
    spec_ref, sum_ref, wh_ref, wl_ref, shifted_ref, mid_ref,
):
    spectrum(near_ref, own_ref, cross_ref, fy_ref, fxh_ref, fxl_ref, spec_ref, wh_ref, wl_ref)
    phases = depth_ref[0], depth_ref[1]
    image_points(q_ref, *phases, spec_ref, left_ref, columns_ref, shifted_ref, mid_ref, None, sum_ref)


def second_kernel(
    spec_ref, left_ref, sum_ref, columns_ref, depth_ref, q_ref, acid_ref, cross_ref, own_ref, shifted_ref, mid_ref, acc_ref
):
    phases = depth_ref[0], depth_ref[1]
    image_points(q_ref, *phases, spec_ref, left_ref, columns_ref, shifted_ref, mid_ref, sum_ref, acc_ref)
    dose = depth_ref[2]
    shape = (HALO_ROWS, DEPTHS, LANES)
    head = acc_ref[:, :LANES].reshape(shape)
    tail = acc_ref[:, LANES:].reshape(shape)
    acid_head = 1.0 - jnp.exp(-dose * head)
    acid_tail = 1.0 - jnp.exp(-dose * tail)
    acid_ref[:, :, :LANES] = acid_head
    acid_ref[:, :, LANES:] = acid_tail
    lane1 = lane_iota((DEPTHS, LANES))
    left = jnp.zeros((DEPTHS, LANES), f32)
    right = jnp.zeros((DEPTHS, LANES), f32)
    for y in range(HALO_ROWS):
        here = (lane1 >= 4 * y) & (lane1 < 4 * y + 4)
        left = jnp.where(here, pltpu.roll(acid_head[y], 4 * y, 1) if y else acid_head[y], left)
        turn = (4 * y - 60) % LANES
        right = jnp.where(here, pltpu.roll(acid_tail[y], turn, 1) if turn else acid_tail[y], right)
    even_tile = lax.axis_index("tile") % 2 == 0
    own_ref[...] = jnp.where(even_tile, right, left)
    cross_ref[...] = jnp.where(even_tile, left, right)


def bake_kernel(acid_ref, cross_ref, own_ref, depth_ref, out_ref):
    me = lax.axis_index("src")
    tile = lax.axis_index("tile")
    lane1 = lane_iota((DEPTHS, LANES))
    depth = lax.broadcasted_iota(jnp.int32, (DEPTHS, LANES), 0)
    load = depth_ref[3]
    has_left = (tile > 0).astype(f32)
    has_right = (tile < TILES - 1).astype(f32)
    left_cells = lane1 >= 124
    right_cells = (lane1 >= 64) & (lane1 < 68)
    keep_tail = jnp.where(lane1 < 64, 1.0, jnp.where(left_cells, has_left, jnp.where(right_cells, has_right, 0.0)))

    def keep_row(y):
        row = me * ROWS - BAKE_STEPS + y
        return ((row >= 0) & (row < CORE)).astype(f32)

    even_tile = tile % 2 == 0
    own, cross = own_ref[...], cross_ref[...]
    from_left, from_right = jnp.where(even_tile, cross, own), jnp.where(even_tile, own, cross)
    acid, quencher = [], []
    for y in range(HALO_ROWS):
        tail = acid_ref[y, :, LANES:]
        turn_left, turn_right = (124 - 4 * y) % LANES, (64 - 4 * y) % LANES
        moved_left = pltpu.roll(from_left, turn_left, 1) if turn_left else from_left
        moved_right = pltpu.roll(from_right, turn_right, 1) if turn_right else from_right
        tail = jnp.where(lane1 < 64, tail, jnp.where(left_cells, moved_left, moved_right)) * keep_tail
        head = acid_ref[y, :, :LANES]
        pair = [head, tail]
        loads = [load, load * keep_tail]
        if y < BAKE_STEPS or y >= HALO_ROWS - BAKE_STEPS:
            keep = keep_row(y)
            pair = [v * keep for v in pair]
            loads = [v * keep for v in loads]
        acid.append(pair)
        quencher.append(loads)

    first_lane, last_lane = lane1 == 0, lane1 == LANES - 1
    top, bottom = depth == 0, depth == DEPTHS - 1

    def spread(values, y, k, rate):
        here = values[y][k]
        other = values[y][1 - k]
        before = jnp.where(first_lane, pltpu.roll(other, 1, 1), pltpu.roll(here, 1, 1))
        after = jnp.where(last_lane, pltpu.roll(other, LANES - 1, 1), pltpu.roll(here, LANES - 1, 1))
        lateral = values[y + 1][k] + values[y - 1][k] + (before + after)
        above = jnp.where(top, here, pltpu.roll(here, 1, 0))
        below = jnp.where(bottom, here, pltpu.roll(here, DEPTHS - 1, 0))
        spread_value = rate * lateral + depth_rate * (above + below)
        rest = round(1.0 - 4.0 * rate - 2.0 * depth_rate, 12)
        return spread_value + rest * here if rest else spread_value

    for step in range(1, BAKE_STEPS + 1):
        next_acid, next_quencher = list(acid), list(quencher)
        for y in range(step, HALO_ROWS - step):
            pair, loads = [], []
            for k in range(2):
                reaction = react_rate * acid[y][k] * quencher[y][k]
                new_acid = spread(acid, y, k, acid_rate) - reaction
                pair.append(new_acid)
                if step < BAKE_STEPS:
                    loads.append(spread(quencher, y, k, quench_rate) - reaction)
            if step < BAKE_STEPS:
                pair[1] = pair[1] * keep_tail
                loads[1] = loads[1] * keep_tail
                if y < BAKE_STEPS or y >= HALO_ROWS - BAKE_STEPS:
                    keep = keep_row(y)
                    pair = [v * keep for v in pair]
                    loads = [v * keep for v in loads]
            next_acid[y] = pair
            next_quencher[y] = loads
        acid, quencher = next_acid, next_quencher

    low64 = lane1 < 64
    for k in range(ROWS // 2):
        even_head, even_tail = acid[BAKE_STEPS + 2 * k]
        odd_head, odd_tail = (pltpu.roll(v, 64, 1) for v in acid[BAKE_STEPS + 2 * k + 1])
        base = 384 * k
        out_ref[:, 0, base:base + 128] = even_head
        out_ref[:, 0, base + 128:base + 256] = jnp.where(low64, even_tail, odd_head)
        out_ref[:, 0, base + 256:base + 384] = jnp.where(low64, odd_head, odd_tail)


def vmem(n):
    return [pl.BlockSpec(memory_space=pltpu.VMEM)] * n


def hbm(n):
    return [pl.BlockSpec(memory_space=pltpu.HBM)] * n


def in_hbm(values):
    return pltpu.with_memory_space_constraint(values, pltpu.HBM)


def grant(mib):
    return pltpu.CompilerParams(vmem_limit_bytes=mib * 2**20)


def smem(n):
    return [pl.BlockSpec(memory_space=pltpu.SMEM)] * n


def same(tile):
    return tile


def own_chip(tile):
    return tile ^ 1


def across(tile):
    if tile in (0, TILES - 1):
        return tile
    return tile + 1 if tile % 2 else tile - 1


def nearer_half(tile):
    return tile ^ (TILES // 2)


def route(turn, move, flip=0):
    pairs = []
    for s in range(SECTORS):
        upper, y = divmod(s, 4)
        target = (upper ^ flip) * 4 + (y + turn) % 4
        for t in range(TILES):
            source, place = s * TILES + t, target * TILES + move(t)
            pairs.append((source, (s ^ 1) * TILES + t if place == source else place))
    return pairs


def on_device(near_field, source_shift, source_weight, defocus, dose, quencher_load):
    both = ("src", "tile")
    near = near_field.reshape(2, CORE * CORE // LANES, LANES)
    packed = jax.ShapeDtypeStruct((CORE // 2 + 8, LANES), f32)
    edge = jax.ShapeDtypeStruct((DEPTHS, LANES), f32)
    points = pl.pallas_call(
        points_kernel,
        out_shape=edge,
        in_specs=hbm(2),
        out_specs=vmem(1)[0],
        scratch_shapes=[
            pltpu.SMEM(source_shift.shape, jnp.int32),
            pltpu.SMEM(source_weight.shape, f32),
            pltpu.SemaphoreType.DMA((2,)),
        ],
        compiler_params=grant(4),
        name="points",
    )(in_hbm(source_shift), in_hbm(source_weight))
    turned = lax.ppermute(points, both, route(2, same))
    cross, own = pl.pallas_call(
        edges_kernel,
        out_shape=(packed, packed),
        in_specs=hbm(1) + vmem(1),
        out_specs=tuple(vmem(2)),
        scratch_shapes=[pltpu.VMEM(near.shape, f32), pltpu.SemaphoreType.DMA(())],
        compiler_params=grant(4),
        name="edges",
    )(in_hbm(near), points)
    from_cross = lax.ppermute(cross, both, route(3, across))
    from_own = lax.ppermute(own, both, route(1, own_chip))
    last = CORE // 2
    half_points = jnp.concatenate(
        [points[:1, :8], from_cross[last:last + 1, :8], from_own[last:last + 1, :8], turned[:1, :8]], 0
    )
    other_points = lax.ppermute(half_points, both, route(0, nearer_half, 1))

    high, low = inverse_columns()
    tables = [np.concatenate(forward_rows(), 0), *forward_columns(), np.concatenate([high, high, low], 0)]
    rows = HALO_ROWS * DEPTHS
    *tables, left, depth = pl.pallas_call(
        prepare_kernel,
        out_shape=(
            *(jax.ShapeDtypeStruct(v.shape, bf16) for v in tables),
            jax.ShapeDtypeStruct((2 * rows, 256), bf16),
            jax.ShapeDtypeStruct((4, DEPTHS, LANES), f32),
        ),
        in_specs=smem(3) + hbm(5),
        out_specs=tuple(vmem(6)),
        scratch_shapes=[pltpu.VMEM((CORE + 2 * BAKE_STEPS, 256), f32), pltpu.SemaphoreType.DMA((5,))],
        compiler_params=grant(4),
        cost_estimate=pl.CostEstimate(flops=1_000_000, bytes_accessed=5_000_000, transcendentals=0),
        name="prepare",
    )(defocus, dose, quencher_load, *(in_hbm(jnp.asarray(v)) for v in (*tables, inverse_rows())))
    columns = tables[-1]
    total = jax.ShapeDtypeStruct((rows, 256), f32)
    shifted = pltpu.VMEM((SECTORS // 2 * POINTS, 2, 256, 256), bf16)
    middle = pltpu.VMEM((2, SECTORS // 2 * POINTS, rows, 256), bf16)
    window = pltpu.VMEM((2 * CORE, 512), bf16)
    spec, acc = pl.pallas_call(
        first_kernel,
        out_shape=(jax.ShapeDtypeStruct((8, SPEC_ROWS, LANES), f32), total),
        in_specs=vmem(3) + smem(1) + vmem(6),
        out_specs=tuple(vmem(2)),
        scratch_shapes=[window, window, shifted, middle],
        cost_estimate=pl.CostEstimate(flops=8_000_000_000, bytes_accessed=4_000_000, transcendentals=0),
        compiler_params=grant(24),
        name="first",
    )(near, from_cross, from_own, half_points, depth, *tables, left)
    acid, cross, own = pl.pallas_call(
        second_kernel,
        out_shape=(jax.ShapeDtypeStruct((HALO_ROWS, DEPTHS, 256), f32), edge, edge),
        in_specs=vmem(5) + smem(1),
        out_specs=tuple(vmem(3)),
        scratch_shapes=[shifted, middle, pltpu.VMEM(total.shape, f32)],
        compiler_params=grant(24),
        name="second",
    )(spec, left, acc, columns, depth, other_points)
    from_cross = lax.ppermute(cross, both, route(0, across))
    from_own = lax.ppermute(own, both, route(0, own_chip))
    return pl.pallas_call(
        bake_kernel,
        out_shape=jax.ShapeDtypeStruct((DEPTHS, 1, ROWS * CORE), f32),
        in_specs=vmem(4),
        out_specs=vmem(1)[0],
        compiler_params=grant(8),
        name="bake",
    )(acid, from_cross, from_own, depth)


def solution(mesh):
    return jax.shard_map(
        on_device,
        mesh=mesh,
        in_specs=(P(None, "tile", None), P("src", None, None), P("src", None), P(), P(), P()),
        out_specs=P(None, "tile", "src"),
        check_vma=False,
    )
```

```python
import numpy as np

import jax
import jax.numpy as jnp
from jax import lax
from jax.experimental import pallas as pl
from jax.experimental.pallas import tpu as pltpu
from jax.sharding import PartitionSpec as P

CORE = 192
MARGIN = 32
LENGTH = CORE + 2 * MARGIN
RADIUS = 48
SHIFT_MAX = 38
DEPTHS = 8
BAKE_STEPS = 4
SECTORS = 8
TILES = 32
POINTS = 2
ROWS = CORE // SECTORS
HALO_ROWS = ROWS + 2 * BAKE_STEPS
LOW = 88
SPEC_ROWS = 208
LANES = 128
GROUP_SHIFT = 8
GROUP = 8
CHUNK = 128

acid_rate = 0.24
quench_rate = 0.12
depth_rate = 0.02
react_rate = 0.8

bf16 = jnp.bfloat16
f32 = jnp.float32


def two_parts(table):
    table = table.astype(np.float32)
    high = table.astype(bf16)
    low = (table - high.astype(np.float32)).astype(bf16)
    return high, low


def waves(left, right):
    angle = 2.0 * np.pi / LENGTH * (np.outer(left, right) % LENGTH)
    return np.cos(angle), np.sin(angle)


def forward_rows():
    order = np.concatenate([np.arange(0, CORE, 2), np.arange(1, CORE, 2)])
    real, imag = waves(np.arange(SPEC_ROWS) - LOW, order + MARGIN)
    return two_parts(np.concatenate([real, -imag], 1))


def forward_columns():
    order = np.concatenate(
        [np.arange(CORE) + MARGIN, np.arange(MARGIN), np.arange(MARGIN) + MARGIN + CORE]
    )
    bins = np.arange(LANES) - SHIFT_MAX
    real, imag = waves(order, np.concatenate([bins, -bins]))
    imag = -imag
    return two_parts(np.block([[real, imag], [-imag, real]]))


def inverse_columns():
    bins = np.arange(64)
    real, imag = waves(bins, np.arange(256) + MARGIN)
    keep = np.where(bins <= RADIUS, np.where(bins == 0, 0.5, 1.0), 0.0)[:, None] / LENGTH
    keep = keep * (np.arange(256) < CORE)[None, :]
    return two_parts(np.concatenate([real * keep, imag * keep], 0))


def inverse_rows():
    bins = np.arange(LANES) - RADIUS
    rows = np.arange(CORE + 2 * BAKE_STEPS) - BAKE_STEPS + MARGIN
    real, imag = waves(rows, bins)
    keep = (np.abs(bins) <= RADIUS)[None, :] / LENGTH
    return np.concatenate([real * keep, imag * keep], 1).astype(np.float32)


def split(values):
    high = values.astype(bf16)
    low = (values - high.astype(f32)).astype(bf16)
    return high, low


def product(left, right_high, right_low):
    rows = left.shape[0] // 2
    both = jnp.dot(left, right_high, preferred_element_type=f32)
    low = jnp.dot(left[:rows], right_low, preferred_element_type=f32)
    return both[:rows] + (both[rows:] + low)


def lane_iota(shape):
    return lax.broadcasted_iota(jnp.int32, shape, len(shape) - 1)


def edges_kernel(
    near_hbm, shift_hbm, weight_hbm, cross_ref, own_ref, points_ref, near_ref, shift_ref, weight_ref, sems
):
    copies = [
        pltpu.make_async_copy(source, target, sems.at[k])
        for k, (source, target) in enumerate(
            ((near_hbm, near_ref), (shift_hbm, shift_ref), (weight_hbm, weight_ref))
        )
    ]
    for copy in copies:
        copy.start()
    for copy in copies:
        copy.wait()
    half = CORE // 4
    even_tile = lax.axis_index("tile") % 2 == 0
    lane = lane_iota((half, LANES))
    odd = lane >= 64
    second = (lane % 64) >= 32
    for part in range(2):
        def rows(start, offset):
            return near_ref[part, pl.ds(3 * start + offset, half, stride=3), :]

        def right(start):
            return jnp.where(odd, rows(start, 2), rows(start, 1))

        def left(start):
            return jnp.where(odd, rows(start, 1), rows(start, 0))

        right_edge = jnp.where(second, right(0), pltpu.roll(right(half), 96, 1))
        left_edge = jnp.where(second, pltpu.roll(left(half), 32, 1), left(0))
        own_ref[pl.ds(part * half, half), :] = jnp.where(even_tile, right_edge, left_edge)
        cross_ref[pl.ds(part * half, half), :] = jnp.where(even_tile, left_edge, right_edge)

    lane1 = lane_iota((8, LANES))
    values = jnp.zeros((8, LANES), f32)
    for j in range(POINTS):
        for axis in range(2):
            values = jnp.where(lane1 == 2 * j + axis, shift_ref[0, j, axis].astype(f32), values)
    weights = jnp.ones((8, LANES), f32)
    for j in range(POINTS):
        weights = jnp.where(lane1 == 4 + j, weight_ref[0, j], weights)
    values = jnp.where(lane1 < 4, values, jnp.sqrt(weights))
    own_ref[pl.ds(2 * half, 8), :] = values
    cross_ref[pl.ds(2 * half, 8), :] = values
    points_ref[...] = values


def by_depth(ref):
    depth = lax.broadcasted_iota(jnp.int32, (DEPTHS, LANES), 0)
    out = jnp.zeros((DEPTHS, LANES), f32)
    for d in range(DEPTHS):
        out = jnp.where(depth == d, ref[d], out)
    return out


def depth_phase(defocus_ref, bins):
    phase = by_depth(defocus_ref) * (bins * bins).astype(f32) / float(RADIUS * RADIUS)
    return jnp.cos(phase), jnp.sin(phase)


def half_spectrum(near_ref, margins, column_tile, rows_ref, fxh_ref, fxl_ref, wh_ref, wl_ref):
    half = CORE // 4
    lane = lane_iota((half, LANES))
    low64 = lane < 64
    quarter = lane // 32
    for part in range(2):
        for piece in range(2):
            def rows(offset):
                return near_ref[part, pl.ds(3 * piece * half + offset, half, stride=3), :]

            ct = pltpu.roll(rows(2), 64, 1)
            if column_tile == 0:
                blocks = rows(0), jnp.where(low64, pltpu.roll(rows(1), 64, 1), ct)
            else:
                from_left, from_right = margins(part)
                turns = ((32, 96), (96, 32)) if piece == 0 else ((64, 64), (0, 0))
                blocks = []
                for core, (turn_left, turn_right) in zip((rows(1), ct), turns):
                    left = pltpu.roll(from_left, turn_left, 1) if turn_left else from_left
                    right = pltpu.roll(from_right, turn_right, 1) if turn_right else from_right
                    blocks.append(jnp.where(low64, core, jnp.where(quarter == 2, left, right)))
            for base, block in zip((0, CORE // 2), blocks):
                for ref, value in zip((wh_ref, wl_ref), split(block)):
                    upper = pl.ds(base + piece * half, half)
                    lower = pl.ds(CORE + base + piece * half, half)
                    ref[upper, part * LANES:(part + 1) * LANES] = value
                    ref[lower, (1 - part) * LANES:(2 - part) * LANES] = -value if part else value

    def columns(ref):
        first = column_tile * LANES
        return jnp.concatenate([ref[first:first + LANES], ref[256 + first:256 + first + LANES]], 0)

    mixed = product(rows_ref[...], wh_ref[...], wl_ref[...])
    return product(jnp.concatenate(split(mixed), 0), columns(fxh_ref), columns(fxl_ref))


def spectrum(near_ref, own_ref, cross_ref, rows_ref, fxh_ref, fxl_ref, head_ref, spec_ref, wh_ref, wl_ref):
    tile = lax.axis_index("tile")
    even_tile = tile % 2 == 0
    has_left = (tile > 0).astype(f32)
    has_right = (tile < TILES - 1).astype(f32)
    half = CORE // 4

    def margins(part):
        own, cross = own_ref[pl.ds(part * half, half), :], cross_ref[pl.ds(part * half, half), :]
        return jnp.where(even_tile, cross, own) * has_left, jnp.where(even_tile, own, cross) * has_right

    spec = head_ref[...] + half_spectrum(near_ref, margins, 1, rows_ref, fxh_ref, fxl_ref, wh_ref, wl_ref)
    ahead_real, back_real, ahead_imag, back_imag = (spec[:, k * LANES:(k + 1) * LANES] for k in range(4))
    for k, value in enumerate((ahead_real, back_real, ahead_imag, back_imag)):
        spec_ref[k] = value
    for k, value in enumerate((-ahead_imag, back_imag, ahead_real, -back_real)):
        spec_ref[4 + k] = pltpu.roll(value, 64, 1)


def row_tables(rows_ref, phase_real, phase_imag, left_ref):
    me = lax.axis_index("src")
    table = rows_ref[pl.ds(pl.multiple_of(me * ROWS, 8), HALO_ROWS), :]
    table_real = table[:, None, :LANES]
    table_imag = table[:, None, LANES:]
    left_real = (table_real * phase_real - table_imag * phase_imag).reshape(HALO_ROWS * DEPTHS, LANES)
    left_imag = (table_real * phase_imag + table_imag * phase_real).reshape(HALO_ROWS * DEPTHS, LANES)
    for k, block in ((0, left_real), (1, left_imag)):
        high, low = split(block)
        left_ref[:HALO_ROWS * DEPTHS, k * LANES:(k + 1) * LANES] = high
        left_ref[HALO_ROWS * DEPTHS:, k * LANES:(k + 1) * LANES] = low


def image_points(q_ref, phase_real, phase_imag, spec_ref, left_ref, columns_ref, shifted_ref, mid_ref, before_ref, sum_ref):
    rowbin = lax.broadcasted_iota(jnp.int32, (LANES, LANES), 0) - RADIUS
    colbin = lane_iota((LANES, LANES)) % 64
    inside = rowbin * rowbin + colbin * colbin <= RADIUS * RADIUS
    rows = HALO_ROWS * DEPTHS
    shape = (HALO_ROWS, DEPTHS, LANES)

    def shift_spectrum(n):
        row, j = n // POINTS, n % POINTS
        start = (LOW - RADIUS) - q_ref[row, 2 * j].astype(jnp.int32)
        shift = q_ref[row, 2 * j + 1].astype(jnp.int32)

        lane = lane_iota((LANES, LANES))

        def moved(k, first):
            near = ((lane - first) & (LANES - 1)) < 64
            rows_here = pl.ds(start, LANES)
            value = jnp.where(near, spec_ref[k, rows_here, :], spec_ref[4 + k, rows_here, :])
            return pltpu.roll(value, LANES - first, 1)

        ahead, back = SHIFT_MAX - shift, SHIFT_MAX + shift
        folded = [moved(k, ahead) + moved(k + 1, back) for k in (0, 2)]
        for k in range(2):
            for part, value in enumerate(split(jnp.where(inside, folded[k], 0.0))):
                shifted_ref[n, part, :LANES, k * LANES:(k + 1) * LANES] = value
                shifted_ref[n, part, LANES:, (1 - k) * LANES:(2 - k) * LANES] = -value if k else value

    def transform_rows(n):
        amp = q_ref[n // POINTS, 4 + n % POINTS]
        turn_real, turn_imag = phase_real * amp, phase_imag * amp
        both = jnp.dot(left_ref[...], shifted_ref[n, 0], preferred_element_type=f32)
        low = jnp.dot(left_ref[:rows, :], shifted_ref[n, 1], preferred_element_type=f32)
        middle = both[:rows] + (both[rows:] + low)
        mid_real = middle[:, :LANES].reshape(shape)
        mid_imag = middle[:, LANES:].reshape(shape)
        out_real = (mid_real * turn_real - mid_imag * turn_imag).reshape(rows, LANES)
        out_imag = (mid_real * turn_imag + mid_imag * turn_real).reshape(rows, LANES)
        for k, value in enumerate((out_real, out_imag)):
            high, low = split(value)
            mid_ref[k, n, :, :LANES] = high
            mid_ref[k, n, :, LANES:] = low

    points = SECTORS // 2 * POINTS

    def in_groups(size, body):
        if size == points:
            for n in range(points):
                body(n)
        else:
            @pl.loop(0, points // size)
            def _(g):
                for n in range(size):
                    body(g * size + n)

    in_groups(GROUP_SHIFT, shift_spectrum)
    in_groups(GROUP, transform_rows)

    for c in range(rows // CHUNK):
        here = slice(c * CHUNK, (c + 1) * CHUNK)
        total = None if before_ref is None else before_ref[here, :]
        for k in range(2):
            part = mid_ref[k, :, here, :].reshape(points * CHUNK, 256)
            part = jnp.concatenate([part, part[:, :LANES]], 1)
            image = jnp.dot(part, columns_ref[...], preferred_element_type=f32)
            power = (image * image).reshape(points, CHUNK, 256)
            for n in range(points):
                total = power[n] if total is None else total + power[n]
        sum_ref[here, :] = total


def prepare_kernel(
    defocus_ref, dose_ref, load_ref, near_hbm, fy_hbm, fxh_hbm, fxl_hbm, columns_hbm, rows_hbm,
    fy_ref, fxh_ref, fxl_ref, columns_ref, left_ref, depth_ref, head_ref, near_ref, wh_ref, wl_ref, rows_ref, sems,
):
    pairs = (
        (rows_hbm, rows_ref), (near_hbm, near_ref), (fy_hbm, fy_ref), (fxh_hbm, fxh_ref), (fxl_hbm, fxl_ref),
        (columns_hbm, columns_ref),
    )
    copies = [pltpu.make_async_copy(source, target, sems.at[k]) for k, (source, target) in enumerate(pairs)]
    for copy in copies:
        copy.start()
    lane = lane_iota((DEPTHS, LANES))
    depth_ref[0], depth_ref[1] = depth_phase(defocus_ref, lane % 64)
    phase_real, phase_imag = depth_phase(defocus_ref, lane - RADIUS)
    depth_ref[2], depth_ref[3] = by_depth(dose_ref), by_depth(load_ref)
    copies[0].wait()
    row_tables(rows_ref, phase_real, phase_imag, left_ref)
    for copy in copies[1:]:
        copy.wait()
    head_ref[...] = half_spectrum(near_ref, None, 0, fy_ref, fxh_ref, fxl_ref, wh_ref, wl_ref)


def first_kernel(
    near_ref, cross_ref, own_ref, q_ref, depth_ref, fy_ref, fxh_ref, fxl_ref, columns_ref, left_ref, head_ref,
    spec_ref, sum_ref, wh_ref, wl_ref, shifted_ref, mid_ref,
):
    spectrum(near_ref, own_ref, cross_ref, fy_ref, fxh_ref, fxl_ref, head_ref, spec_ref, wh_ref, wl_ref)
    phases = depth_ref[0], depth_ref[1]
    image_points(q_ref, *phases, spec_ref, left_ref, columns_ref, shifted_ref, mid_ref, None, sum_ref)


def second_kernel(
    spec_ref, left_ref, sum_ref, columns_ref, depth_ref, q_ref, acid_ref, cross_ref, own_ref, shifted_ref, mid_ref, acc_ref
):
    phases = depth_ref[0], depth_ref[1]
    image_points(q_ref, *phases, spec_ref, left_ref, columns_ref, shifted_ref, mid_ref, sum_ref, acc_ref)
    dose = depth_ref[2]
    shape = (HALO_ROWS, DEPTHS, LANES)
    head = acc_ref[:, :LANES].reshape(shape)
    tail = acc_ref[:, LANES:].reshape(shape)
    acid_head = 1.0 - jnp.exp(-dose * head)
    acid_tail = 1.0 - jnp.exp(-dose * tail)
    acid_ref[:, :, :LANES] = acid_head
    acid_ref[:, :, LANES:] = acid_tail
    lane1 = lane_iota((DEPTHS, LANES))
    left = jnp.zeros((DEPTHS, LANES), f32)
    right = jnp.zeros((DEPTHS, LANES), f32)
    for y in range(HALO_ROWS):
        here = (lane1 >= 4 * y) & (lane1 < 4 * y + 4)
        left = jnp.where(here, pltpu.roll(acid_head[y], 4 * y, 1) if y else acid_head[y], left)
        turn = (4 * y - 60) % LANES
        right = jnp.where(here, pltpu.roll(acid_tail[y], turn, 1) if turn else acid_tail[y], right)
    even_tile = lax.axis_index("tile") % 2 == 0
    own_ref[...] = jnp.where(even_tile, right, left)
    cross_ref[...] = jnp.where(even_tile, left, right)


def bake_kernel(acid_ref, cross_ref, own_ref, depth_ref, out_ref):
    me = lax.axis_index("src")
    tile = lax.axis_index("tile")
    lane1 = lane_iota((DEPTHS, LANES))
    depth = lax.broadcasted_iota(jnp.int32, (DEPTHS, LANES), 0)
    load = depth_ref[3]
    has_left = (tile > 0).astype(f32)
    has_right = (tile < TILES - 1).astype(f32)
    left_cells = lane1 >= 124
    right_cells = (lane1 >= 64) & (lane1 < 68)
    keep_tail = jnp.where(lane1 < 64, 1.0, jnp.where(left_cells, has_left, jnp.where(right_cells, has_right, 0.0)))

    def keep_row(y):
        row = me * ROWS - BAKE_STEPS + y
        return ((row >= 0) & (row < CORE)).astype(f32)

    even_tile = tile % 2 == 0
    own, cross = own_ref[...], cross_ref[...]
    from_left, from_right = jnp.where(even_tile, cross, own), jnp.where(even_tile, own, cross)
    acid, quencher = [], []
    for y in range(HALO_ROWS):
        tail = acid_ref[y, :, LANES:]
        turn_left, turn_right = (124 - 4 * y) % LANES, (64 - 4 * y) % LANES
        moved_left = pltpu.roll(from_left, turn_left, 1) if turn_left else from_left
        moved_right = pltpu.roll(from_right, turn_right, 1) if turn_right else from_right
        tail = jnp.where(lane1 < 64, tail, jnp.where(left_cells, moved_left, moved_right)) * keep_tail
        head = acid_ref[y, :, :LANES]
        pair = [head, tail]
        loads = [load, load * keep_tail]
        if y < BAKE_STEPS or y >= HALO_ROWS - BAKE_STEPS:
            keep = keep_row(y)
            pair = [v * keep for v in pair]
            loads = [v * keep for v in loads]
        acid.append(pair)
        quencher.append(loads)

    first_lane, last_lane = lane1 == 0, lane1 == LANES - 1
    top, bottom = depth == 0, depth == DEPTHS - 1

    def spread(values, y, k, rate):
        here = values[y][k]
        other = values[y][1 - k]
        before = jnp.where(first_lane, pltpu.roll(other, 1, 1), pltpu.roll(here, 1, 1))
        after = jnp.where(last_lane, pltpu.roll(other, LANES - 1, 1), pltpu.roll(here, LANES - 1, 1))
        lateral = values[y + 1][k] + values[y - 1][k] + (before + after)
        above = jnp.where(top, here, pltpu.roll(here, 1, 0))
        below = jnp.where(bottom, here, pltpu.roll(here, DEPTHS - 1, 0))
        spread_value = rate * lateral + depth_rate * (above + below)
        rest = round(1.0 - 4.0 * rate - 2.0 * depth_rate, 12)
        return spread_value + rest * here if rest else spread_value

    for step in range(1, BAKE_STEPS + 1):
        next_acid, next_quencher = list(acid), list(quencher)
        for y in range(step, HALO_ROWS - step):
            pair, loads = [], []
            for k in range(2):
                reaction = react_rate * acid[y][k] * quencher[y][k]
                new_acid = spread(acid, y, k, acid_rate) - reaction
                pair.append(new_acid)
                if step < BAKE_STEPS:
                    loads.append(spread(quencher, y, k, quench_rate) - reaction)
            if step < BAKE_STEPS:
                pair[1] = pair[1] * keep_tail
                loads[1] = loads[1] * keep_tail
                if y < BAKE_STEPS or y >= HALO_ROWS - BAKE_STEPS:
                    keep = keep_row(y)
                    pair = [v * keep for v in pair]
                    loads = [v * keep for v in loads]
            next_acid[y] = pair
            next_quencher[y] = loads
        acid, quencher = next_acid, next_quencher

    low64 = lane1 < 64
    for k in range(ROWS // 2):
        even_head, even_tail = acid[BAKE_STEPS + 2 * k]
        odd_head, odd_tail = (pltpu.roll(v, 64, 1) for v in acid[BAKE_STEPS + 2 * k + 1])
        base = 384 * k
        out_ref[:, 0, base:base + 128] = even_head
        out_ref[:, 0, base + 128:base + 256] = jnp.where(low64, even_tail, odd_head)
        out_ref[:, 0, base + 256:base + 384] = jnp.where(low64, odd_head, odd_tail)


def vmem(n):
    return [pl.BlockSpec(memory_space=pltpu.VMEM)] * n


def hbm(n):
    return [pl.BlockSpec(memory_space=pltpu.HBM)] * n


def in_hbm(values):
    return pltpu.with_memory_space_constraint(values, pltpu.HBM)


def grant(mib):
    return pltpu.CompilerParams(vmem_limit_bytes=mib * 2**20)


def smem(n):
    return [pl.BlockSpec(memory_space=pltpu.SMEM)] * n


def same(tile):
    return tile


def own_chip(tile):
    return tile ^ 1


def across(tile):
    if tile in (0, TILES - 1):
        return tile
    return tile + 1 if tile % 2 else tile - 1


def nearer_half(tile):
    return tile ^ (TILES // 2)


def route(turn, move, flip=0):
    pairs = []
    for s in range(SECTORS):
        upper, y = divmod(s, 4)
        target = (upper ^ flip) * 4 + (y + turn) % 4
        for t in range(TILES):
            source, place = s * TILES + t, target * TILES + move(t)
            pairs.append((source, (s ^ 1) * TILES + t if place == source else place))
    return pairs


def on_device(near_field, source_shift, source_weight, defocus, dose, quencher_load):
    both = ("src", "tile")
    near = near_field.reshape(2, CORE * CORE // LANES, LANES)
    packed = jax.ShapeDtypeStruct((CORE // 2 + 8, LANES), f32)
    edge = jax.ShapeDtypeStruct((DEPTHS, LANES), f32)
    cross, own, points = pl.pallas_call(
        edges_kernel,
        out_shape=(packed, packed, edge),
        in_specs=hbm(3),
        out_specs=tuple(vmem(3)),
        scratch_shapes=[
            pltpu.VMEM(near.shape, f32),
            pltpu.SMEM(source_shift.shape, jnp.int32),
            pltpu.SMEM(source_weight.shape, f32),
            pltpu.SemaphoreType.DMA((3,)),
        ],
        compiler_params=grant(8),
        name="edges",
    )(in_hbm(near), in_hbm(source_shift), in_hbm(source_weight))
    from_cross = lax.ppermute(cross, both, route(3, across))
    from_own = lax.ppermute(own, both, route(1, own_chip))
    turned = lax.ppermute(points, both, route(2, same))
    last = CORE // 2
    half_points = jnp.concatenate(
        [points[:1, :8], from_cross[last:last + 1, :8], from_own[last:last + 1, :8], turned[:1, :8]], 0
    )
    other_points = lax.ppermute(half_points, both, route(0, nearer_half, 1))

    high, low = inverse_columns()
    tables = [np.concatenate(forward_rows(), 0), *forward_columns(), np.concatenate([high, high, low], 0)]
    rows = HALO_ROWS * DEPTHS
    window = pltpu.VMEM((2 * CORE, 256), bf16)
    *tables, left, depth, head = pl.pallas_call(
        prepare_kernel,
        out_shape=(
            *(jax.ShapeDtypeStruct(v.shape, bf16) for v in tables),
            jax.ShapeDtypeStruct((2 * rows, 256), bf16),
            jax.ShapeDtypeStruct((4, DEPTHS, LANES), f32),
            jax.ShapeDtypeStruct((SPEC_ROWS, 512), f32),
        ),
        in_specs=smem(3) + hbm(6),
        out_specs=tuple(vmem(7)),
        scratch_shapes=[
            pltpu.VMEM(near.shape, f32), window, window,
            pltpu.VMEM((CORE + 2 * BAKE_STEPS, 256), f32), pltpu.SemaphoreType.DMA((6,)),
        ],
        compiler_params=grant(8),
        cost_estimate=pl.CostEstimate(flops=1_000_000, bytes_accessed=5_000_000, transcendentals=0),
        name="prepare",
    )(defocus, dose, quencher_load, in_hbm(near), *(in_hbm(jnp.asarray(v)) for v in (*tables, inverse_rows())))
    columns = tables[-1]
    total = jax.ShapeDtypeStruct((rows, 256), f32)
    shifted = pltpu.VMEM((SECTORS // 2 * POINTS, 2, 256, 256), bf16)
    middle = pltpu.VMEM((2, SECTORS // 2 * POINTS, rows, 256), bf16)
    spec, acc = pl.pallas_call(
        first_kernel,
        out_shape=(jax.ShapeDtypeStruct((8, SPEC_ROWS, LANES), f32), total),
        in_specs=vmem(3) + smem(1) + vmem(7),
        out_specs=tuple(vmem(2)),
        scratch_shapes=[window, window, shifted, middle],
        cost_estimate=pl.CostEstimate(flops=8_000_000_000, bytes_accessed=4_000_000, transcendentals=0),
        compiler_params=grant(24),
        name="first",
    )(near, from_cross, from_own, half_points, depth, *tables, left, head)
    acid, cross, own = pl.pallas_call(
        second_kernel,
        out_shape=(jax.ShapeDtypeStruct((HALO_ROWS, DEPTHS, 256), f32), edge, edge),
        in_specs=vmem(5) + smem(1),
        out_specs=tuple(vmem(3)),
        scratch_shapes=[shifted, middle, pltpu.VMEM(total.shape, f32)],
        compiler_params=grant(24),
        name="second",
    )(spec, left, acc, columns, depth, other_points)
    from_cross = lax.ppermute(cross, both, route(0, across))
    from_own = lax.ppermute(own, both, route(0, own_chip))
    return pl.pallas_call(
        bake_kernel,
        out_shape=jax.ShapeDtypeStruct((DEPTHS, 1, ROWS * CORE), f32),
        in_specs=vmem(4),
        out_specs=vmem(1)[0],
        compiler_params=grant(8),
        name="bake",
    )(acid, from_cross, from_own, depth)


def solution(mesh):
    return jax.shard_map(
        on_device,
        mesh=mesh,
        in_specs=(P(None, "tile", None), P("src", None, None), P("src", None), P(), P(), P()),
        out_specs=P(None, "tile", "src"),
        check_vma=False,
    )
```

```python
import numpy as np

import jax
import jax.numpy as jnp
from jax import lax
from jax.experimental import pallas as pl
from jax.experimental.pallas import tpu as pltpu
from jax.sharding import PartitionSpec as P


CORE = 192
MARGIN = 32
LENGTH = CORE + 2 * MARGIN
RADIUS = 48
SHIFT_MAX = 38
DEPTHS = 8
BAKE_STEPS = 4
SECTORS = 8
TILES = 32
POINTS = 2
ROWS = CORE // SECTORS
HALO_ROWS = ROWS + 2 * BAKE_STEPS
LOW = 88
SPEC_ROWS = 208
LANES = 128
GROUP_SHIFT = 8
GROUP = 8
CHUNK = 128

acid_rate = 0.24
quench_rate = 0.12
depth_rate = 0.02
react_rate = 0.8

bf16 = jnp.bfloat16
f32 = jnp.float32


def two_parts(table):
    table = table.astype(np.float32)
    high = table.astype(bf16)
    low = (table - high.astype(np.float32)).astype(bf16)
    return high, low


def waves(left, right):
    angle = 2.0 * np.pi / LENGTH * (np.outer(left, right) % LENGTH)
    return np.cos(angle), np.sin(angle)


def forward_rows():
    order = np.concatenate([np.arange(0, CORE, 2), np.arange(1, CORE, 2)])
    real, imag = waves(np.arange(SPEC_ROWS) - LOW, order + MARGIN)
    return two_parts(np.concatenate([real, -imag], 1))


def forward_columns():
    order = np.concatenate(
        [np.arange(CORE) + MARGIN, np.arange(MARGIN), np.arange(MARGIN) + MARGIN + CORE]
    )
    bins = np.arange(LANES) - SHIFT_MAX
    real, imag = waves(order, np.concatenate([bins, -bins]))
    imag = -imag
    return two_parts(np.block([[real, imag], [-imag, real]]))


def inverse_columns():
    bins = np.arange(64)
    real, imag = waves(bins, np.arange(256) + MARGIN)
    keep = np.where(bins <= RADIUS, np.where(bins == 0, 0.5, 1.0), 0.0)[:, None] / LENGTH
    keep = keep * (np.arange(256) < CORE)[None, :]
    return two_parts(np.concatenate([real * keep, imag * keep], 0))


def inverse_rows():
    bins = np.arange(LANES) - RADIUS
    rows = np.arange(CORE + 2 * BAKE_STEPS) - BAKE_STEPS + MARGIN
    real, imag = waves(rows, bins)
    keep = (np.abs(bins) <= RADIUS)[None, :] / LENGTH
    return np.concatenate([real * keep, imag * keep], 1).astype(np.float32)


def split(values):
    high = values.astype(bf16)
    low = (values - high.astype(f32)).astype(bf16)
    return high, low


def product(left, right_high, right_low):
    rows = left.shape[0] // 2
    both = jnp.dot(left, right_high, preferred_element_type=f32)
    low = jnp.dot(left[:rows], right_low, preferred_element_type=f32)
    return both[:rows] + (both[rows:] + low)


def lane_iota(shape):
    return lax.broadcasted_iota(jnp.int32, shape, len(shape) - 1)


def edges_kernel(
    near_hbm, shift_hbm, weight_hbm, cross_ref, own_ref, points_ref, near_ref, shift_ref, weight_ref, sems
):
    copies = [
        pltpu.make_async_copy(source, target, sems.at[k])
        for k, (source, target) in enumerate(
            ((near_hbm, near_ref), (shift_hbm, shift_ref), (weight_hbm, weight_ref))
        )
    ]
    for copy in copies:
        copy.start()
    for copy in copies:
        copy.wait()
    half = CORE // 4
    even_tile = lax.axis_index("tile") % 2 == 0
    lane = lane_iota((half, LANES))
    odd = lane >= 64
    second = (lane % 64) >= 32
    for part in range(2):
        def rows(start, offset):
            return near_ref[part, pl.ds(3 * start + offset, half, stride=3), :]

        def right(start):
            return jnp.where(odd, rows(start, 2), rows(start, 1))

        def left(start):
            return jnp.where(odd, rows(start, 1), rows(start, 0))

        right_edge = jnp.where(second, right(0), pltpu.roll(right(half), 96, 1))
        left_edge = jnp.where(second, pltpu.roll(left(half), 32, 1), left(0))
        own_ref[pl.ds(part * half, half), :] = jnp.where(even_tile, right_edge, left_edge)
        cross_ref[pl.ds(part * half, half), :] = jnp.where(even_tile, left_edge, right_edge)

    lane1 = lane_iota((8, LANES))
    values = jnp.zeros((8, LANES), f32)
    for j in range(POINTS):
        for axis in range(2):
            values = jnp.where(lane1 == 2 * j + axis, shift_ref[0, j, axis].astype(f32), values)
    weights = jnp.ones((8, LANES), f32)
    for j in range(POINTS):
        weights = jnp.where(lane1 == 4 + j, weight_ref[0, j], weights)
    values = jnp.where(lane1 < 4, values, jnp.sqrt(weights))
    own_ref[pl.ds(2 * half, 8), :] = values
    cross_ref[pl.ds(2 * half, 8), :] = values
    points_ref[...] = values


def by_depth(ref):
    depth = lax.broadcasted_iota(jnp.int32, (DEPTHS, LANES), 0)
    out = jnp.zeros((DEPTHS, LANES), f32)
    for d in range(DEPTHS):
        out = jnp.where(depth == d, ref[d], out)
    return out


def depth_phase(defocus_ref, bins):
    phase = by_depth(defocus_ref) * (bins * bins).astype(f32) / float(RADIUS * RADIUS)
    return jnp.cos(phase), jnp.sin(phase)


def half_spectrum(near_ref, margins, column_tile, rows_ref, fxh_ref, fxl_ref, wh_ref, wl_ref):
    half = CORE // 4
    lane = lane_iota((half, LANES))
    low64 = lane < 64
    quarter = lane // 32
    for part in range(2):
        for piece in range(2):
            def rows(offset):
                return near_ref[part, pl.ds(3 * piece * half + offset, half, stride=3), :]

            ct = pltpu.roll(rows(2), 64, 1)
            if column_tile == 0:
                blocks = rows(0), jnp.where(low64, pltpu.roll(rows(1), 64, 1), ct)
            else:
                from_left, from_right = margins(part)
                turns = ((32, 96), (96, 32)) if piece == 0 else ((64, 64), (0, 0))
                blocks = []
                for core, (turn_left, turn_right) in zip((rows(1), ct), turns):
                    left = pltpu.roll(from_left, turn_left, 1) if turn_left else from_left
                    right = pltpu.roll(from_right, turn_right, 1) if turn_right else from_right
                    blocks.append(jnp.where(low64, core, jnp.where(quarter == 2, left, right)))
            for base, block in zip((0, CORE // 2), blocks):
                for ref, value in zip((wh_ref, wl_ref), split(block)):
                    upper = pl.ds(base + piece * half, half)
                    lower = pl.ds(CORE + base + piece * half, half)
                    ref[upper, part * LANES:(part + 1) * LANES] = value
                    ref[lower, (1 - part) * LANES:(2 - part) * LANES] = -value if part else value

    def columns(ref):
        first = column_tile * LANES
        return jnp.concatenate([ref[first:first + LANES], ref[256 + first:256 + first + LANES]], 0)

    mixed = product(rows_ref[...], wh_ref[...], wl_ref[...])
    return product(jnp.concatenate(split(mixed), 0), columns(fxh_ref), columns(fxl_ref))


def spectrum(near_ref, own_ref, cross_ref, rows_ref, fxh_ref, fxl_ref, head_ref, spec_ref, wh_ref, wl_ref):
    tile = lax.axis_index("tile")
    even_tile = tile % 2 == 0
    has_left = (tile > 0).astype(f32)
    has_right = (tile < TILES - 1).astype(f32)
    half = CORE // 4

    def margins(part):
        own, cross = own_ref[pl.ds(part * half, half), :], cross_ref[pl.ds(part * half, half), :]
        return jnp.where(even_tile, cross, own) * has_left, jnp.where(even_tile, own, cross) * has_right

    spec = head_ref[...] + half_spectrum(near_ref, margins, 1, rows_ref, fxh_ref, fxl_ref, wh_ref, wl_ref)
    ahead_real, back_real, ahead_imag, back_imag = (spec[:, k * LANES:(k + 1) * LANES] for k in range(4))
    for k, value in enumerate((ahead_real, back_real, ahead_imag, back_imag)):
        spec_ref[k] = value
    for k, value in enumerate((-ahead_imag, back_imag, ahead_real, -back_real)):
        spec_ref[4 + k] = pltpu.roll(value, 64, 1)


def row_tables(rows_ref, phase_real, phase_imag, left_ref):
    me = lax.axis_index("src")
    table = rows_ref[pl.ds(pl.multiple_of(me * ROWS, 8), HALO_ROWS), :]
    table_real = table[:, None, :LANES]
    table_imag = table[:, None, LANES:]
    left_real = (table_real * phase_real - table_imag * phase_imag).reshape(HALO_ROWS * DEPTHS, LANES)
    left_imag = (table_real * phase_imag + table_imag * phase_real).reshape(HALO_ROWS * DEPTHS, LANES)
    for k, block in ((0, left_real), (1, left_imag)):
        high, low = split(block)
        left_ref[:HALO_ROWS * DEPTHS, k * LANES:(k + 1) * LANES] = high
        left_ref[HALO_ROWS * DEPTHS:, k * LANES:(k + 1) * LANES] = low


def image_points(q_ref, phase_real, phase_imag, spec_ref, left_ref, columns_ref, shifted_ref, mid_ref, before_ref, sum_ref):
    rowbin = lax.broadcasted_iota(jnp.int32, (LANES, LANES), 0) - RADIUS
    colbin = lane_iota((LANES, LANES)) % 64
    inside = rowbin * rowbin + colbin * colbin <= RADIUS * RADIUS
    rows = HALO_ROWS * DEPTHS
    shape = (HALO_ROWS, DEPTHS, LANES)

    def shift_spectrum(n):
        row, j = n // POINTS, n % POINTS
        start = (LOW - RADIUS) - q_ref[row, 2 * j].astype(jnp.int32)
        shift = q_ref[row, 2 * j + 1].astype(jnp.int32)

        lane = lane_iota((LANES, LANES))

        def moved(k, first):
            near = ((lane - first) & (LANES - 1)) < 64
            rows_here = pl.ds(start, LANES)
            value = jnp.where(near, spec_ref[k, rows_here, :], spec_ref[4 + k, rows_here, :])
            return pltpu.roll(value, LANES - first, 1)

        ahead, back = SHIFT_MAX - shift, SHIFT_MAX + shift
        folded = [moved(k, ahead) + moved(k + 1, back) for k in (0, 2)]
        for k in range(2):
            for part, value in enumerate(split(jnp.where(inside, folded[k], 0.0))):
                shifted_ref[n, part, :LANES, k * LANES:(k + 1) * LANES] = value
                shifted_ref[n, part, LANES:, (1 - k) * LANES:(2 - k) * LANES] = -value if k else value

    def transform_rows(n):
        amp = q_ref[n // POINTS, 4 + n % POINTS]
        turn_real, turn_imag = phase_real * amp, phase_imag * amp
        both = jnp.dot(left_ref[...], shifted_ref[n, 0], preferred_element_type=f32)
        low = jnp.dot(left_ref[:rows, :], shifted_ref[n, 1], preferred_element_type=f32)
        middle = both[:rows] + (both[rows:] + low)
        mid_real = middle[:, :LANES].reshape(shape)
        mid_imag = middle[:, LANES:].reshape(shape)
        out_real = (mid_real * turn_real - mid_imag * turn_imag).reshape(rows, LANES)
        out_imag = (mid_real * turn_imag + mid_imag * turn_real).reshape(rows, LANES)
        for k, value in enumerate((out_real, out_imag)):
            high, low = split(value)
            mid_ref[k, n, :, :LANES] = high
            mid_ref[k, n, :, LANES:] = low

    points = SECTORS // 2 * POINTS

    def in_groups(size, body):
        if size == points:
            for n in range(points):
                body(n)
        else:
            @pl.loop(0, points // size)
            def _(g):
                for n in range(size):
                    body(g * size + n)

    in_groups(GROUP_SHIFT, shift_spectrum)
    in_groups(GROUP, transform_rows)

    for c in range(rows // CHUNK):
        here = slice(c * CHUNK, (c + 1) * CHUNK)
        total = None if before_ref is None else before_ref[here, :]
        for k in range(2):
            part = mid_ref[k, :, here, :].reshape(points * CHUNK, 256)
            part = jnp.concatenate([part, part[:, :LANES]], 1)
            image = jnp.dot(part, columns_ref[...], preferred_element_type=f32)
            power = (image * image).reshape(points, CHUNK, 256)
            for n in range(points):
                total = power[n] if total is None else total + power[n]
        sum_ref[here, :] = total


def prepare_kernel(
    defocus_ref, dose_ref, load_ref, near_hbm, fy_hbm, fxh_hbm, fxl_hbm, columns_hbm, rows_hbm,
    fy_ref, fxh_ref, fxl_ref, columns_ref, left_ref, depth_ref, head_ref, near_ref, wh_ref, wl_ref, rows_ref, sems,
):
    pairs = (
        (rows_hbm, rows_ref), (near_hbm, near_ref), (fy_hbm, fy_ref), (fxh_hbm, fxh_ref), (fxl_hbm, fxl_ref),
        (columns_hbm, columns_ref),
    )
    copies = [pltpu.make_async_copy(source, target, sems.at[k]) for k, (source, target) in enumerate(pairs)]
    for copy in copies:
        copy.start()
    lane = lane_iota((DEPTHS, LANES))
    depth_ref[0], depth_ref[1] = depth_phase(defocus_ref, lane % 64)
    phase_real, phase_imag = depth_phase(defocus_ref, lane - RADIUS)
    depth_ref[2], depth_ref[3] = by_depth(dose_ref), by_depth(load_ref)
    copies[0].wait()
    row_tables(rows_ref, phase_real, phase_imag, left_ref)
    for copy in copies[1:]:
        copy.wait()
    head_ref[...] = half_spectrum(near_ref, None, 0, fy_ref, fxh_ref, fxl_ref, wh_ref, wl_ref)


def first_kernel(
    near_ref, cross_ref, own_ref, q_ref, depth_ref, fy_ref, fxh_ref, fxl_ref, columns_ref, left_ref, head_ref,
    spec_ref, sum_ref, wh_ref, wl_ref, shifted_ref, mid_ref,
):
    spectrum(near_ref, own_ref, cross_ref, fy_ref, fxh_ref, fxl_ref, head_ref, spec_ref, wh_ref, wl_ref)
    phases = depth_ref[0], depth_ref[1]
    image_points(q_ref, *phases, spec_ref, left_ref, columns_ref, shifted_ref, mid_ref, None, sum_ref)


def second_kernel(
    spec_ref, left_ref, sum_ref, columns_ref, depth_ref, q_ref, acid_ref, cross_ref, own_ref, shifted_ref, mid_ref, acc_ref
):
    phases = depth_ref[0], depth_ref[1]
    image_points(q_ref, *phases, spec_ref, left_ref, columns_ref, shifted_ref, mid_ref, sum_ref, acc_ref)
    dose = depth_ref[2]
    shape = (HALO_ROWS, DEPTHS, LANES)
    head = acc_ref[:, :LANES].reshape(shape)
    tail = acc_ref[:, LANES:].reshape(shape)
    acid_head = 1.0 - jnp.exp(-dose * head)
    acid_tail = 1.0 - jnp.exp(-dose * tail)
    acid_ref[:, :, :LANES] = acid_head
    acid_ref[:, :, LANES:] = acid_tail
    lane1 = lane_iota((DEPTHS, LANES))
    left = jnp.zeros((DEPTHS, LANES), f32)
    right = jnp.zeros((DEPTHS, LANES), f32)
    for y in range(HALO_ROWS):
        here = (lane1 >= 4 * y) & (lane1 < 4 * y + 4)
        left = jnp.where(here, pltpu.roll(acid_head[y], 4 * y, 1) if y else acid_head[y], left)
        turn = (4 * y - 60) % LANES
        right = jnp.where(here, pltpu.roll(acid_tail[y], turn, 1) if turn else acid_tail[y], right)
    even_tile = lax.axis_index("tile") % 2 == 0
    own_ref[...] = jnp.where(even_tile, right, left)
    cross_ref[...] = jnp.where(even_tile, left, right)


def bake_kernel(acid_ref, cross_ref, own_ref, depth_ref, out_ref):
    me = lax.axis_index("src")
    tile = lax.axis_index("tile")
    lane1 = lane_iota((DEPTHS, LANES))
    depth = lax.broadcasted_iota(jnp.int32, (DEPTHS, LANES), 0)
    load = depth_ref[3]
    has_left = (tile > 0).astype(f32)
    has_right = (tile < TILES - 1).astype(f32)
    left_cells = lane1 >= 124
    right_cells = (lane1 >= 64) & (lane1 < 68)
    keep_tail = jnp.where(lane1 < 64, 1.0, jnp.where(left_cells, has_left, jnp.where(right_cells, has_right, 0.0)))

    def keep_row(y):
        row = me * ROWS - BAKE_STEPS + y
        return ((row >= 0) & (row < CORE)).astype(f32)

    even_tile = tile % 2 == 0
    own, cross = own_ref[...], cross_ref[...]
    from_left, from_right = jnp.where(even_tile, cross, own), jnp.where(even_tile, own, cross)
    acid, quencher = [], []
    for y in range(HALO_ROWS):
        tail = acid_ref[y, :, LANES:]
        turn_left, turn_right = (124 - 4 * y) % LANES, (64 - 4 * y) % LANES
        moved_left = pltpu.roll(from_left, turn_left, 1) if turn_left else from_left
        moved_right = pltpu.roll(from_right, turn_right, 1) if turn_right else from_right
        tail = jnp.where(lane1 < 64, tail, jnp.where(left_cells, moved_left, moved_right)) * keep_tail
        head = acid_ref[y, :, :LANES]
        pair = [head, tail]
        loads = [load, load * keep_tail]
        if y < BAKE_STEPS or y >= HALO_ROWS - BAKE_STEPS:
            keep = keep_row(y)
            pair = [v * keep for v in pair]
            loads = [v * keep for v in loads]
        acid.append(pair)
        quencher.append(loads)

    first_lane, last_lane = lane1 == 0, lane1 == LANES - 1
    top, bottom = depth == 0, depth == DEPTHS - 1

    def spread(values, y, k, rate):
        here = values[y][k]
        other = values[y][1 - k]
        before = jnp.where(first_lane, pltpu.roll(other, 1, 1), pltpu.roll(here, 1, 1))
        after = jnp.where(last_lane, pltpu.roll(other, LANES - 1, 1), pltpu.roll(here, LANES - 1, 1))
        lateral = values[y + 1][k] + values[y - 1][k] + (before + after)
        above = jnp.where(top, here, pltpu.roll(here, 1, 0))
        below = jnp.where(bottom, here, pltpu.roll(here, DEPTHS - 1, 0))
        spread_value = rate * lateral + depth_rate * (above + below)
        rest = round(1.0 - 4.0 * rate - 2.0 * depth_rate, 12)
        return spread_value + rest * here if rest else spread_value

    for step in range(1, BAKE_STEPS + 1):
        next_acid, next_quencher = list(acid), list(quencher)
        for y in range(step, HALO_ROWS - step):
            pair, loads = [], []
            for k in range(2):
                reaction = react_rate * acid[y][k] * quencher[y][k]
                new_acid = spread(acid, y, k, acid_rate) - reaction
                pair.append(new_acid)
                if step < BAKE_STEPS:
                    loads.append(spread(quencher, y, k, quench_rate) - reaction)
            if step < BAKE_STEPS:
                pair[1] = pair[1] * keep_tail
                loads[1] = loads[1] * keep_tail
                if y < BAKE_STEPS or y >= HALO_ROWS - BAKE_STEPS:
                    keep = keep_row(y)
                    pair = [v * keep for v in pair]
                    loads = [v * keep for v in loads]
            next_acid[y] = pair
            next_quencher[y] = loads
        acid, quencher = next_acid, next_quencher

    low64 = lane1 < 64
    for k in range(ROWS // 2):
        even_head, even_tail = acid[BAKE_STEPS + 2 * k]
        odd_head, odd_tail = (pltpu.roll(v, 64, 1) for v in acid[BAKE_STEPS + 2 * k + 1])
        base = 384 * k
        out_ref[:, 0, base:base + 128] = even_head
        out_ref[:, 0, base + 128:base + 256] = jnp.where(low64, even_tail, odd_head)
        out_ref[:, 0, base + 256:base + 384] = jnp.where(low64, odd_head, odd_tail)


def vmem(n):
    return [pl.BlockSpec(memory_space=pltpu.VMEM)] * n


def hbm(n):
    return [pl.BlockSpec(memory_space=pltpu.HBM)] * n


def in_hbm(values):
    return pltpu.with_memory_space_constraint(values, pltpu.HBM)


def grant(mib):
    return pltpu.CompilerParams(vmem_limit_bytes=mib * 2**20)


def smem(n):
    return [pl.BlockSpec(memory_space=pltpu.SMEM)] * n


def same(tile):
    return tile


def own_chip(tile):
    return tile ^ 1


def across(tile):
    if tile in (0, TILES - 1):
        return tile
    return tile + 1 if tile % 2 else tile - 1


def nearer_half(tile):
    return tile ^ (TILES // 2)


def route(turn, move, flip=0):
    pairs = []
    for s in range(SECTORS):
        upper, y = divmod(s, 4)
        target = (upper ^ flip) * 4 + (y + turn) % 4
        for t in range(TILES):
            source, place = s * TILES + t, target * TILES + move(t)
            pairs.append((source, (s ^ 1) * TILES + t if place == source else place))
    return pairs


def on_device(near_field, source_shift, source_weight, defocus, dose, quencher_load):
    both = ("src", "tile")
    near = near_field.reshape(2, CORE * CORE // LANES, LANES)
    packed = jax.ShapeDtypeStruct((CORE // 2 + 8, LANES), f32)
    edge = jax.ShapeDtypeStruct((DEPTHS, LANES), f32)
    cross, own, points = pl.pallas_call(
        edges_kernel,
        out_shape=(packed, packed, edge),
        in_specs=hbm(3),
        out_specs=tuple(vmem(3)),
        scratch_shapes=[
            pltpu.VMEM(near.shape, f32),
            pltpu.SMEM(source_shift.shape, jnp.int32),
            pltpu.SMEM(source_weight.shape, f32),
            pltpu.SemaphoreType.DMA((3,)),
        ],
        compiler_params=grant(8),
        name="edges",
    )(in_hbm(near), in_hbm(source_shift), in_hbm(source_weight))
    from_cross = lax.ppermute(cross, both, route(0, across))
    from_own = lax.ppermute(own, both, route(1, own_chip))
    turned = lax.ppermute(points, both, route(2, same))
    turned_back = lax.ppermute(points, both, route(3, same))
    last = CORE // 2
    half_points = jnp.concatenate(
        [points[:1, :8], turned_back[:1, :8], from_own[last:last + 1, :8], turned[:1, :8]], 0
    )
    other_points = lax.ppermute(half_points, both, route(0, nearer_half, 1))

    high, low = inverse_columns()
    tables = [np.concatenate(forward_rows(), 0), *forward_columns(), np.concatenate([high, high, low], 0)]
    rows = HALO_ROWS * DEPTHS
    window = pltpu.VMEM((2 * CORE, 256), bf16)
    *tables, left, depth, head = pl.pallas_call(
        prepare_kernel,
        out_shape=(
            *(jax.ShapeDtypeStruct(v.shape, bf16) for v in tables),
            jax.ShapeDtypeStruct((2 * rows, 256), bf16),
            jax.ShapeDtypeStruct((4, DEPTHS, LANES), f32),
            jax.ShapeDtypeStruct((SPEC_ROWS, 512), f32),
        ),
        in_specs=smem(3) + hbm(6),
        out_specs=tuple(vmem(7)),
        scratch_shapes=[
            pltpu.VMEM(near.shape, f32), window, window,
            pltpu.VMEM((CORE + 2 * BAKE_STEPS, 256), f32), pltpu.SemaphoreType.DMA((6,)),
        ],
        compiler_params=grant(8),
        cost_estimate=pl.CostEstimate(flops=1_000_000, bytes_accessed=5_000_000, transcendentals=0),
        name="prepare",
    )(defocus, dose, quencher_load, in_hbm(near), *(in_hbm(jnp.asarray(v)) for v in (*tables, inverse_rows())))
    columns = tables[-1]
    total = jax.ShapeDtypeStruct((rows, 256), f32)
    shifted = pltpu.VMEM((SECTORS // 2 * POINTS, 2, 256, 256), bf16)
    middle = pltpu.VMEM((2, SECTORS // 2 * POINTS, rows, 256), bf16)
    spec, acc = pl.pallas_call(
        first_kernel,
        out_shape=(jax.ShapeDtypeStruct((8, SPEC_ROWS, LANES), f32), total),
        in_specs=vmem(3) + smem(1) + vmem(7),
        out_specs=tuple(vmem(2)),
        scratch_shapes=[window, window, shifted, middle],
        cost_estimate=pl.CostEstimate(flops=8_000_000_000, bytes_accessed=4_000_000, transcendentals=0),
        compiler_params=grant(24),
        name="first",
    )(near, from_cross, from_own, half_points, depth, *tables, left, head)
    acid, cross, own = pl.pallas_call(
        second_kernel,
        out_shape=(jax.ShapeDtypeStruct((HALO_ROWS, DEPTHS, 256), f32), edge, edge),
        in_specs=vmem(5) + smem(1),
        out_specs=tuple(vmem(3)),
        scratch_shapes=[shifted, middle, pltpu.VMEM(total.shape, f32)],
        compiler_params=grant(24),
        name="second",
    )(spec, left, acc, columns, depth, other_points)
    from_cross = lax.ppermute(cross, both, route(0, across))
    from_own = lax.ppermute(own, both, route(0, own_chip))
    return pl.pallas_call(
        bake_kernel,
        out_shape=jax.ShapeDtypeStruct((DEPTHS, 1, ROWS * CORE), f32),
        in_specs=vmem(4),
        out_specs=vmem(1)[0],
        compiler_params=grant(8),
        name="bake",
    )(acid, from_cross, from_own, depth)


def solution(mesh):
    return jax.shard_map(
        on_device,
        mesh=mesh,
        in_specs=(P(None, "tile", None), P("src", None, None), P("src", None), P(), P(), P()),
        out_specs=P(None, "tile", "src"),
        check_vma=False,
    )
```

```python
import numpy as np

import jax
import jax.numpy as jnp
from jax import lax
from jax.experimental import pallas as pl
from jax.experimental.pallas import tpu as pltpu
from jax.sharding import PartitionSpec as P

CORE = 192
MARGIN = 32
LENGTH = CORE + 2 * MARGIN
RADIUS = 48
SHIFT_MAX = 38
DEPTHS = 8
BAKE_STEPS = 4
SECTORS = 8
TILES = 32
POINTS = 2
ROWS = CORE // SECTORS
HALO_ROWS = ROWS + 2 * BAKE_STEPS
LOW = 88
SPEC_ROWS = 208
LANES = 128
GROUP_SHIFT = 8
GROUP = 8
CHUNK = 128

acid_rate = 0.24
quench_rate = 0.12
depth_rate = 0.02
react_rate = 0.8

bf16 = jnp.bfloat16
f32 = jnp.float32


def two_parts(table):
    table = table.astype(np.float32)
    high = table.astype(bf16)
    low = (table - high.astype(np.float32)).astype(bf16)
    return high, low


def waves(left, right):
    angle = 2.0 * np.pi / LENGTH * (np.outer(left, right) % LENGTH)
    return np.cos(angle), np.sin(angle)


def forward_rows():
    order = np.concatenate([np.arange(0, CORE, 2), np.arange(1, CORE, 2)])
    real, imag = waves(np.arange(SPEC_ROWS) - LOW, order + MARGIN)
    return two_parts(np.concatenate([real, -imag], 1))


def forward_columns():
    order = np.concatenate(
        [np.arange(CORE) + MARGIN, np.arange(MARGIN), np.arange(MARGIN) + MARGIN + CORE]
    )
    bins = np.arange(LANES) - SHIFT_MAX
    real, imag = waves(order, np.concatenate([bins, -bins]))
    imag = -imag
    return two_parts(np.block([[real, imag], [-imag, real]]))


def inverse_columns():
    bins = np.arange(64)
    real, imag = waves(bins, np.arange(256) + MARGIN)
    keep = np.where(bins <= RADIUS, np.where(bins == 0, 0.5, 1.0), 0.0)[:, None] / LENGTH
    keep = keep * (np.arange(256) < CORE)[None, :]
    return two_parts(np.concatenate([real * keep, imag * keep], 0))


def inverse_rows():
    bins = np.arange(LANES) - RADIUS
    rows = np.arange(CORE + 2 * BAKE_STEPS) - BAKE_STEPS + MARGIN
    real, imag = waves(rows, bins)
    keep = (np.abs(bins) <= RADIUS)[None, :] / LENGTH
    return np.concatenate([real * keep, imag * keep], 1).astype(np.float32)


def split(values):
    high = values.astype(bf16)
    low = (values - high.astype(f32)).astype(bf16)
    return high, low


def product(left, right_high, right_low):
    rows = left.shape[0] // 2
    both = jnp.dot(left, right_high, preferred_element_type=f32)
    low = jnp.dot(left[:rows], right_low, preferred_element_type=f32)
    return both[:rows] + (both[rows:] + low)


def lane_iota(shape):
    return lax.broadcasted_iota(jnp.int32, shape, len(shape) - 1)


def edges_kernel(
    near_hbm, shift_hbm, weight_hbm, cross_ref, own_ref, points_ref, near_ref, shift_ref, weight_ref, sems
):
    copies = [
        pltpu.make_async_copy(source, target, sems.at[k])
        for k, (source, target) in enumerate(
            ((near_hbm, near_ref), (shift_hbm, shift_ref), (weight_hbm, weight_ref))
        )
    ]
    for copy in copies:
        copy.start()
    for copy in copies:
        copy.wait()
    half = CORE // 4
    even_tile = lax.axis_index("tile") % 2 == 0
    lane = lane_iota((half, LANES))
    odd = lane >= 64
    second = (lane % 64) >= 32
    for part in range(2):
        def rows(start, offset):
            return near_ref[part, pl.ds(3 * start + offset, half, stride=3), :]

        def right(start):
            return jnp.where(odd, rows(start, 2), rows(start, 1))

        def left(start):
            return jnp.where(odd, rows(start, 1), rows(start, 0))

        right_edge = jnp.where(second, right(0), pltpu.roll(right(half), 96, 1))
        left_edge = jnp.where(second, pltpu.roll(left(half), 32, 1), left(0))
        own_ref[pl.ds(part * half, half), :] = jnp.where(even_tile, right_edge, left_edge)
        cross_ref[pl.ds(part * half, half), :] = jnp.where(even_tile, left_edge, right_edge)

    lane1 = lane_iota((8, LANES))
    values = jnp.zeros((8, LANES), f32)
    for j in range(POINTS):
        for axis in range(2):
            values = jnp.where(lane1 == 2 * j + axis, shift_ref[0, j, axis].astype(f32), values)
    weights = jnp.ones((8, LANES), f32)
    for j in range(POINTS):
        weights = jnp.where(lane1 == 4 + j, weight_ref[0, j], weights)
    values = jnp.where(lane1 < 4, values, jnp.sqrt(weights))
    own_ref[pl.ds(2 * half, 8), :] = values
    cross_ref[pl.ds(2 * half, 8), :] = values
    points_ref[...] = values


def by_depth(ref):
    depth = lax.broadcasted_iota(jnp.int32, (DEPTHS, LANES), 0)
    out = jnp.zeros((DEPTHS, LANES), f32)
    for d in range(DEPTHS):
        out = jnp.where(depth == d, ref[d], out)
    return out


def depth_phase(defocus_ref, bins):
    phase = by_depth(defocus_ref) * (bins * bins).astype(f32) / float(RADIUS * RADIUS)
    return jnp.cos(phase), jnp.sin(phase)


def half_spectrum(near_ref, margins, column_tile, rows_ref, fxh_ref, fxl_ref, wh_ref, wl_ref):
    half = CORE // 4
    lane = lane_iota((half, LANES))
    low64 = lane < 64
    quarter = lane // 32
    for part in range(2):
        for piece in range(2):
            def rows(offset):
                return near_ref[part, pl.ds(3 * piece * half + offset, half, stride=3), :]

            ct = pltpu.roll(rows(2), 64, 1)
            if column_tile == 0:
                blocks = rows(0), jnp.where(low64, pltpu.roll(rows(1), 64, 1), ct)
            else:
                from_left, from_right = margins(part)
                turns = ((32, 96), (96, 32)) if piece == 0 else ((64, 64), (0, 0))
                blocks = []
                for core, (turn_left, turn_right) in zip((rows(1), ct), turns):
                    left = pltpu.roll(from_left, turn_left, 1) if turn_left else from_left
                    right = pltpu.roll(from_right, turn_right, 1) if turn_right else from_right
                    blocks.append(jnp.where(low64, core, jnp.where(quarter == 2, left, right)))
            for base, block in zip((0, CORE // 2), blocks):
                for ref, value in zip((wh_ref, wl_ref), split(block)):
                    upper = pl.ds(base + piece * half, half)
                    lower = pl.ds(CORE + base + piece * half, half)
                    ref[upper, part * LANES:(part + 1) * LANES] = value
                    ref[lower, (1 - part) * LANES:(2 - part) * LANES] = -value if part else value

    def columns(ref):
        first = column_tile * LANES
        return jnp.concatenate([ref[first:first + LANES], ref[256 + first:256 + first + LANES]], 0)

    mixed = product(rows_ref[...], wh_ref[...], wl_ref[...])
    return product(jnp.concatenate(split(mixed), 0), columns(fxh_ref), columns(fxl_ref))


def spectrum(near_ref, own_ref, cross_ref, rows_ref, fxh_ref, fxl_ref, head_ref, spec_ref, wh_ref, wl_ref):
    tile = lax.axis_index("tile")
    even_tile = tile % 2 == 0
    has_left = (tile > 0).astype(f32)
    has_right = (tile < TILES - 1).astype(f32)
    half = CORE // 4

    def margins(part):
        own, cross = own_ref[pl.ds(part * half, half), :], cross_ref[pl.ds(part * half, half), :]
        return jnp.where(even_tile, cross, own) * has_left, jnp.where(even_tile, own, cross) * has_right

    spec = head_ref[...] + half_spectrum(near_ref, margins, 1, rows_ref, fxh_ref, fxl_ref, wh_ref, wl_ref)
    ahead_real, back_real, ahead_imag, back_imag = (spec[:, k * LANES:(k + 1) * LANES] for k in range(4))
    for k, value in enumerate((ahead_real, back_real, ahead_imag, back_imag)):
        spec_ref[k] = value
    for k, value in enumerate((-ahead_imag, back_imag, ahead_real, -back_real)):
        spec_ref[4 + k] = pltpu.roll(value, 64, 1)


def row_tables(rows_ref, phase_real, phase_imag, left_ref):
    me = lax.axis_index("src")
    table = rows_ref[pl.ds(pl.multiple_of(me * ROWS, 8), HALO_ROWS), :]
    table_real = table[:, None, :LANES]
    table_imag = table[:, None, LANES:]
    left_real = (table_real * phase_real - table_imag * phase_imag).reshape(HALO_ROWS * DEPTHS, LANES)
    left_imag = (table_real * phase_imag + table_imag * phase_real).reshape(HALO_ROWS * DEPTHS, LANES)
    for k, block in ((0, left_real), (1, left_imag)):
        high, low = split(block)
        left_ref[:HALO_ROWS * DEPTHS, k * LANES:(k + 1) * LANES] = high
        left_ref[HALO_ROWS * DEPTHS:, k * LANES:(k + 1) * LANES] = low


def image_points(q_ref, phase_real, phase_imag, spec_ref, left_ref, columns_ref, shifted_ref, mid_ref, before_ref, sum_ref):
    rowbin = lax.broadcasted_iota(jnp.int32, (LANES, LANES), 0) - RADIUS
    colbin = lane_iota((LANES, LANES)) % 64
    inside = rowbin * rowbin + colbin * colbin <= RADIUS * RADIUS
    rows = HALO_ROWS * DEPTHS
    shape = (HALO_ROWS, DEPTHS, LANES)

    def shift_spectrum(n):
        row, j = n // POINTS, n % POINTS
        start = (LOW - RADIUS) - q_ref[row, 2 * j].astype(jnp.int32)
        shift = q_ref[row, 2 * j + 1].astype(jnp.int32)

        lane = lane_iota((LANES, LANES))

        def moved(k, first):
            near = ((lane - first) & (LANES - 1)) < 64
            rows_here = pl.ds(start, LANES)
            value = jnp.where(near, spec_ref[k, rows_here, :], spec_ref[4 + k, rows_here, :])
            return pltpu.roll(value, LANES - first, 1)

        ahead, back = SHIFT_MAX - shift, SHIFT_MAX + shift
        folded = [moved(k, ahead) + moved(k + 1, back) for k in (0, 2)]
        for k in range(2):
            for part, value in enumerate(split(jnp.where(inside, folded[k], 0.0))):
                shifted_ref[n, part, :LANES, k * LANES:(k + 1) * LANES] = value
                shifted_ref[n, part, LANES:, (1 - k) * LANES:(2 - k) * LANES] = -value if k else value

    def transform_rows(n):
        amp = q_ref[n // POINTS, 4 + n % POINTS]
        turn_real, turn_imag = phase_real * amp, phase_imag * amp
        both = jnp.dot(left_ref[...], shifted_ref[n, 0], preferred_element_type=f32)
        low = jnp.dot(left_ref[:rows, :], shifted_ref[n, 1], preferred_element_type=f32)
        middle = both[:rows] + (both[rows:] + low)
        mid_real = middle[:, :LANES].reshape(shape)
        mid_imag = middle[:, LANES:].reshape(shape)
        out_real = (mid_real * turn_real - mid_imag * turn_imag).reshape(rows, LANES)
        out_imag = (mid_real * turn_imag + mid_imag * turn_real).reshape(rows, LANES)
        for k, value in enumerate((out_real, out_imag)):
            high, low = split(value)
            mid_ref[k, n, :, :LANES] = high
            mid_ref[k, n, :, LANES:] = low

    points = SECTORS // 2 * POINTS

    def in_groups(size, body):
        if size == points:
            for n in range(points):
                body(n)
        else:
            @pl.loop(0, points // size)
            def _(g):
                for n in range(size):
                    body(g * size + n)

    in_groups(GROUP_SHIFT, shift_spectrum)
    in_groups(GROUP, transform_rows)

    for c in range(rows // CHUNK):
        here = slice(c * CHUNK, (c + 1) * CHUNK)
        total = None if before_ref is None else before_ref[here, :]
        for k in range(2):
            part = mid_ref[k, :, here, :].reshape(points * CHUNK, 256)
            part = jnp.concatenate([part, part[:, :LANES]], 1)
            image = jnp.dot(part, columns_ref[...], preferred_element_type=f32)
            power = (image * image).reshape(points, CHUNK, 256)
            for n in range(points):
                total = power[n] if total is None else total + power[n]
        sum_ref[here, :] = total


def prepare_kernel(
    defocus_ref, dose_ref, load_ref, near_hbm, fy_hbm, fxh_hbm, fxl_hbm, columns_hbm, rows_hbm,
    fy_ref, fxh_ref, fxl_ref, columns_ref, left_ref, depth_ref, head_ref, near_ref, wh_ref, wl_ref, rows_ref, sems,
):
    pairs = (
        (rows_hbm, rows_ref), (near_hbm, near_ref), (fy_hbm, fy_ref), (fxh_hbm, fxh_ref), (fxl_hbm, fxl_ref),
        (columns_hbm, columns_ref),
    )
    copies = [pltpu.make_async_copy(source, target, sems.at[k]) for k, (source, target) in enumerate(pairs)]
    for copy in copies:
        copy.start()
    lane = lane_iota((DEPTHS, LANES))
    depth_ref[0], depth_ref[1] = depth_phase(defocus_ref, lane % 64)
    phase_real, phase_imag = depth_phase(defocus_ref, lane - RADIUS)
    depth_ref[2], depth_ref[3] = by_depth(dose_ref), by_depth(load_ref)
    copies[0].wait()
    row_tables(rows_ref, phase_real, phase_imag, left_ref)
    for copy in copies[1:]:
        copy.wait()
    head_ref[...] = half_spectrum(near_ref, None, 0, fy_ref, fxh_ref, fxl_ref, wh_ref, wl_ref)


def first_kernel(
    near_ref, cross_ref, own_ref, q_ref, depth_ref, fy_ref, fxh_ref, fxl_ref, columns_ref, left_ref, head_ref,
    spec_ref, sum_ref, wh_ref, wl_ref, shifted_ref, mid_ref,
):
    spectrum(near_ref, own_ref, cross_ref, fy_ref, fxh_ref, fxl_ref, head_ref, spec_ref, wh_ref, wl_ref)
    phases = depth_ref[0], depth_ref[1]
    image_points(q_ref, *phases, spec_ref, left_ref, columns_ref, shifted_ref, mid_ref, None, sum_ref)


def second_kernel(
    spec_ref, left_ref, sum_ref, columns_ref, depth_ref, q_ref, acid_ref, cross_ref, own_ref, shifted_ref, mid_ref, acc_ref
):
    phases = depth_ref[0], depth_ref[1]
    image_points(q_ref, *phases, spec_ref, left_ref, columns_ref, shifted_ref, mid_ref, sum_ref, acc_ref)
    dose = depth_ref[2]
    shape = (HALO_ROWS, DEPTHS, LANES)
    head = acc_ref[:, :LANES].reshape(shape)
    tail = acc_ref[:, LANES:].reshape(shape)
    acid_head = 1.0 - jnp.exp(-dose * head)
    acid_tail = 1.0 - jnp.exp(-dose * tail)
    acid_ref[:, :, :LANES] = acid_head
    acid_ref[:, :, LANES:] = acid_tail
    lane1 = lane_iota((DEPTHS, LANES))
    left = jnp.zeros((DEPTHS, LANES), f32)
    right = jnp.zeros((DEPTHS, LANES), f32)
    for y in range(HALO_ROWS):
        here = (lane1 >= 4 * y) & (lane1 < 4 * y + 4)
        left = jnp.where(here, pltpu.roll(acid_head[y], 4 * y, 1) if y else acid_head[y], left)
        turn = (4 * y - 60) % LANES
        right = jnp.where(here, pltpu.roll(acid_tail[y], turn, 1) if turn else acid_tail[y], right)
    even_tile = lax.axis_index("tile") % 2 == 0
    own_ref[...] = jnp.where(even_tile, right, left)
    cross_ref[...] = jnp.where(even_tile, left, right)


def bake_kernel(acid_ref, cross_ref, own_ref, depth_ref, out_ref):
    me = lax.axis_index("src")
    tile = lax.axis_index("tile")
    lane1 = lane_iota((DEPTHS, LANES))
    depth = lax.broadcasted_iota(jnp.int32, (DEPTHS, LANES), 0)
    load = depth_ref[3]
    has_left = (tile > 0).astype(f32)
    has_right = (tile < TILES - 1).astype(f32)
    left_cells = lane1 >= 124
    right_cells = (lane1 >= 64) & (lane1 < 68)
    keep_tail = jnp.where(lane1 < 64, 1.0, jnp.where(left_cells, has_left, jnp.where(right_cells, has_right, 0.0)))

    def keep_row(y):
        row = me * ROWS - BAKE_STEPS + y
        return ((row >= 0) & (row < CORE)).astype(f32)

    even_tile = tile % 2 == 0
    own, cross = own_ref[...], cross_ref[...]
    from_left, from_right = jnp.where(even_tile, cross, own), jnp.where(even_tile, own, cross)
    acid, quencher = [], []
    for y in range(HALO_ROWS):
        tail = acid_ref[y, :, LANES:]
        turn_left, turn_right = (124 - 4 * y) % LANES, (64 - 4 * y) % LANES
        moved_left = pltpu.roll(from_left, turn_left, 1) if turn_left else from_left
        moved_right = pltpu.roll(from_right, turn_right, 1) if turn_right else from_right
        tail = jnp.where(lane1 < 64, tail, jnp.where(left_cells, moved_left, moved_right)) * keep_tail
        head = acid_ref[y, :, :LANES]
        pair = [head, tail]
        loads = [load, load * keep_tail]
        if y < BAKE_STEPS or y >= HALO_ROWS - BAKE_STEPS:
            keep = keep_row(y)
            pair = [v * keep for v in pair]
            loads = [v * keep for v in loads]
        acid.append(pair)
        quencher.append(loads)

    first_lane, last_lane = lane1 == 0, lane1 == LANES - 1
    top, bottom = depth == 0, depth == DEPTHS - 1

    def spread(values, y, k, rate):
        here = values[y][k]
        other = values[y][1 - k]
        before = jnp.where(first_lane, pltpu.roll(other, 1, 1), pltpu.roll(here, 1, 1))
        after = jnp.where(last_lane, pltpu.roll(other, LANES - 1, 1), pltpu.roll(here, LANES - 1, 1))
        lateral = values[y + 1][k] + values[y - 1][k] + (before + after)
        above = jnp.where(top, here, pltpu.roll(here, 1, 0))
        below = jnp.where(bottom, here, pltpu.roll(here, DEPTHS - 1, 0))
        spread_value = rate * lateral + depth_rate * (above + below)
        rest = round(1.0 - 4.0 * rate - 2.0 * depth_rate, 12)
        return spread_value + rest * here if rest else spread_value

    for step in range(1, BAKE_STEPS + 1):
        next_acid, next_quencher = list(acid), list(quencher)
        for y in range(step, HALO_ROWS - step):
            pair, loads = [], []
            for k in range(2):
                reaction = react_rate * acid[y][k] * quencher[y][k]
                new_acid = spread(acid, y, k, acid_rate) - reaction
                pair.append(new_acid)
                if step < BAKE_STEPS:
                    loads.append(spread(quencher, y, k, quench_rate) - reaction)
            if step < BAKE_STEPS:
                pair[1] = pair[1] * keep_tail
                loads[1] = loads[1] * keep_tail
                if y < BAKE_STEPS or y >= HALO_ROWS - BAKE_STEPS:
                    keep = keep_row(y)
                    pair = [v * keep for v in pair]
                    loads = [v * keep for v in loads]
            next_acid[y] = pair
            next_quencher[y] = loads
        acid, quencher = next_acid, next_quencher

    low64 = lane1 < 64
    for k in range(ROWS // 2):
        even_head, even_tail = acid[BAKE_STEPS + 2 * k]
        odd_head, odd_tail = (pltpu.roll(v, 64, 1) for v in acid[BAKE_STEPS + 2 * k + 1])
        base = 384 * k
        out_ref[:, 0, base:base + 128] = even_head
        out_ref[:, 0, base + 128:base + 256] = jnp.where(low64, even_tail, odd_head)
        out_ref[:, 0, base + 256:base + 384] = jnp.where(low64, odd_head, odd_tail)


def vmem(n):
    return [pl.BlockSpec(memory_space=pltpu.VMEM)] * n


def hbm(n):
    return [pl.BlockSpec(memory_space=pltpu.HBM)] * n


def in_hbm(values):
    return pltpu.with_memory_space_constraint(values, pltpu.HBM)


def grant(mib):
    return pltpu.CompilerParams(vmem_limit_bytes=mib * 2**20)


def smem(n):
    return [pl.BlockSpec(memory_space=pltpu.SMEM)] * n


def same(tile):
    return tile


def own_chip(tile):
    return tile ^ 1


def across(tile):
    if tile in (0, TILES - 1):
        return tile
    return tile + 1 if tile % 2 else tile - 1


def nearer_half(tile):
    return tile ^ (TILES // 2)


def route(turn, move, flip=0):
    pairs = []
    for s in range(SECTORS):
        upper, y = divmod(s, 4)
        target = (upper ^ flip) * 4 + (y + turn) % 4
        for t in range(TILES):
            source, place = s * TILES + t, target * TILES + move(t)
            pairs.append((source, (s ^ 1) * TILES + t if place == source else place))
    return pairs


def on_device(near_field, source_shift, source_weight, defocus, dose, quencher_load):
    both = ("src", "tile")
    near = near_field.reshape(2, CORE * CORE // LANES, LANES)
    packed = jax.ShapeDtypeStruct((CORE // 2 + 8, LANES), f32)
    edge = jax.ShapeDtypeStruct((DEPTHS, LANES), f32)
    cross, own, points = pl.pallas_call(
        edges_kernel,
        out_shape=(packed, packed, edge),
        in_specs=hbm(3),
        out_specs=tuple(vmem(3)),
        scratch_shapes=[
            pltpu.VMEM(near.shape, f32),
            pltpu.SMEM(source_shift.shape, jnp.int32),
            pltpu.SMEM(source_weight.shape, f32),
            pltpu.SemaphoreType.DMA((3,)),
        ],
        compiler_params=grant(8),
        name="edges",
    )(in_hbm(near), in_hbm(source_shift), in_hbm(source_weight))
    from_cross = lax.ppermute(cross, both, route(3, across))
    from_own = lax.ppermute(own, both, route(1, own_chip))
    turned = lax.ppermute(points, both, route(2, same))
    last = CORE // 2
    half_points = jnp.concatenate(
        [points[:1, :8], from_cross[last:last + 1, :8], from_own[last:last + 1, :8], turned[:1, :8]], 0
    )
    other_points = lax.ppermute(half_points, both, route(0, nearer_half, 1))

    high, low = inverse_columns()
    tables = [np.concatenate(forward_rows(), 0), *forward_columns(), np.concatenate([high, high, low], 0)]
    rows = HALO_ROWS * DEPTHS
    window = pltpu.VMEM((2 * CORE, 256), bf16)
    *tables, left, depth, head = pl.pallas_call(
        prepare_kernel,
        out_shape=(
            *(jax.ShapeDtypeStruct(v.shape, bf16) for v in tables),
            jax.ShapeDtypeStruct((2 * rows, 256), bf16),
            jax.ShapeDtypeStruct((4, DEPTHS, LANES), f32),
            jax.ShapeDtypeStruct((SPEC_ROWS, 512), f32),
        ),
        in_specs=smem(3) + hbm(6),
        out_specs=tuple(vmem(7)),
        scratch_shapes=[
            pltpu.VMEM(near.shape, f32), window, window,
            pltpu.VMEM((CORE + 2 * BAKE_STEPS, 256), f32), pltpu.SemaphoreType.DMA((6,)),
        ],
        compiler_params=grant(8),
        cost_estimate=pl.CostEstimate(flops=1_000_000, bytes_accessed=5_000_000, transcendentals=0),
        name="prepare",
    )(defocus, dose, quencher_load, in_hbm(near), *(in_hbm(jnp.asarray(v)) for v in (*tables, inverse_rows())))
    columns = tables[-1]
    total = jax.ShapeDtypeStruct((rows, 256), f32)
    shifted = pltpu.VMEM((SECTORS // 2 * POINTS, 2, 256, 256), bf16)
    middle = pltpu.VMEM((2, SECTORS // 2 * POINTS, rows, 256), bf16)
    spec, acc = pl.pallas_call(
        first_kernel,
        out_shape=(jax.ShapeDtypeStruct((8, SPEC_ROWS, LANES), f32), total),
        in_specs=vmem(3) + smem(1) + vmem(7),
        out_specs=tuple(vmem(2)),
        scratch_shapes=[window, window, shifted, middle],
        cost_estimate=pl.CostEstimate(flops=8_000_000_000, bytes_accessed=4_000_000, transcendentals=0),
        compiler_params=grant(24),
        name="first",
    )(near, from_cross, from_own, half_points, depth, *tables, left, head)
    acid, cross, own = pl.pallas_call(
        second_kernel,
        out_shape=(jax.ShapeDtypeStruct((HALO_ROWS, DEPTHS, 256), f32), edge, edge),
        in_specs=vmem(5) + smem(1),
        out_specs=tuple(vmem(3)),
        scratch_shapes=[shifted, middle, pltpu.VMEM(total.shape, f32)],
        compiler_params=pltpu.CompilerParams(
            vmem_limit_bytes=24 * 2**20
        ),
        name="second",
    )(spec, left, acc, columns, depth, other_points)
    from_cross = lax.ppermute(cross, both, route(0, across))
    from_own = lax.ppermute(own, both, route(0, own_chip))
    return pl.pallas_call(
        bake_kernel,
        out_shape=jax.ShapeDtypeStruct((DEPTHS, 1, ROWS * CORE), f32),
        in_specs=vmem(4),
        out_specs=vmem(1)[0],
        compiler_params=grant(8),
        name="bake",
    )(acid, from_cross, from_own, depth)


def solution(mesh):
    return jax.shard_map(
        on_device,
        mesh=mesh,
        in_specs=(P(None, "tile", None), P("src", None, None), P("src", None), P(), P(), P()),
        out_specs=P(None, "tile", "src"),
        check_vma=False,
    )
```
